32 devices in a mesh: req: 16 (over z, x, core), tp: 2 (over y).
Axes of the slice: x: 2, y: 2, z: 4, core: 2. Of those that a mesh axis runs over, the one named last changes fastest.
Arguments:
- queries: bfloat16 [2048, 16, 192], P('req', 'tp'), may hold values from -160 to 160
- stretch_cache: bfloat16 [2048, 576], P('req'), may hold values from -6 to 6
- prefix_pool: bfloat16 [192, 64, 576], P('req'), may hold values from -6 to 6
- page_table: int32 [16, 12], P('req'), may hold values from 0 to 11, each once within a row
- prefix_len: int32 [16], replicated, may hold values from 1 to 768, 6144 in all
- prompt_cache: bfloat16 [2, 256, 576], P(None, 'req'), may hold values from -6 to 6
- prompt_len: int32 [2], replicated, may hold values from 1 to 256, 384 in all
- group_ids: int32 [16], replicated, may hold values from 0 to 1
- absorb_weight: bfloat16 [16, 128, 512], P('tp'), may hold values from -0.5 to 0.5
- value_weight: bfloat16 [16, 512, 128], P('tp'), may hold values from -1 to 1
- out_weight: bfloat16 [2048, 2048], P('tp'), may hold values from -0.125 to 0.125
- residual: bfloat16 [2048, 2048], P('req', 'tp'), may hold values from -20 to 20
- norm_gain: bfloat16 [2048], P('tp'), may hold values from 0.099609375 to 1.8984375
- routes: int32 [2048, 6], P('req'), may hold values from 0 to 15, all different within a row; in each aligned block of 128 rows (0 to 127, 128 to 255, ...) at most 64 rows name the same one
- route_weight: float32 [2048, 6], P('req'), may hold values from 0.05 to 0.45
- gate_weight: bfloat16 [16, 2048, 1408], P('req', None, 'tp'), may hold values from -0.125 to 0.125
- up_weight: bfloat16 [16, 2048, 1408], P('req', None, 'tp'), may hold values from -0.125 to 0.125
- down_weight: bfloat16 [16, 1408, 2048], P('req', 'tp'), may hold values from -0.15625 to 0.15625
Outputs:
- attended: bfloat16 [2048, 2048], P('req', 'tp')
- mixed: bfloat16 [2048, 2048], P('req', 'tp')
The draws below stay inside these ranges and needn't reach their ends.
Inputs may be any that keep to these rules, and one draw needn't show every extreme that they name: `page_table`: every row of a request is an order of its 12 pages. `prefix_len`: one request has a prefix of exactly 768. `routes`: in the rows of one request no expert is named more than 64 times, a bound that some block reaches.
All inputs are finite; a program needn't handle non-finite values.
Results may differ from the reference program's by a relative error of at most 0.023.
Values may be sent and summed in bfloat16 or wider, within the bound.
A program may use at most 64 MiB of HBM per device.

```python
import math
import jax
import jax.numpy as jnp
import numpy as np
from jax import lax

D = 2048
HEADS = 16
NOPE = 128
ROPE = 64
VDIM = 128
RANK = 512
FF_EXP = 1408
TOP = 6
TOK_DEV = 128
PAGE = 64
PAGES = 12
REQS = 16
TOKENS = 2048
EXPERTS = 16
LMAX = 768
SHARED = 256
CAP = 64
N_TP = 2


def attention_draw(key):
    base = jax.random.fold_in(key, 7)
    key_one, key_two = jax.random.split(base, 2)
    stretch = jnp.clip(jax.random.normal(key_one, (TOKENS, RANK + ROPE), jnp.float32), -6.0, 6.0)
    query = jnp.clip(jax.random.normal(key_two, (TOKENS, HEADS, NOPE + ROPE), jnp.float32), -6.0, 6.0)
    return (stretch, query)


def draw_queries(key, part):
    return attention_draw(key)[1].astype(jnp.bfloat16)


def draw_stretch_cache(key, part):
    return attention_draw(key)[0].astype(jnp.bfloat16)


def draw_residual(key, part):
    key_one, key_two, key_three = jax.random.split(jax.random.fold_in(key, 11), 3)
    column = jnp.arange(D).astype(jnp.float32) / D
    row_scale = 0.5 * jnp.exp(jax.random.uniform(key_two, (TOKENS, 1), jnp.float32, 0.0, math.log(10.0)))
    values = jnp.clip(jax.random.normal(key_one, (TOKENS, D), jnp.float32), -4.0, 4.0)
    rise = jnp.exp(math.log(30.0) * (column - 1.0))
    column_scale = jnp.exp(jax.random.uniform(key_three, (D,), jnp.float32, math.log(0.5), 0.0)) * rise
    return (values * row_scale * column_scale[None, :]).astype(jnp.bfloat16)


def set_ends(result, key, low, high):
    shape = result.shape
    spot = [jax.random.randint(jax.random.fold_in(key, axis), (), 0, shape[axis]) for axis in range(len(shape))]
    result = result.at[tuple(spot)].set(low)
    longest = shape.index(max(shape))
    spot[longest] = (spot[longest] + 1) % shape[longest]
    return result.at[tuple(spot)].set(high)


def shard_levels(own_key, dims, cuts, least, high):
    level, own = 1.0, jax.random.fold_in(own_key, 6)
    for axis_at, shards_of in cuts:
        steps = jnp.exp(jax.random.uniform(jax.random.fold_in(own, axis_at), (shards_of,), jnp.float32, least / len(cuts), high / len(cuts)))
        level = level * jnp.repeat(steps, dims[axis_at] // shards_of).reshape([-1 if axis == axis_at else 1 for axis in range(len(dims))])
    return level


def profile(amount, total, limit, lean):
    portions = [(1 << 20) // math.isqrt(standing ** lean) + 1 for standing in range(2, amount + 1)]
    spare, counts = total - limit - (amount - 1), [1] * (amount - 1)
    while spare > 0:
        movable = [i for i in range(amount - 1) if counts[i] < limit]
        mass, left = sum([portions[i] for i in movable]), spare
        for i in movable:
            addition = min(limit - counts[i], max(1, left * portions[i] // mass), spare)
            counts[i] = counts[i] + addition
            spare = spare - addition
    return np.array([limit] + counts)


def uneven_parts(key, amount, total, bound, lean):
    if amount == 2:
        one = jax.random.randint(key, (), max(1, total - bound), min(bound, total - 1) + 1)
        return jnp.stack([one, total - one])
    tallies = jnp.asarray(profile(amount, total, bound, lean), jnp.int32)
    couples = (amount - 1) // 2
    source_of, receiver = tallies[1:1 + 2 * couples:2], tallies[2:2 + 2 * couples:2]
    margin = jnp.minimum(source_of - 1, bound - receiver)
    shifted = jax.random.randint(jax.random.fold_in(key, 1), (couples,), 0, 1 << 20) % (margin + 1)
    tallies = tallies.at[1:1 + 2 * couples:2].set(source_of - shifted).at[2:2 + 2 * couples:2].set(receiver + shifted)
    return tallies[jax.random.permutation(jax.random.fold_in(key, 2), amount)]


def assign_block(rng, own, number, rows, number_of, top, limit, skew):
    sequence = jax.random.permutation(rng, number_of)
    heavy_load, usual = load_shares(number_of, rows * top, limit, skew, True), load_shares(number_of, rows * top, limit, skew, False)
    places = jnp.arange(number_of)

    def named(lengths, turn):
        used = int((lengths > 0).sum())
        fixed = max(1, used // 4)
        passed = fixed + (places - fixed + turn * (used - fixed)) % max(1, number_of - fixed)
        return jnp.zeros((number_of,), jnp.int32).at[sequence[jnp.where(places < fixed, places, passed)]].set(jnp.asarray(lengths, jnp.int32))

    lengths = jnp.where(number % 4 == 0, named(heavy_load, number // 4), named(usual, number - number // 4 - 1))
    mixed = jax.random.permutation(jax.random.fold_in(own, 3), number_of)
    donor, taker = mixed[0:number_of // 2 * 2:2], mixed[1:number_of // 2 * 2:2]
    slack = jnp.minimum(lengths[donor] - 1, limit - lengths[taker]) // 2
    slack = jnp.where((donor == sequence[0]) | (taker == sequence[0]) | (lengths[taker] == 0), 0, jnp.maximum(slack, 0))
    passed = jax.random.randint(jax.random.fold_in(own, 4), (number_of // 2,), 0, 1 << 20) % (slack + 1)
    lengths = lengths.at[donor].add(-passed).at[taker].add(passed)
    items = jnp.searchsorted(jnp.cumsum(lengths), jnp.arange(rows * top), side="right").astype(jnp.int32)
    listing = items.reshape(top, rows).T
    listing = listing[jax.random.permutation(jax.random.fold_in(own, 1), rows)]
    turn = jax.random.randint(jax.random.fold_in(own, 2), (rows, 1), 0, top)
    return jnp.take_along_axis(listing, (jnp.arange(top)[None, :] + turn) % top, axis=1)


def load_shares(count, total, most, slope, full):
    weights = [(1 << 20) // math.isqrt(grade ** slope) + 1 for grade in range(1, count + 1)]
    largest = most if full else min(most, max(-(-total // count), total * weights[0] // sum(weights)))
    least = 1 if total - largest >= count - 1 else 0
    holding, spare = [largest] + [least] * (count - 1), total - largest - least * (count - 1)
    while spare > 0:
        free = [i for i in range(1, count) if holding[i] < largest] or [i for i in range(1, count) if holding[i] < most]
        mass, budget = sum([weights[i] for i in free]), spare
        for i in free:
            addition = min(most - holding[i], max(1, budget * weights[i] // mass), spare)
            holding[i] = holding[i] + addition
            spare = spare - addition
    return np.array(holding)


def centred(stream_key, dims, scale, limit, shards=(), kind=jnp.bfloat16):
    factor_of = shard_levels(stream_key, dims, shards, -0.22, 0.18) if shards else 1.0
    entries = jax.random.normal(stream_key, dims, jnp.float32) * scale * factor_of
    return jnp.minimum(jnp.maximum(entries, -limit), limit).astype(kind)


def setup_inputs(seed: int = 0) -> dict:
    splits = jax.random.split(jax.random.key(seed), 19)
    queries = draw_queries(jax.random.fold_in(splits[18], 71), 0)
    stretch_cache = draw_stretch_cache(jax.random.fold_in(splits[18], 71), 0)
    prefix_pool = centred(splits[2], (REQS * PAGES, PAGE, RANK + ROPE), 1.0, 6.0, ((0, 16),))
    page_table = jax.vmap(lambda own: jax.random.permutation(own, PAGES))(jax.random.split(splits[3], REQS)).reshape((REQS, PAGES)).astype(jnp.int32)
    prefix_len = uneven_parts(splits[4], REQS, REQS * LMAX // 2, LMAX, 2).astype(jnp.int32)
    prompt_cache = centred(splits[5], (2, SHARED, RANK + ROPE), 1.0, 6.0, ((1, 16),))
    prompt_len = uneven_parts(splits[6], 2, SHARED + SHARED // 2, SHARED, 0).astype(jnp.int32)
    group_ids = set_ends(jax.random.randint(splits[7], (REQS,), 0, 2), jax.random.fold_in(splits[7], 1), 0, 1).astype(jnp.int32)
    absorb_weight = centred(splits[8], (HEADS, NOPE, RANK), NOPE ** -0.5, 0.5, ((0, 2),))
    value_weight = centred(splits[9], (HEADS, RANK, VDIM), (RANK // 16) ** -0.5, 1.0, ((0, 2),))
    out_weight = centred(splits[10], (HEADS * VDIM, D), (HEADS * VDIM) ** -0.5, 0.125, ((0, 2),))
    residual = draw_residual(jax.random.fold_in(splits[18], 71), 0)
    norm_gain = jnp.clip(1.0 + 0.18 * jax.random.normal(splits[12], (D,), jnp.float32), 0.099609375, 1.8984375).astype(jnp.bfloat16)
    routes_keys = jax.random.split(jax.random.fold_in(splits[13], 1), TOKENS // TOK_DEV)
    routes_turns = jax.random.permutation(jax.random.fold_in(splits[13], 3), TOKENS // TOK_DEV)
    routes = jax.vmap(lambda own, number: assign_block(jax.random.fold_in(splits[13], 2), own, number, TOK_DEV, EXPERTS, TOP, CAP, 2))(routes_keys, routes_turns).reshape((TOKENS, TOP))
    route_weight = jnp.clip(0.05 + 0.39999999 * jax.random.uniform(splits[14], (TOKENS, TOP), jnp.float32) ** shard_levels(splits[14], (TOKENS, TOP), ((0, 16),), -0.2, 0.2), 0.05, 0.45)
    gate_weight = centred(splits[15], (EXPERTS, D, FF_EXP), D ** -0.5, 0.125, ((0, 16), (2, 2)))
    up_weight = centred(splits[16], (EXPERTS, D, FF_EXP), D ** -0.5, 0.125, ((0, 16), (2, 2)))
    down_weight = centred(splits[17], (EXPERTS, FF_EXP, D), FF_EXP ** -0.5, 0.15625, ((0, 16), (1, 2)))
    return dict(queries=queries, stretch_cache=stretch_cache, prefix_pool=prefix_pool, page_table=page_table, prefix_len=prefix_len, prompt_cache=prompt_cache, prompt_len=prompt_len, group_ids=group_ids, absorb_weight=absorb_weight, value_weight=value_weight, out_weight=out_weight, residual=residual, norm_gain=norm_gain, routes=routes, route_weight=route_weight, gate_weight=gate_weight, up_weight=up_weight, down_weight=down_weight)


NEGATIVE = -1e+30

def rounded(value):
    return lax.optimization_barrier(value.astype(jnp.bfloat16)).astype(jnp.float32)

def reference(queries, stretch_cache, prefix_pool, page_table, prefix_len, prompt_cache, prompt_len, group_ids, absorb_weight, value_weight, out_weight, residual, norm_gain, routes, route_weight, gate_weight, up_weight, down_weight):
    scale = 1.0 / math.sqrt(NOPE + ROPE)
    pools = prefix_pool.reshape(REQS, PAGES, PAGE, RANK + ROPE)
    absorb32 = absorb_weight.astype(jnp.float32)
    value32 = value_weight.astype(jnp.float32)
    span = SHARED + LMAX + TOK_DEV
    place = jnp.arange(span, dtype=jnp.int32)
    position = jnp.arange(TOK_DEV, dtype=jnp.int32)

    def one_request(item):
        query, stretch, pool, table, length, group = item
        q32 = query.astype(jnp.float32)
        nope_part = jnp.einsum('thn,hnr->thr', q32[:, :, :NOPE], absorb32)
        absorbed = rounded(jnp.concatenate([nope_part, q32[:, :, NOPE:]], axis=2))
        prompt = prompt_cache[group]
        prefix = pool[table].reshape(LMAX, RANK + ROPE)
        keys = jnp.concatenate([prompt, prefix, stretch], axis=0).astype(jnp.float32)
        in_prompt = place < prompt_len[group]
        in_prefix = (place >= SHARED) & (place < SHARED + length)
        in_stretch = (place >= SHARED + LMAX)[None, :] & ((place - SHARED - LMAX)[None, :] <= position[:, None])
        valid = (in_prompt | in_prefix)[None, :] | in_stretch
        scores = jnp.einsum('thc,kc->thk', absorbed, keys) * scale
        masked = jnp.where(valid[:, None, :], scores, NEGATIVE)
        top = lax.optimization_barrier(jnp.max(masked, axis=2, keepdims=True))
        weights = jnp.where(valid[:, None, :], jnp.exp(masked - top), 0.0)
        total = lax.optimization_barrier(jnp.sum(weights, axis=2, keepdims=True))
        latent = jnp.einsum('thk,kr->thr', rounded(weights), keys[:, :RANK]) / total
        latent = rounded(latent)
        return jnp.einsum('thr,hrv->thv', latent, value32).astype(jnp.bfloat16)
    heads_out = lax.map(one_request, (queries.reshape(REQS, TOK_DEV, HEADS, NOPE + ROPE), stretch_cache.reshape(REQS, TOK_DEV, RANK + ROPE), pools, page_table, prefix_len, group_ids))
    projected = jnp.dot(heads_out.reshape(TOKENS, HEADS * VDIM), out_weight, preferred_element_type=jnp.float32)
    attended = (residual.astype(jnp.float32) + projected).astype(jnp.bfloat16)
    stream = attended.astype(jnp.float32)
    square_mean = lax.optimization_barrier(jnp.mean(stream * stream, axis=1, keepdims=True))
    normed = (stream * lax.rsqrt(square_mean + 1e-06) * norm_gain.astype(jnp.float32)).astype(jnp.bfloat16)
    flat = routes.reshape(REQS, TOK_DEV * TOP).astype(jnp.int32)
    onehot = (flat[:, :, None] == jnp.arange(EXPERTS, dtype=jnp.int32)[None, None, :]).astype(jnp.int32)
    slot = (lax.optimization_barrier(jnp.sum(jnp.cumsum(onehot, axis=1) * onehot, axis=2)) - 1).astype(jnp.int32)
    source = jnp.arange(REQS, dtype=jnp.int32)[:, None]
    dest = (flat * (REQS * CAP) + source * CAP + slot).astype(jnp.int32).reshape(-1)
    token_index = (source * TOK_DEV + jnp.arange(TOK_DEV * TOP, dtype=jnp.int32)[None, :] // TOP).astype(jnp.int32).reshape(-1)
    token_of = jnp.full((EXPERTS * REQS * CAP,), TOKENS, dtype=jnp.int32).at[dest].set(token_index)
    weight_of = jnp.zeros((EXPERTS * REQS * CAP,), jnp.float32).at[dest].set(route_weight.reshape(-1).astype(jnp.float32))
    padded = jnp.concatenate([normed, jnp.zeros((1, D), jnp.bfloat16)], axis=0)

    def expert_step(total, item):
        index, weights, gate_w, up_w, down_w = item
        rows = padded[index]
        gate = jnp.dot(rows, gate_w, preferred_element_type=jnp.float32)
        up = jnp.dot(rows, up_w, preferred_element_type=jnp.float32)
        hidden = (jax.nn.silu(gate) * up).astype(jnp.bfloat16)
        groups = hidden.astype(jnp.float32).reshape(REQS * CAP, N_TP, FF_EXP // N_TP)
        downs = down_w.astype(jnp.float32).reshape(N_TP, FF_EXP // N_TP, D)
        parts = jnp.einsum('rgf,gfd->grd', groups, downs).astype(jnp.bfloat16)
        contrib = lax.optimization_barrier(jnp.sum(parts.astype(jnp.float32), axis=0)) * weights[:, None]
        return (total.at[index].add(contrib), None)
    start = jnp.zeros((TOKENS + 1, D), jnp.float32)
    total, _ = lax.scan(expert_step, start, (token_of.reshape(EXPERTS, REQS * CAP), weight_of.reshape(EXPERTS, REQS * CAP), gate_weight, up_weight, down_weight))
    mixed = (stream + total[:TOKENS]).astype(jnp.bfloat16)
    return (attended, mixed)
```

```python
import jax
import jax.numpy as jnp
from jax import lax
from jax.experimental import pallas as pl
from jax.experimental.pallas import tpu as pltpu
from jax.sharding import PartitionSpec as P

NEGATIVE = -1e30
EPSILON = 1e-06


def on_device(
    queries, stretch_cache, prefix_pool, page_table, prefix_len, prompt_cache, prompt_len,
    group_ids, absorb_weight, value_weight, out_weight, residual, norm_gain, routes,
    route_weight, gate_weight, up_weight, down_weight,
):
    tokens = queries.shape[0]
    prompts = lax.all_gather(prompt_cache, "req", axis=1, tiled=True)
    projected = attend(
        queries, stretch_cache, prefix_pool, page_table, prefix_len, prompts, prompt_len,
        group_ids, absorb_weight, value_weight, out_weight,
    )
    attention_part = lax.psum_scatter(
        projected.astype(jnp.bfloat16), "tp", scatter_dimension=1, tiled=True
    ).astype(jnp.float32)
    attended = (residual.astype(jnp.float32) + attention_part).astype(jnp.bfloat16)
    stream = attended.astype(jnp.float32)
    squares = lax.psum(jnp.sum(stream * stream, axis=1), "tp")
    model_width = out_weight.shape[1]
    normed = (
        stream * lax.rsqrt(squares / model_width + EPSILON)[:, None] * norm_gain.astype(jnp.float32)
    ).astype(jnp.bfloat16)
    experts = lax.axis_size("req")
    top = routes.shape[1]
    capacity = max(2, tokens * top * 4 // (3 * experts))
    choice = routes[:, :, None] == jnp.arange(experts, dtype=jnp.int32)[None, None, :]
    share = jnp.sum(jnp.where(choice, route_weight[:, :, None], 0.0), axis=1).T
    named = share > 0.0
    before = jnp.arange(tokens)[:, None] <= jnp.arange(tokens)[None, :]
    slot = jnp.dot(
        named.astype(jnp.bfloat16), before.astype(jnp.bfloat16), preferred_element_type=jnp.float32
    ).astype(jnp.int32) - 1
    picks = (
        slot[:, None, :] == jnp.arange(capacity, dtype=jnp.int32)[None, :, None]
    ) & named[:, None, :]
    chooser = picks.astype(jnp.bfloat16).reshape(experts * capacity, tokens)
    level = jnp.sum(jnp.where(picks, share[:, None, :], 0.0), axis=2)
    whole = lax.all_gather(normed, "tp", axis=1, tiled=True)
    buffer = (
        jnp.dot(chooser, whole, preferred_element_type=jnp.float32)
        .astype(jnp.bfloat16)
        .reshape(experts, capacity, -1)
    )
    received = lax.all_to_all(buffer, "req", split_axis=0, concat_axis=0, tiled=True)
    gate = jnp.einsum("snd,df->snf", received, gate_weight[0], preferred_element_type=jnp.float32)
    up = jnp.einsum("snd,df->snf", received, up_weight[0], preferred_element_type=jnp.float32)
    hidden = (jax.nn.silu(gate) * up).astype(jnp.bfloat16)
    part_out = jnp.einsum(
        "snf,fd->snd", hidden, down_weight[0], preferred_element_type=jnp.float32
    ).astype(jnp.bfloat16)
    returned = lax.all_to_all(part_out, "req", split_axis=0, concat_axis=0, tiled=True)
    weighted = (returned.astype(jnp.float32) * level[:, :, None]).astype(jnp.bfloat16)
    combined = lax.dot_general(
        chooser, weighted.reshape(experts * capacity, -1), (((0,), (0,)), ((), ())),
        preferred_element_type=jnp.float32,
    )
    expert_part = lax.psum_scatter(
        combined.astype(jnp.bfloat16), "tp", scatter_dimension=1, tiled=True
    ).astype(jnp.float32)
    mixed = (stream + expert_part).astype(jnp.bfloat16)
    return (attended, mixed)


def attend(
    queries, stretch_cache, prefix_pool, page_table, prefix_len, prompts, prompt_len,
    group_ids, absorb_weight, value_weight, out_weight,
):
    tokens, heads, width = queries.shape
    nope, rank = absorb_weight.shape[1], value_weight.shape[1]
    me = lax.axis_index("req")
    requests = jnp.arange(group_ids.shape[0], dtype=jnp.int32) == me
    group = jnp.sum(jnp.where(requests, group_ids, 0))
    own_length = jnp.sum(jnp.where(requests, prefix_len, 0))
    prompt_length = jnp.where(group == 0, prompt_len[0], prompt_len[1])
    pages, page = prefix_pool.shape[:2]
    order = jnp.arange(pages, dtype=jnp.int32)
    logical = jnp.sum(
        jnp.where(page_table[0][None, :] == order[:, None], order[None, :], 0), axis=1
    )
    prefix_at = (logical[:, None] * page + jnp.arange(page, dtype=jnp.int32)[None, :]).reshape(-1)
    prompt = jnp.where(group == 0, prompts[0], prompts[1])
    keys = jnp.concatenate(
        [stretch_cache, prompt, prefix_pool.reshape(pages * page, -1)], axis=0
    )
    seen = jnp.concatenate(
        [jnp.arange(prompt.shape[0]) < prompt_length, prefix_at < own_length]
    )
    token = jnp.arange(tokens)
    visible = jnp.concatenate(
        [
            token[None, :] <= token[:, None],
            jnp.broadcast_to(seen[None, :], (tokens, seen.shape[0])),
        ],
        axis=1,
    )
    turned = jnp.transpose(queries, (1, 0, 2))
    absorbed = jnp.concatenate(
        [
            jnp.einsum(
                "htn,hnr->htr", turned[:, :, :nope], absorb_weight,
                preferred_element_type=jnp.float32,
            ).astype(jnp.bfloat16),
            turned[:, :, nope:],
        ],
        axis=2,
    )
    scores = jnp.einsum("htc,kc->htk", absorbed, keys, preferred_element_type=jnp.float32)
    scores = jnp.where(visible[None], scores * width ** (-0.5), NEGATIVE)
    weights = jnp.exp(scores - jnp.max(scores, axis=2, keepdims=True))
    weights = jnp.where(visible[None], weights, 0.0)
    totals = jnp.sum(weights, axis=2, keepdims=True)
    latent = jnp.einsum(
        "htk,kr->htr", weights.astype(jnp.bfloat16), keys[:, :rank],
        preferred_element_type=jnp.float32,
    )
    latent = (latent / totals).astype(jnp.bfloat16)
    heads_out = jnp.einsum(
        "htr,hrv->thv", latent, value_weight, preferred_element_type=jnp.float32
    ).astype(jnp.bfloat16)
    return jnp.dot(
        heads_out.reshape(tokens, -1), out_weight, preferred_element_type=jnp.float32
    )


MESH = pl.DeviceIdType.MESH


def coordinates():
    me = lax.axis_index("req")
    return me // 4, (me // 2) % 2, me % 2, lax.axis_index("tp")


def place(z, x, core, y):
    return {"req": (z * 2 + x) * 2 + core, "tp": y}


def prompt_kernel(block_ref, share_ref, keys_ref, mine_ref, send, recv, send_w, recv_w, local):
    me = lax.axis_index("req")
    y = lax.axis_index("tp")
    barrier = pltpu.get_barrier_semaphore()
    for step in range(1, 16):
        pl.semaphore_signal(
            barrier, inc=1, device_id={"req": (me + step) % 16, "tp": y}, device_id_type=MESH
        )
    pl.semaphore_wait(barrier, 15)
    rows = pl.ds(pl.multiple_of(me * 16, 16), 16)

    def shares(step):
        peer = (me + step) % 16
        return pltpu.make_async_remote_copy(
            share_ref.at[peer], mine_ref.at[me], send_w.at[step], recv_w.at[step],
            device_id={"req": peer, "tp": y}, device_id_type=MESH,
        )

    core, other = me % 2, me + 1 - 2 * (me % 2)

    def relay(step):
        source = (me + 2 * step) % 16
        lines = pl.ds(pl.multiple_of(source * 16, 16), 16)
        arrival = pltpu.make_async_remote_copy(
            keys_ref.at[:, lines, :], keys_ref.at[:, lines, :], send.at[8 - step],
            recv.at[8 - step], device_id={"req": source, "tp": y}, device_id_type=MESH,
        )
        passing = pltpu.make_async_remote_copy(
            keys_ref.at[:, lines, :], keys_ref.at[:, lines, :], send.at[8 + source // 2],
            recv.at[8 + source // 2], device_id={"req": other, "tp": y}, device_id_type=MESH,
        )
        return arrival, passing

    def arriving(step):
        source = (me + 2 * step) % 16 + 1 - 2 * core
        lines = pl.ds(pl.multiple_of(source * 16, 16), 16)
        return pltpu.make_async_remote_copy(
            keys_ref.at[:, lines, :], keys_ref.at[:, lines, :], send.at[8 + source // 2],
            recv.at[8 + source // 2], device_id={"req": other, "tp": y}, device_id_type=MESH,
        )

    def direct(step):
        return pltpu.make_async_remote_copy(
            block_ref, keys_ref.at[:, rows, :], send.at[step], recv.at[step],
            device_id={"req": (me + 2 * step) % 16, "tp": y}, device_id_type=MESH,
        )

    home = pltpu.make_async_remote_copy(
        block_ref, keys_ref.at[:, rows, :], send.at[8 + me // 2], recv.at[8 + me // 2],
        device_id={"req": other, "tp": y}, device_id_type=MESH,
    )
    for step in range(1, 8):
        direct(step).start()
    home.start()
    for step in range(1, 16):
        shares(step).start()
    own = pltpu.make_async_copy(block_ref, keys_ref.at[:, rows, :], local.at[0])
    own_share = pltpu.make_async_copy(share_ref.at[me], mine_ref.at[me], local.at[1])
    own.start()
    own_share.start()
    own.wait()
    own_share.wait()
    for step in range(1, 8):
        arrival, passing = relay(step)
        arrival.wait_recv()
        passing.start()
    for step in range(8):
        arriving(step).wait_recv()
    home.wait_send()
    for step in range(1, 8):
        direct(step).wait_send()
        relay(step)[1].wait_send()
    for step in range(1, 16):
        shares(step).wait()


def share_prompts(prompt_cache, share):
    groups, rows, width = prompt_cache.shape
    tokens = share.shape[2]
    return pl.pallas_call(
        prompt_kernel,
        out_shape=(
            jax.ShapeDtypeStruct((groups, rows * 16, width), prompt_cache.dtype),
            jax.ShapeDtypeStruct((16, 1, tokens), jnp.float32),
        ),
        in_specs=[pl.BlockSpec(memory_space=pltpu.VMEM)] * 2,
        out_specs=(pl.BlockSpec(memory_space=pltpu.VMEM),) * 2,
        scratch_shapes=[pltpu.SemaphoreType.DMA((16,))] * 4 + [pltpu.SemaphoreType.DMA((2,))],
        compiler_params=pltpu.CompilerParams(collective_id=0, has_side_effects=True),
    )(prompt_cache, share)


def greet():
    z, x, core, y = coordinates()
    me = lax.axis_index("req")
    barrier = pltpu.get_barrier_semaphore()
    for step in range(1, 16):
        pl.semaphore_signal(
            barrier, inc=1, device_id={"req": (me + step) % 16, "tp": y}, device_id_type=MESH
        )
    pl.semaphore_signal(barrier, inc=1, device_id=place(z, x, core, 1 - y), device_id_type=MESH)
    pl.semaphore_wait(barrier, 16)


def plane_at(place_in_turn):
    z = coordinates()[0]
    high = z // 2
    near = z + high * (3 - 2 * z)
    late = place_in_turn // 2
    odd = place_in_turn % 2
    first = (1 - odd) * (1 - late) * near + odd * (1 - late) * (1 - near) + late * place_in_turn
    return first + high * (3 - 2 * first)


def spread_tokens(whole, send, recv):
    z, x, core, y = coordinates()
    half_rows, half_cols = whole.shape[1] // 2, whole.shape[2] // 2

    def piece(zp, xp, yp, half, cp):
        return whole.at[
            (zp * 2 + xp) * 2 + cp,
            pl.ds(half * half_rows, half_rows),
            pl.ds(pl.multiple_of(yp * half_cols, half_cols), half_cols),
        ]

    def hop(zp, xp, yp, half, cp, kind, peer):
        slot = zp * 8 + xp * 4 + yp * 2 + half
        part = piece(zp, xp, yp, half, cp)
        return pltpu.make_async_remote_copy(
            part, part, send.at[kind, slot], recv.at[cp, slot], device_id=peer, device_id_type=MESH
        )

    up, down = place(z + 1, x, core, y), place(z - 1, x, core, y)
    over_x, over_y, other = place(z, 1 - x, core, y), place(z, x, core, 1 - y), place(z, x, 1 - core, y)

    def column(zp, finish, halves=(0, 1)):
        for half in halves:
            for go, kind, peer in (
                ((zp <= z) & (z < 3), 0, up), ((zp >= z) & (z > 0), 1, down)
            ):
                @pl.when(go)
                def _(kind=kind, peer=peer, half=half):
                    copy = hop(zp, x, y, half, core, kind, peer)
                    copy.wait_send() if finish else copy.start()
        for kind, peer, half in ((2, over_x, 0), (3, over_y, 1), (2, over_x, 1), (3, over_y, 0)):
            if half in halves:
                copy = hop(zp, x, y, half, core, kind, peer)
                copy.wait_send() if finish else copy.start()
        for half in halves:
            copy = hop(zp, x, y, half, core, 4, other)
            copy.wait_send() if finish else copy.start()

    def arrive(zp):
        for half in range(2):
            hop(zp, x, y, half, core, 0, over_x).wait_recv()
        column(zp, False)

    def beside(zp, finish):
        if not finish:
            for half in range(2):
                hop(zp, 1 - x, y, half, core, 2, over_x).wait_recv()
                hop(zp, x, 1 - y, half, core, 3, over_y).wait_recv()
        copies = [hop(zp, 1 - x, y, 0, core, 3, over_y), hop(zp, x, 1 - y, 1, core, 2, over_x)]
        for half in range(2):
            copies.append(hop(zp, 1 - x, y, half, core, 4, other))
            copies.append(hop(zp, x, 1 - y, half, core, 4, other))
        for copy in copies:
            copy.wait_send() if finish else copy.start()

    def diagonal(zp, finish):
        for half in range(2):
            copy = hop(zp, 1 - x, 1 - y, half, core, 4, other)
            if finish:
                copy.wait_send()
            else:
                hop(zp, 1 - x, 1 - y, half, core, 2, over_x).wait_recv()
                copy.start()

    def complete(zp):
        for xp in range(2):
            for yp in range(2):
                for half in range(2):
                    hop(zp, xp, yp, half, 1 - core, 4, other).wait_recv()

    def close(zp):
        column(zp, True)
        beside(zp, True)
        diagonal(zp, True)

    return column, arrive, beside, diagonal, complete, close


def return_sums(parts, part_in, chooser, acc, x_diag, y_diag, x_in, y_in, z_in, sems):
    z, x, core, y = coordinates()
    rows, half_cols = acc.shape[2], acc.shape[3] // 2
    half_rows = rows // 2
    over_x, over_y, other = place(z, 1 - x, core, y), place(z, x, core, 1 - y), place(z, x, 1 - core, y)
    mine = pl.ds(pl.multiple_of(y * half_cols, half_cols), half_cols)
    theirs = pl.ds(pl.multiple_of((1 - y) * half_cols, half_cols), half_cols)
    top, low = pl.ds(0, half_rows), pl.ds(half_rows, half_rows)

    def copy(source, target, kind, zp, peer):
        return pltpu.make_async_remote_copy(
            source, target, sems.at[0, kind, zp], sems.at[1, kind, zp],
            device_id=peer, device_id_type=MESH,
        )

    def core_copy(zp, xp):
        return copy(parts.at[zp, xp * 2 + 1 - core], part_in.at[zp, xp], xp, zp, other)

    def diag_copies(zp):
        far = acc.at[zp, 1 - x]
        return (
            copy(far.at[top, theirs], y_diag.at[zp], 2, zp, over_y),
            copy(far.at[low, theirs], x_diag.at[zp], 3, zp, over_x),
        )

    def free_copies(zp):
        return (
            copy(acc.at[zp, 1 - x].at[low, mine], x_in.at[zp, low], 4, zp, over_x),
            copy(acc.at[zp, x].at[top, theirs], y_in.at[zp, top], 5, zp, over_y),
        )

    def last_copies(zp):
        return (
            copy(acc.at[zp, 1 - x].at[top, mine], x_in.at[zp, top], 6, zp, over_x),
            copy(acc.at[zp, x].at[low, theirs], y_in.at[zp, low], 7, zp, over_y),
        )

    def plane_copy(zp):
        return pltpu.make_async_remote_copy(
            acc.at[zp, x].at[:, mine], z_in.at[z], sems.at[0, 8, zp], sems.at[1, 8, z],
            device_id=place(zp, x, core, y), device_id_type=MESH,
        )

    def plane_arrival(zp):
        return pltpu.make_async_remote_copy(
            acc.at[zp, x].at[:, mine], z_in.at[zp], sems.at[0, 8, zp], sems.at[1, 8, zp],
            device_id=place(zp, x, core, y), device_id_type=MESH,
        )

    def add(target, *terms):
        total = target[...].astype(jnp.float32)
        for term in terms:
            total = total + term[...].astype(jnp.float32)
        target[...] = total.astype(target.dtype)

    def cores(zp):
        down = (((0,), (0,)), ((), ()))
        for xp in range(2):
            core_copy(zp, xp).wait_recv()
            request = (zp * 2 + xp) * 2 + core
            total = lax.dot_general(
                chooser[0, request], parts[zp, xp * 2 + core], down,
                preferred_element_type=jnp.float32,
            ) + lax.dot_general(
                chooser[1, request], part_in[zp, xp], down, preferred_element_type=jnp.float32
            )
            acc[zp, xp] = total.astype(jnp.bfloat16)
        for item in diag_copies(zp) + free_copies(zp):
            item.start()

    def corners(zp):
        from_y, from_x = diag_copies(zp)
        over_x_copy, over_y_copy = last_copies(zp)
        from_y.wait_recv()
        add(acc.at[zp, 1 - x].at[top, mine], y_diag.at[zp])
        over_x_copy.start()
        from_x.wait_recv()
        add(acc.at[zp, x].at[low, theirs], x_diag.at[zp])
        over_y_copy.start()

    def arrivals(zp):
        for item in free_copies(zp) + last_copies(zp):
            item.wait_recv()

    def columns(zp):
        arrivals(zp)
        add(acc.at[zp, x].at[:, mine], x_in.at[zp], y_in.at[zp])
        plane_copy(zp).start()

    def final(attended, mixed):
        arrivals(z)
        total = attended[...].astype(jnp.float32) + acc[z, x, :, mine].astype(jnp.float32)
        total = total + x_in[z].astype(jnp.float32) + y_in[z].astype(jnp.float32)
        for turn in range(1, 4):
            zp = plane_at(turn)
            plane_arrival(zp).wait_recv()
            total = total + z_in[zp].astype(jnp.float32)
        mixed[...] = total.astype(jnp.bfloat16)

    def close(zp):
        for xp in range(2):
            core_copy(zp, xp).wait_send()
        for item in diag_copies(zp) + free_copies(zp) + last_copies(zp):
            item.wait_send()

        @pl.when(zp != z)
        def _():
            plane_copy(zp).wait_send()

    return core_copy, cores, corners, columns, final, close


def choose(mine, chooser, which):
    requests, tokens = mine.shape
    capacity = chooser.shape[2]
    named = jnp.where(mine[...] > 0.0, 1.0, 0.0)
    rows = lax.broadcasted_iota(jnp.int32, (tokens, tokens), 0)
    columns = lax.broadcasted_iota(jnp.int32, (tokens, tokens), 1)
    before = jnp.where(rows <= columns, 1.0, 0.0).astype(jnp.bfloat16)
    slot = jnp.dot(named.astype(jnp.bfloat16), before, preferred_element_type=jnp.float32)
    wanted = jnp.where(named > 0.0, slot - 1.0, -1.0).astype(jnp.int32)
    places = lax.broadcasted_iota(jnp.int32, (capacity, tokens), 0)
    for request in range(requests):
        picks = jnp.where(wanted[request : request + 1, :] == places, 1.0, 0.0)
        chooser[which, request] = picks.astype(jnp.bfloat16)


def expert_kernel(
    projected, residual, gain, mine_share, gate_hbm, up_hbm, down_hbm,
    attended, mixed,
    whole, outgoing, incoming, squares_out, squares_in, gains, other_share, roots, chooser, level,
    gate_w, up_w, down_w, rows, hidden, parts, part_in, acc, x_diag, y_diag, x_in, y_in, z_in,
    pair_sems, load_sems, root_sems, send, recv, sems,
):
    z, x, core, y = coordinates()
    me = lax.axis_index("req")
    tokens, half_cols = residual.shape
    half_rows = tokens // 2
    loads = [
        pltpu.make_async_copy(source, target, load_sems.at[index])
        for index, (source, target) in enumerate(
            ((gate_hbm, gate_w), (up_hbm, up_w), (down_hbm, down_w))
        )
    ]
    for load in loads:
        load.start()
    mine = pl.ds(pl.multiple_of(y * half_cols, half_cols), half_cols)
    theirs = pl.ds(pl.multiple_of((1 - y) * half_cols, half_cols), half_cols)
    over_y, other = place(z, x, core, 1 - y), place(z, x, 1 - core, y)

    def pair(source, target, index, peer=over_y):
        return pltpu.make_async_remote_copy(
            source, target, pair_sems.at[0, index], pair_sems.at[1, index],
            device_id=peer, device_id_type=MESH,
        )

    def swap(half):
        lines = pl.ds(half * half_rows, half_rows)
        return pair(outgoing.at[lines], incoming.at[lines], half)

    outgoing[...] = projected[:, theirs].astype(jnp.bfloat16)
    gains[y] = gain[...]
    greet()
    swap(0).start()
    swap(1).start()
    squares = pair(squares_out, squares_in, 2)
    gain_copy = pair(gains.at[y], gains.at[y], 3)
    share_copy = pair(mine_share, other_share, 4, other)
    share_copy.start()
    gain_copy.start()
    choose(mine_share, chooser, 0)
    column, arrive, beside, diagonal, complete, close_spread = spread_tokens(whole, send, recv)
    diag = lax.broadcasted_iota(jnp.int32, (half_rows, tokens), 1) - lax.broadcasted_iota(
        jnp.int32, (half_rows, tokens), 0
    )
    sums = jnp.zeros((1, tokens), jnp.float32)
    for half in range(2):
        lines = pl.ds(half * half_rows, half_rows)
        swap(half).wait_recv()
        stream = (
            residual[lines, :].astype(jnp.float32)
            + projected[lines, mine]
            + incoming[lines, :].astype(jnp.float32)
        )
        rounded = stream.astype(jnp.bfloat16)
        attended[lines, :] = rounded
        whole[me, lines, mine] = rounded
        stream = rounded.astype(jnp.float32)
        line_sums = jnp.sum(stream * stream, axis=1, keepdims=True)
        sums = sums + jnp.sum(
            jnp.where(diag == half * half_rows, line_sums, 0.0), axis=0, keepdims=True
        )
        if half == 1:
            squares_out[...] = sums
            squares.start()
        column(z, False, (half,))
    share_copy.wait_recv()
    choose(other_share, chooser, 1)

    def root_copy(step):
        peer = (me + step) % 16
        return pltpu.make_async_remote_copy(
            roots.at[me], roots.at[me], root_sems.at[0, peer], root_sems.at[1, me],
            device_id={"req": peer, "tp": y}, device_id_type=MESH,
        )

    def root_arrival(request):
        return pltpu.make_async_remote_copy(
            roots.at[request], roots.at[request], root_sems.at[0, request],
            root_sems.at[1, request], device_id=over_y, device_id_type=MESH,
        )

    arrive(plane_at(1))
    beside(z, False)
    squares.wait_recv()
    roots[me] = lax.rsqrt((squares_out[...] + squares_in[...]) / (2 * half_cols) + EPSILON)

    def send_root(step, carry):
        root_copy(step).start()
        return carry

    lax.fori_loop(1, 16, send_root, 0)
    gain_copy.wait_recv()
    for load in loads:
        load.wait()
    capacity = chooser.shape[2]
    core_copy, cores, corners, columns, final, close_return = return_sums(
        parts, part_in, chooser, acc, x_diag, y_diag, x_in, y_in, z_in, sems
    )

    def compute(zp):
        for index in range(4):
            request = zp * 4 + index

            @pl.when(request != me)
            def _(request=request):
                root_arrival(request).wait_recv()

        for index in range(4):
            request = zp * 4 + index
            lines = pl.ds(index * capacity, capacity)
            picks = chooser[0, request]
            picked = jnp.dot(picks, whole[request], preferred_element_type=jnp.float32)
            wide = picks.astype(jnp.float32)
            picked = picked * jnp.sum(wide * roots[request], axis=1, keepdims=True)
            share = jnp.sum(
                wide * mine_share[pl.ds(request, 1), :], axis=1, keepdims=True
            )
            level[lines, :] = jnp.broadcast_to(share, (capacity, level.shape[1]))
            for side in range(2):
                span = pl.ds(side * half_cols, half_cols)
                scaled = picked[:, side * half_cols : (side + 1) * half_cols] * gains[side]
                rows[lines, span] = scaled.astype(jnp.bfloat16)
        across = (((1,), (1,)), ((), ()))
        gate = lax.dot_general(rows[...], gate_w[...], across, preferred_element_type=jnp.float32)
        up = lax.dot_general(rows[...], up_w[...], across, preferred_element_type=jnp.float32)
        hidden[...] = (gate / (1.0 + jnp.exp(-gate)) * up * level[:, :1]).astype(jnp.bfloat16)
        part = jnp.dot(hidden[...], down_w[...], preferred_element_type=jnp.float32)
        for index in range(4):
            parts[zp, index] = part[index * capacity : (index + 1) * capacity].astype(jnp.bfloat16)
        for xp in range(2):
            core_copy(zp, xp).start()

    def step(turn, carry):
        @pl.when(turn < 3)
        def _():
            arrive(plane_at(turn + 1))

        @pl.when(turn < 4)
        def _():
            beside(plane_at(turn), False)

        @pl.when((turn >= 4) & (turn < 8))
        def _():
            cores(plane_at((turn - 3) % 4))

        @pl.when(turn < 5)
        def _():
            zp = plane_at(turn - 1)
            diagonal(zp, False)
            complete(zp)
            compute(zp)

        @pl.when((turn >= 5) & (turn < 9))
        def _():
            corners(plane_at((turn - 4) % 4))

        @pl.when((turn >= 6) & (turn < 9))
        def _():
            columns(plane_at(turn - 5))

        return carry

    lax.fori_loop(1, 9, step, 0)
    final(attended, mixed)

    def close(zp, carry):
        close_spread(zp)
        close_return(zp)
        return carry

    lax.fori_loop(0, 4, close, 0)

    def close_root(step, carry):
        root_copy(step).wait_send()
        return carry

    lax.fori_loop(1, 16, close_root, 0)
    for item in (swap(0), swap(1), squares, gain_copy, share_copy):
        item.wait_send()


def run_experts(projected, residual, gain, mine, gate_w, up_w, down_w, capacity):
    tokens, width = projected.shape
    half = residual.shape[1]
    units = gate_w.shape[0]
    bf16, f32 = jnp.bfloat16, jnp.float32
    dma = pltpu.SemaphoreType.DMA
    vmem = pl.BlockSpec(memory_space=pltpu.VMEM)
    anywhere = pl.BlockSpec(memory_space=pl.ANY)
    return pl.pallas_call(
        expert_kernel,
        out_shape=(jax.ShapeDtypeStruct((tokens, half), bf16),) * 2,
        in_specs=[vmem] * 4 + [anywhere] * 3,
        out_specs=(vmem, vmem),
        scratch_shapes=[
            pltpu.VMEM((16, tokens, width), bf16),
            pltpu.VMEM((tokens, half), bf16),
            pltpu.VMEM((tokens, half), bf16),
            pltpu.VMEM((1, tokens), f32),
            pltpu.VMEM((1, tokens), f32),
            pltpu.VMEM((2, 1, half), f32),
            pltpu.VMEM((16, tokens), f32),
            pltpu.VMEM((16, 1, tokens), f32),
            pltpu.VMEM((2, 16, capacity, tokens), bf16),
            pltpu.VMEM((4 * capacity, 128), f32),
            pltpu.VMEM((units, width), bf16),
            pltpu.VMEM((units, width), bf16),
            pltpu.VMEM((units, width), bf16),
            pltpu.VMEM((4 * capacity, width), bf16),
            pltpu.VMEM((4 * capacity, units), bf16),
            pltpu.VMEM((4, 4, capacity, width), bf16),
            pltpu.VMEM((4, 2, capacity, width), bf16),
            pltpu.VMEM((4, 2, tokens, width), bf16),
            pltpu.VMEM((4, tokens // 2, half), bf16),
            pltpu.VMEM((4, tokens // 2, half), bf16),
            pltpu.VMEM((4, tokens, half), bf16),
            pltpu.VMEM((4, tokens, half), bf16),
            pltpu.VMEM((4, tokens, half), bf16),
            dma((2, 5)),
            dma((3,)),
            dma((2, 16)),
            dma((5, 32)),
            dma((2, 32)),
            dma((2, 9, 4)),
        ],
        compiler_params=pltpu.CompilerParams(
            collective_id=1, has_side_effects=True, vmem_limit_bytes=58 << 20
        ),
    )(projected, residual, gain, mine, gate_w, up_w, down_w)


def on_block(
    queries, stretch_cache, prefix_pool, page_table, prefix_len, prompt_cache, prompt_len,
    group_ids, absorb_weight, value_weight, out_weight, residual, norm_gain, routes,
    route_weight, gate_weight, up_weight, down_weight,
):
    tokens, heads, width = queries.shape
    nope, rank = absorb_weight.shape[1], value_weight.shape[1]
    experts, top = lax.axis_size("req"), routes.shape[1]
    capacity = max(2, tokens * top * 4 // (3 * experts))
    me = lax.axis_index("req")
    choice = routes[:, :, None] == jnp.arange(experts, dtype=jnp.int32)[None, None, :]
    share = jnp.sum(jnp.where(choice, route_weight[:, :, None], 0.0), axis=1)
    prompts, mine = share_prompts(prompt_cache, share.T[:, None, :])
    mine = mine[:, 0, :]
    requests = jnp.arange(group_ids.shape[0], dtype=jnp.int32) == me
    group = jnp.sum(jnp.where(requests, group_ids, 0))
    own_length = jnp.sum(jnp.where(requests, prefix_len, 0))
    prompt_length = jnp.where(group == 0, prompt_len[0], prompt_len[1])
    pages, page = prefix_pool.shape[:2]
    order = jnp.arange(pages, dtype=jnp.int32)
    logical = jnp.sum(
        jnp.where(page_table[0][None, :] == order[:, None], order[None, :], 0), axis=1
    )
    prefix_at = (logical[:, None] * page + jnp.arange(page, dtype=jnp.int32)[None, :]).reshape(-1)
    prompt = jnp.where(group == 0, prompts[0], prompts[1])
    keys = jnp.concatenate(
        [stretch_cache, prompt, prefix_pool.reshape(pages * page, -1)], axis=0
    )
    seen = jnp.concatenate(
        [jnp.arange(prompt.shape[0]) < prompt_length, prefix_at < own_length]
    )
    token = jnp.arange(tokens)
    visible = jnp.concatenate(
        [
            token[None, :] <= token[:, None],
            jnp.broadcast_to(seen[None, :], (tokens, seen.shape[0])),
        ],
        axis=1,
    )
    turned = jnp.transpose(queries, (1, 0, 2))
    absorbed = jnp.concatenate(
        [
            jnp.einsum(
                "htn,hnr->htr", turned[:, :, :nope], absorb_weight,
                preferred_element_type=jnp.float32,
            ).astype(jnp.bfloat16),
            turned[:, :, nope:],
        ],
        axis=2,
    )
    scores = jnp.einsum("htc,kc->htk", absorbed, keys, preferred_element_type=jnp.float32)
    scores = jnp.where(visible[None], scores * width ** (-0.5), NEGATIVE)
    weights = jnp.exp(scores - jnp.max(scores, axis=2, keepdims=True))
    weights = jnp.where(visible[None], weights, 0.0)
    totals = jnp.sum(weights, axis=2, keepdims=True)
    latent = jnp.einsum(
        "htk,kr->htr", weights.astype(jnp.bfloat16), keys[:, :rank],
        preferred_element_type=jnp.float32,
    )
    latent = (latent / totals).astype(jnp.bfloat16)
    heads_out = jnp.einsum(
        "htr,hrv->thv", latent, value_weight, preferred_element_type=jnp.float32
    ).astype(jnp.bfloat16)
    projected = jnp.dot(
        heads_out.reshape(tokens, -1), out_weight, preferred_element_type=jnp.float32
    )
    return run_experts(
        projected, residual, norm_gain[None, :].astype(jnp.float32), mine,
        jnp.swapaxes(gate_weight[0], 0, 1), jnp.swapaxes(up_weight[0], 0, 1), down_weight[0],
        capacity,
    )


def solution(mesh):
    in_specs = (
        P("req", "tp", None),
        P("req", None),
        P("req", None, None),
        P("req", None),
        P(),
        P(None, "req", None),
        P(),
        P(),
        P("tp", None, None),
        P("tp", None, None),
        P("tp", None),
        P("req", "tp"),
        P("tp"),
        P("req", None),
        P("req", None),
        P("req", None, "tp"),
        P("req", None, "tp"),
        P("req", "tp", None),
    )
    out_specs = (P("req", "tp"), P("req", "tp"))
    body = on_block if mesh.shape["req"] == 16 and mesh.shape["tp"] == 2 else on_device
    return jax.shard_map(
        body, mesh=mesh, in_specs=in_specs, out_specs=out_specs, check_vma=False
    )
```

```python
import math

import jax
import jax.numpy as jnp
from jax import lax
from jax.experimental import pallas as pl
from jax.experimental.pallas import tpu as pltpu
from jax.sharding import PartitionSpec as P

NEGATIVE = -1e30
EPSILON = 1e-06


def on_device(
    queries, stretch_cache, prefix_pool, page_table, prefix_len, prompt_cache, prompt_len,
    group_ids, absorb_weight, value_weight, out_weight, residual, norm_gain, routes,
    route_weight, gate_weight, up_weight, down_weight,
):
    tokens = queries.shape[0]
    prompts = lax.all_gather(prompt_cache, "req", axis=1, tiled=True)
    projected = attend(
        queries, stretch_cache, prefix_pool, page_table, prefix_len, prompts, prompt_len,
        group_ids, absorb_weight, value_weight, out_weight,
    )
    attention_part = lax.psum_scatter(
        projected.astype(jnp.bfloat16), "tp", scatter_dimension=1, tiled=True
    ).astype(jnp.float32)
    attended = (residual.astype(jnp.float32) + attention_part).astype(jnp.bfloat16)
    stream = attended.astype(jnp.float32)
    squares = lax.psum(jnp.sum(stream * stream, axis=1), "tp")
    model_width = out_weight.shape[1]
    normed = (
        stream * lax.rsqrt(squares / model_width + EPSILON)[:, None] * norm_gain.astype(jnp.float32)
    ).astype(jnp.bfloat16)
    experts = lax.axis_size("req")
    top = routes.shape[1]
    capacity = max(2, tokens * top * 4 // (3 * experts))
    choice = routes[:, :, None] == jnp.arange(experts, dtype=jnp.int32)[None, None, :]
    share = jnp.sum(jnp.where(choice, route_weight[:, :, None], 0.0), axis=1).T
    named = share > 0.0
    before = jnp.arange(tokens)[:, None] <= jnp.arange(tokens)[None, :]
    slot = jnp.dot(
        named.astype(jnp.bfloat16), before.astype(jnp.bfloat16), preferred_element_type=jnp.float32
    ).astype(jnp.int32) - 1
    picks = (
        slot[:, None, :] == jnp.arange(capacity, dtype=jnp.int32)[None, :, None]
    ) & named[:, None, :]
    chooser = picks.astype(jnp.bfloat16).reshape(experts * capacity, tokens)
    level = jnp.sum(jnp.where(picks, share[:, None, :], 0.0), axis=2)
    whole = lax.all_gather(normed, "tp", axis=1, tiled=True)
    buffer = (
        jnp.dot(chooser, whole, preferred_element_type=jnp.float32)
        .astype(jnp.bfloat16)
        .reshape(experts, capacity, -1)
    )
    received = lax.all_to_all(buffer, "req", split_axis=0, concat_axis=0, tiled=True)
    gate = jnp.einsum("snd,df->snf", received, gate_weight[0], preferred_element_type=jnp.float32)
    up = jnp.einsum("snd,df->snf", received, up_weight[0], preferred_element_type=jnp.float32)
    hidden = (jax.nn.silu(gate) * up).astype(jnp.bfloat16)
    part_out = jnp.einsum(
        "snf,fd->snd", hidden, down_weight[0], preferred_element_type=jnp.float32
    ).astype(jnp.bfloat16)
    returned = lax.all_to_all(part_out, "req", split_axis=0, concat_axis=0, tiled=True)
    weighted = (returned.astype(jnp.float32) * level[:, :, None]).astype(jnp.bfloat16)
    combined = lax.dot_general(
        chooser, weighted.reshape(experts * capacity, -1), (((0,), (0,)), ((), ())),
        preferred_element_type=jnp.float32,
    )
    expert_part = lax.psum_scatter(
        combined.astype(jnp.bfloat16), "tp", scatter_dimension=1, tiled=True
    ).astype(jnp.float32)
    mixed = (stream + expert_part).astype(jnp.bfloat16)
    return (attended, mixed)


def attend(
    queries, stretch_cache, prefix_pool, page_table, prefix_len, prompts, prompt_len,
    group_ids, absorb_weight, value_weight, out_weight,
):
    tokens, heads, width = queries.shape
    nope, rank = absorb_weight.shape[1], value_weight.shape[1]
    me = lax.axis_index("req")
    requests = jnp.arange(group_ids.shape[0], dtype=jnp.int32) == me
    group = jnp.sum(jnp.where(requests, group_ids, 0))
    own_length = jnp.sum(jnp.where(requests, prefix_len, 0))
    prompt_length = jnp.where(group == 0, prompt_len[0], prompt_len[1])
    pages, page = prefix_pool.shape[:2]
    order = jnp.arange(pages, dtype=jnp.int32)
    logical = jnp.sum(
        jnp.where(page_table[0][None, :] == order[:, None], order[None, :], 0), axis=1
    )
    prefix_at = (logical[:, None] * page + jnp.arange(page, dtype=jnp.int32)[None, :]).reshape(-1)
    prompt = jnp.where(group == 0, prompts[0], prompts[1])
    keys = jnp.concatenate(
        [stretch_cache, prompt, prefix_pool.reshape(pages * page, -1)], axis=0
    )
    seen = jnp.concatenate(
        [jnp.arange(prompt.shape[0]) < prompt_length, prefix_at < own_length]
    )
    token = jnp.arange(tokens)
    visible = jnp.concatenate(
        [
            token[None, :] <= token[:, None],
            jnp.broadcast_to(seen[None, :], (tokens, seen.shape[0])),
        ],
        axis=1,
    )
    turned = jnp.transpose(queries, (1, 0, 2))
    absorbed = jnp.concatenate(
        [
            jnp.einsum(
                "htn,hnr->htr", turned[:, :, :nope], absorb_weight,
                preferred_element_type=jnp.float32,
            ).astype(jnp.bfloat16),
            turned[:, :, nope:],
        ],
        axis=2,
    )
    scores = jnp.einsum("htc,kc->htk", absorbed, keys, preferred_element_type=jnp.float32)
    scores = jnp.where(visible[None], scores * width ** (-0.5), NEGATIVE)
    weights = jnp.exp(scores - jnp.max(scores, axis=2, keepdims=True))
    weights = jnp.where(visible[None], weights, 0.0)
    totals = jnp.sum(weights, axis=2, keepdims=True)
    latent = jnp.einsum(
        "htk,kr->htr", weights.astype(jnp.bfloat16), keys[:, :rank],
        preferred_element_type=jnp.float32,
    )
    latent = (latent / totals).astype(jnp.bfloat16)
    heads_out = jnp.einsum(
        "htr,hrv->thv", latent, value_weight, preferred_element_type=jnp.float32
    ).astype(jnp.bfloat16)
    return jnp.dot(
        heads_out.reshape(tokens, -1), out_weight, preferred_element_type=jnp.float32
    )


MESH = pl.DeviceIdType.MESH


def coordinates():
    me = lax.axis_index("req")
    return me // 4, (me // 2) % 2, me % 2, lax.axis_index("tp")


def place(z, x, core, y):
    return {"req": (z * 2 + x) * 2 + core, "tp": y}


def greet():
    z, x, core, y = coordinates()
    me = lax.axis_index("req")
    barrier = pltpu.get_barrier_semaphore()
    for step in range(1, 16):
        pl.semaphore_signal(
            barrier, inc=1, device_id={"req": (me + step) % 16, "tp": y}, device_id_type=MESH
        )
    pl.semaphore_signal(barrier, inc=1, device_id=place(z, x, core, 1 - y), device_id_type=MESH)
    pl.semaphore_wait(barrier, 16)


def plane_at(place_in_turn):
    z = coordinates()[0]
    high = z // 2
    near = z + high * (3 - 2 * z)
    late = place_in_turn // 2
    odd = place_in_turn % 2
    first = (1 - odd) * (1 - late) * near + odd * (1 - late) * (1 - near) + late * place_in_turn
    return first + high * (3 - 2 * first)


def spread_tokens(whole, send, recv):
    z, x, core, y = coordinates()
    half_rows, half_cols = whole.shape[1] // 2, whole.shape[2] // 2

    def piece(zp, xp, yp, half, cp):
        return whole.at[
            (zp * 2 + xp) * 2 + cp,
            pl.ds(half * half_rows, half_rows),
            pl.ds(pl.multiple_of(yp * half_cols, half_cols), half_cols),
        ]

    def hop(zp, xp, yp, half, cp, kind, peer):
        slot = zp * 8 + xp * 4 + yp * 2 + half
        part = piece(zp, xp, yp, half, cp)
        return pltpu.make_async_remote_copy(
            part, part, send.at[kind, slot], recv.at[cp, slot], device_id=peer, device_id_type=MESH
        )

    up, down = place(z + 1, x, core, y), place(z - 1, x, core, y)
    over_x, over_y, other = place(z, 1 - x, core, y), place(z, x, core, 1 - y), place(z, x, 1 - core, y)

    def column(zp, finish, halves=(0, 1)):
        for half in halves:
            for go, kind, peer in (
                ((zp <= z) & (z < 3), 0, up), ((zp >= z) & (z > 0), 1, down)
            ):
                @pl.when(go)
                def _(kind=kind, peer=peer, half=half):
                    copy = hop(zp, x, y, half, core, kind, peer)
                    copy.wait_send() if finish else copy.start()
        for kind, peer, half in ((2, over_x, 0), (3, over_y, 1), (2, over_x, 1), (3, over_y, 0)):
            if half in halves:
                copy = hop(zp, x, y, half, core, kind, peer)
                copy.wait_send() if finish else copy.start()
        for half in halves:
            copy = hop(zp, x, y, half, core, 4, other)
            copy.wait_send() if finish else copy.start()

    def arrive(zp):
        for half in range(2):
            hop(zp, x, y, half, core, 0, over_x).wait_recv()
        column(zp, False)

    def beside(zp, finish):
        if not finish:
            for half in range(2):
                hop(zp, 1 - x, y, half, core, 2, over_x).wait_recv()
                hop(zp, x, 1 - y, half, core, 3, over_y).wait_recv()
        copies = [hop(zp, 1 - x, y, 0, core, 3, over_y), hop(zp, x, 1 - y, 1, core, 2, over_x)]
        for half in range(2):
            copies.append(hop(zp, 1 - x, y, half, core, 4, other))
            copies.append(hop(zp, x, 1 - y, half, core, 4, other))
        for copy in copies:
            copy.wait_send() if finish else copy.start()

    def diagonal(zp, finish):
        for half in range(2):
            copy = hop(zp, 1 - x, 1 - y, half, core, 4, other)
            if finish:
                copy.wait_send()
            else:
                hop(zp, 1 - x, 1 - y, half, core, 2, over_x).wait_recv()
                copy.start()

    def complete(zp):
        for xp in range(2):
            for yp in range(2):
                for half in range(2):
                    hop(zp, xp, yp, half, 1 - core, 4, other).wait_recv()

    def close(zp):
        column(zp, True)
        beside(zp, True)
        diagonal(zp, True)

    return column, arrive, beside, diagonal, complete, close


def return_sums(parts, part_in, chooser, acc, x_diag, y_diag, x_in, y_in, z_in, sems):
    z, x, core, y = coordinates()
    rows, half_cols = acc.shape[2], acc.shape[3] // 2
    half_rows = rows // 2
    over_x, over_y, other = place(z, 1 - x, core, y), place(z, x, core, 1 - y), place(z, x, 1 - core, y)
    mine = pl.ds(pl.multiple_of(y * half_cols, half_cols), half_cols)
    theirs = pl.ds(pl.multiple_of((1 - y) * half_cols, half_cols), half_cols)
    top, low = pl.ds(0, half_rows), pl.ds(half_rows, half_rows)

    def copy(source, target, kind, zp, peer):
        return pltpu.make_async_remote_copy(
            source, target, sems.at[0, kind, zp], sems.at[1, kind, zp],
            device_id=peer, device_id_type=MESH,
        )

    def core_copy(zp, xp):
        return copy(parts.at[zp, xp * 2 + 1 - core], part_in.at[zp, xp], xp, zp, other)

    def diag_copies(zp):
        far = acc.at[zp, 1 - x]
        return (
            copy(far.at[top, theirs], y_diag.at[zp], 2, zp, over_y),
            copy(far.at[low, theirs], x_diag.at[zp], 3, zp, over_x),
        )

    def free_copies(zp):
        return (
            copy(acc.at[zp, 1 - x].at[low, mine], x_in.at[zp, low], 4, zp, over_x),
            copy(acc.at[zp, x].at[top, theirs], y_in.at[zp, top], 5, zp, over_y),
        )

    def last_copies(zp):
        return (
            copy(acc.at[zp, 1 - x].at[top, mine], x_in.at[zp, top], 6, zp, over_x),
            copy(acc.at[zp, x].at[low, theirs], y_in.at[zp, low], 7, zp, over_y),
        )

    def plane_copy(zp):
        return pltpu.make_async_remote_copy(
            acc.at[zp, x].at[:, mine], z_in.at[z], sems.at[0, 8, zp], sems.at[1, 8, z],
            device_id=place(zp, x, core, y), device_id_type=MESH,
        )

    def plane_arrival(zp):
        return pltpu.make_async_remote_copy(
            acc.at[zp, x].at[:, mine], z_in.at[zp], sems.at[0, 8, zp], sems.at[1, 8, zp],
            device_id=place(zp, x, core, y), device_id_type=MESH,
        )

    def add(target, *terms):
        total = target[...].astype(jnp.float32)
        for term in terms:
            total = total + term[...].astype(jnp.float32)
        target[...] = total.astype(target.dtype)

    def cores(zp):
        down = (((0,), (0,)), ((), ()))
        for xp in range(2):
            core_copy(zp, xp).wait_recv()
            request = (zp * 2 + xp) * 2 + core
            total = lax.dot_general(
                chooser[0, request], parts[zp, xp * 2 + core], down,
                preferred_element_type=jnp.float32,
            ) + lax.dot_general(
                chooser[1, request], part_in[zp, xp], down, preferred_element_type=jnp.float32
            )
            acc[zp, xp] = total.astype(jnp.bfloat16)
        for item in diag_copies(zp) + free_copies(zp):
            item.start()

    def corners(zp):
        from_y, from_x = diag_copies(zp)
        over_x_copy, over_y_copy = last_copies(zp)
        from_y.wait_recv()
        add(acc.at[zp, 1 - x].at[top, mine], y_diag.at[zp])
        over_x_copy.start()
        from_x.wait_recv()
        add(acc.at[zp, x].at[low, theirs], x_diag.at[zp])
        over_y_copy.start()

    def arrivals(zp):
        for item in free_copies(zp) + last_copies(zp):
            item.wait_recv()

    def columns(zp):
        arrivals(zp)
        add(acc.at[zp, x].at[:, mine], x_in.at[zp], y_in.at[zp])
        plane_copy(zp).start()

    def final(attended, mixed):
        arrivals(z)
        total = attended[...].astype(jnp.float32) + acc[z, x, :, mine].astype(jnp.float32)
        total = total + x_in[z].astype(jnp.float32) + y_in[z].astype(jnp.float32)
        for turn in range(1, 4):
            zp = plane_at(turn)
            plane_arrival(zp).wait_recv()
            total = total + z_in[zp].astype(jnp.float32)
        mixed[...] = total.astype(jnp.bfloat16)

    def close(zp):
        for xp in range(2):
            core_copy(zp, xp).wait_send()
        for item in diag_copies(zp) + free_copies(zp) + last_copies(zp):
            item.wait_send()

        @pl.when(zp != z)
        def _():
            plane_copy(zp).wait_send()

    return core_copy, cores, corners, columns, final, close


def choose(mine, chooser, which):
    requests, tokens = mine.shape
    capacity = chooser.shape[2]
    named = jnp.where(mine[...] > 0.0, 1.0, 0.0)
    rows = lax.broadcasted_iota(jnp.int32, (tokens, tokens), 0)
    columns = lax.broadcasted_iota(jnp.int32, (tokens, tokens), 1)
    before = jnp.where(rows <= columns, 1.0, 0.0).astype(jnp.bfloat16)
    slot = jnp.dot(named.astype(jnp.bfloat16), before, preferred_element_type=jnp.float32)
    wanted = jnp.where(named > 0.0, slot - 1.0, -1.0).astype(jnp.int32)
    places = lax.broadcasted_iota(jnp.int32, (capacity, tokens), 0)
    for request in range(requests):
        picks = jnp.where(wanted[request : request + 1, :] == places, 1.0, 0.0)
        chooser[which, request] = picks.astype(jnp.bfloat16)


def share_prompts(block_ref, share_ref, keys_ref, mine_ref, send, recv, send_w, recv_w, local):
    me = lax.axis_index("req")
    y = lax.axis_index("tp")
    depth = block_ref.shape[1]
    rows = pl.ds(pl.multiple_of(me * depth, depth), depth)
    core, other = me % 2, me + 1 - 2 * (me % 2)

    def block(source):
        return keys_ref.at[:, pl.ds(pl.multiple_of(source * depth, depth), depth), :]

    def shares(step):
        peer = (me + step) % 16
        return pltpu.make_async_remote_copy(
            share_ref.at[peer], mine_ref.at[me], send_w.at[step], recv_w.at[step],
            device_id={"req": peer, "tp": y}, device_id_type=MESH,
        )

    def direct(step):
        return pltpu.make_async_remote_copy(
            block_ref, keys_ref.at[:, rows, :], send.at[step], recv.at[step],
            device_id={"req": (me + 2 * step) % 16, "tp": y}, device_id_type=MESH,
        )

    def across(source, index):
        return pltpu.make_async_remote_copy(
            block(source), block(source), send.at[index], recv.at[index],
            device_id={"req": other, "tp": y}, device_id_type=MESH,
        )

    home = pltpu.make_async_remote_copy(
        block_ref, keys_ref.at[:, rows, :], send.at[8 + me // 2], recv.at[8 + me // 2],
        device_id={"req": other, "tp": y}, device_id_type=MESH,
    )
    own = pltpu.make_async_copy(block_ref, keys_ref.at[:, rows, :], local.at[0])
    own_share = pltpu.make_async_copy(share_ref.at[me], mine_ref.at[me], local.at[1])

    def start():
        for step in range(1, 8):
            direct(step).start()
        home.start()
        own.start()
        own_share.start()

        def send_share(step, carry):
            shares(step).start()
            return carry

        lax.fori_loop(1, 16, send_share, 0)

    def relay(step):
        source = (me + 2 * step) % 16
        across(source, 8 - step).wait_recv()
        across(source, 8 + source // 2).start()

    def finish():
        own.wait()
        for step in range(8):
            source = (me + 2 * step) % 16 + 1 - 2 * core
            across(source, 8 + source // 2).wait_recv()

    def finish_shares():
        own_share.wait()

        def wait_share(step, carry):
            shares(step).wait_recv()
            return carry

        lax.fori_loop(1, 16, wait_share, 0)

    def close():
        home.wait_send()
        for step in range(1, 8):
            direct(step).wait_send()
            source = (me + 2 * step) % 16
            across(source, 8 + source // 2).wait_send()

        def close_share(step, carry):
            shares(step).wait_send()
            return carry

        lax.fori_loop(1, 16, close_share, 0)

    return start, relay, finish, finish_shares, close


def layer_kernel(
    page_table, prefix_len, prompt_len, group_ids,
    routes, route_weight, gain, residual, prompt_block,
    query_hbm, stretch_hbm, pool_hbm, absorb_hbm, value_hbm, out_hbm, gate_hbm, up_hbm, down_hbm,
    attended, mixed,
    query, stretch, keys, absorb, value, out_w, prompts, absorbed, scores, bias, heads,
    share, share_in, projected,
    whole, outgoing, incoming, squares_out, squares_in, gains, mine_share, other_share, roots,
    chooser, level,
    gate_w, up_w, down_w, rows, hidden, parts, part_in, acc, x_diag, y_diag, x_in, y_in, z_in,
    prompt_send, prompt_recv, share_send, share_recv, local_sems,
    pair_sems, load_sems, root_sems, send, recv, sems,
):
    z, x, core, y = coordinates()
    me = lax.axis_index("req")
    tokens, half_cols = residual.shape
    half_rows = tokens // 2
    count, nope, rank = absorb.shape
    width = query.shape[1]
    pool_rows = pool_hbm.shape[0]
    own_rows = pool_rows + tokens
    loads = [
        pltpu.make_async_copy(source, target, load_sems.at[index])
        for index, (source, target) in enumerate(
            (
                (query_hbm, query), (absorb_hbm, absorb), (stretch_hbm, stretch),
                (pool_hbm, keys.at[pl.ds(0, pool_rows)]), (value_hbm, value), (out_hbm, out_w),
                (gate_hbm, gate_w), (up_hbm, up_w), (down_hbm, down_w),
            )
        )
    ]
    for load in loads:
        load.start()
    mine = pl.ds(pl.multiple_of(y * half_cols, half_cols), half_cols)
    theirs = pl.ds(pl.multiple_of((1 - y) * half_cols, half_cols), half_cols)
    over_y, other = place(z, x, core, 1 - y), place(z, x, 1 - core, y)

    def pair(source, target, index, peer=over_y):
        return pltpu.make_async_remote_copy(
            source, target, pair_sems.at[0, index], pair_sems.at[1, index],
            device_id=peer, device_id_type=MESH,
        )

    def swap(half):
        lines = pl.ds(half * half_rows, half_rows)
        return pair(outgoing.at[lines], incoming.at[lines], half)

    squares = pair(squares_out, squares_in, 2)
    gain_copy = pair(gains.at[y], gains.at[y], 3)
    share_copy = pair(mine_share, other_share, 4, other)
    start_prompts, relay, finish_prompts, finish_shares, close_prompts = share_prompts(
        prompt_block, share, prompts, share_in, prompt_send, prompt_recv, share_send, share_recv,
        local_sems,
    )
    expert_of = lax.broadcasted_iota(jnp.int32, (16, tokens), 0)
    given = jnp.zeros((16, tokens), jnp.float32)
    for choice in range(routes.shape[0]):
        hit = routes[choice : choice + 1, :] == expert_of
        given = given + jnp.where(hit, route_weight[choice : choice + 1, :], 0.0)
    for expert in range(16):
        share[expert] = given[expert : expert + 1, :]
    gains[y] = gain[...].astype(jnp.float32)
    greet()
    start_prompts()
    gain_copy.start()
    group = group_ids[me]
    page = pool_rows // page_table.shape[1]
    lane = lax.broadcasted_iota(jnp.int32, (1, pool_rows), 1)
    logical = jnp.zeros((1, pool_rows), jnp.int32)
    for index in range(page_table.shape[1]):
        logical = jnp.where(lane // page == page_table[0, index], index, logical)
    prefix_at = logical * page + lane % page
    bias[:, pl.ds(0, pool_rows)] = jnp.where(prefix_at < prefix_len[me], 0.0, NEGATIVE)
    prompt_rows = prompts.shape[1]
    prompt_lane = lax.broadcasted_iota(jnp.int32, (1, prompt_rows), 1)
    bias[:, pl.ds(pool_rows, prompt_rows)] = jnp.where(prompt_lane < prompt_len[group], 0.0, NEGATIVE)
    loads[2].wait()
    keys[pl.ds(pool_rows, tokens), :] = stretch[...].T
    for index in (0, 1, 3):
        loads[index].wait()
    first = (((0,), (0,)), ((), ()))
    across = (((1,), (1,)), ((), ()))

    def score(head, carry):
        wide = lax.dot_general(
            query[head, pl.ds(0, nope), :], absorb[head], first, preferred_element_type=jnp.float32
        )
        absorbed[head, :, pl.ds(0, rank)] = wide.astype(jnp.bfloat16)
        absorbed[head, :, pl.ds(rank, width - nope)] = query[head, pl.ds(nope, width - nope), :].T
        found = lax.dot_general(
            absorbed[head], keys[pl.ds(0, own_rows), :], across, preferred_element_type=jnp.float32
        )
        scores[head, :, pl.ds(0, pool_rows)] = found[:, :pool_rows] + bias[:, pl.ds(0, pool_rows)]
        later = lax.broadcasted_iota(jnp.int32, (tokens, tokens), 1) > lax.broadcasted_iota(
            jnp.int32, (tokens, tokens), 0
        )
        scores[head, :, pl.ds(pool_rows, tokens)] = jnp.where(later, NEGATIVE, found[:, pool_rows:])

        @pl.when(head > 0)
        def _():
            relay(head)

        return carry

    lax.fori_loop(0, count, score, 0)
    finish_prompts()
    keys[pl.ds(own_rows, prompt_rows), :] = prompts[group]
    loads[4].wait()
    factor = width ** (-0.5) * math.log2(math.e)

    def attend_head(head, carry):
        found = lax.dot_general(
            absorbed[head], keys[pl.ds(own_rows, prompt_rows), :], across,
            preferred_element_type=jnp.float32,
        ) + bias[:, pl.ds(pool_rows, prompt_rows)]
        held = scores[head]
        best = jnp.maximum(
            jnp.max(found, axis=1, keepdims=True), jnp.max(held, axis=1, keepdims=True)
        )
        held = jnp.exp2((held - best) * factor)
        found = jnp.exp2((found - best) * factor)
        total = jnp.sum(held, axis=1, keepdims=True) + jnp.sum(found, axis=1, keepdims=True)
        latent = jnp.dot(
            held.astype(jnp.bfloat16), keys[pl.ds(0, own_rows), pl.ds(0, rank)],
            preferred_element_type=jnp.float32,
        ) + jnp.dot(
            found.astype(jnp.bfloat16), keys[pl.ds(own_rows, prompt_rows), pl.ds(0, rank)],
            preferred_element_type=jnp.float32,
        )
        latent = (latent / total).astype(jnp.bfloat16)
        size = value.shape[2]
        heads[:, pl.ds(pl.multiple_of(head * size, size), size)] = jnp.dot(
            latent, value[head], preferred_element_type=jnp.float32
        ).astype(jnp.bfloat16)
        return carry

    lax.fori_loop(0, count, attend_head, 0)
    loads[5].wait()
    outgoing[...] = jnp.dot(
        heads[...], out_w[:, theirs], preferred_element_type=jnp.float32
    ).astype(jnp.bfloat16)
    swap(0).start()
    swap(1).start()
    projected[...] = jnp.dot(heads[...], out_w[:, mine], preferred_element_type=jnp.float32)
    finish_shares()
    for request in range(16):
        mine_share[request : request + 1, :] = share_in[request]
    share_copy.start()
    choose(mine_share, chooser, 0)
    column, arrive, beside, diagonal, complete, close_spread = spread_tokens(whole, send, recv)
    diag = lax.broadcasted_iota(jnp.int32, (half_rows, tokens), 1) - lax.broadcasted_iota(
        jnp.int32, (half_rows, tokens), 0
    )
    sums = jnp.zeros((1, tokens), jnp.float32)
    for half in range(2):
        lines = pl.ds(half * half_rows, half_rows)
        swap(half).wait_recv()
        stream = (
            residual[lines, :].astype(jnp.float32)
            + projected[lines, :]
            + incoming[lines, :].astype(jnp.float32)
        )
        rounded = stream.astype(jnp.bfloat16)
        attended[lines, :] = rounded
        whole[me, lines, mine] = rounded
        stream = rounded.astype(jnp.float32)
        line_sums = jnp.sum(stream * stream, axis=1, keepdims=True)
        sums = sums + jnp.sum(
            jnp.where(diag == half * half_rows, line_sums, 0.0), axis=0, keepdims=True
        )
        if half == 1:
            squares_out[...] = sums
            squares.start()
        column(z, False, (half,))
    share_copy.wait_recv()
    choose(other_share, chooser, 1)

    def root_copy(step):
        peer = (me + step) % 16
        return pltpu.make_async_remote_copy(
            roots.at[me], roots.at[me], root_sems.at[0, peer], root_sems.at[1, me],
            device_id={"req": peer, "tp": y}, device_id_type=MESH,
        )

    def root_arrival(request):
        return pltpu.make_async_remote_copy(
            roots.at[request], roots.at[request], root_sems.at[0, request],
            root_sems.at[1, request], device_id=over_y, device_id_type=MESH,
        )

    arrive(plane_at(1))
    beside(z, False)
    squares.wait_recv()
    roots[me] = lax.rsqrt((squares_out[...] + squares_in[...]) / (2 * half_cols) + EPSILON)

    def send_root(step, carry):
        root_copy(step).start()
        return carry

    lax.fori_loop(1, 16, send_root, 0)
    gain_copy.wait_recv()
    for load in loads[6:]:
        load.wait()
    capacity = chooser.shape[2]
    core_copy, cores, corners, columns, final, close_return = return_sums(
        parts, part_in, chooser, acc, x_diag, y_diag, x_in, y_in, z_in, sems
    )

    def compute(zp):
        for index in range(4):
            request = zp * 4 + index

            @pl.when(request != me)
            def _(request=request):
                root_arrival(request).wait_recv()

        for index in range(4):
            request = zp * 4 + index
            lines = pl.ds(index * capacity, capacity)
            picks = chooser[0, request]
            picked = jnp.dot(picks, whole[request], preferred_element_type=jnp.float32)
            wide = picks.astype(jnp.float32)
            picked = picked * jnp.sum(wide * roots[request], axis=1, keepdims=True)
            shared = jnp.sum(wide * share_in[request], axis=1, keepdims=True)
            level[lines, :] = jnp.broadcast_to(shared, (capacity, level.shape[1]))
            for side in range(2):
                span = pl.ds(side * half_cols, half_cols)
                scaled = picked[:, side * half_cols : (side + 1) * half_cols] * gains[side]
                rows[lines, span] = scaled.astype(jnp.bfloat16)
        gate = lax.dot_general(rows[...], gate_w[...], across, preferred_element_type=jnp.float32)
        up = lax.dot_general(rows[...], up_w[...], across, preferred_element_type=jnp.float32)
        hidden[...] = (gate / (1.0 + jnp.exp(-gate)) * up * level[:, :1]).astype(jnp.bfloat16)
        part = jnp.dot(hidden[...], down_w[...], preferred_element_type=jnp.float32)
        for index in range(4):
            parts[zp, index] = part[index * capacity : (index + 1) * capacity].astype(jnp.bfloat16)
        for xp in range(2):
            core_copy(zp, xp).start()

    def step(turn, carry):
        @pl.when(turn < 3)
        def _():
            arrive(plane_at(turn + 1))

        @pl.when(turn < 4)
        def _():
            beside(plane_at(turn), False)

        @pl.when((turn >= 4) & (turn < 8))
        def _():
            cores(plane_at((turn - 3) % 4))

        @pl.when(turn < 5)
        def _():
            zp = plane_at(turn - 1)
            diagonal(zp, False)
            complete(zp)
            compute(zp)

        @pl.when((turn >= 5) & (turn < 9))
        def _():
            corners(plane_at((turn - 4) % 4))

        @pl.when((turn >= 6) & (turn < 9))
        def _():
            columns(plane_at(turn - 5))

        return carry

    lax.fori_loop(1, 9, step, 0)
    final(attended, mixed)

    def close(zp, carry):
        close_spread(zp)
        close_return(zp)
        return carry

    lax.fori_loop(0, 4, close, 0)

    def close_root(step, carry):
        root_copy(step).wait_send()
        return carry

    lax.fori_loop(1, 16, close_root, 0)
    for item in (swap(0), swap(1), squares, gain_copy, share_copy):
        item.wait_send()
    close_prompts()


def on_block(
    queries, stretch_cache, prefix_pool, page_table, prefix_len, prompt_cache, prompt_len,
    group_ids, absorb_weight, value_weight, out_weight, residual, norm_gain, routes,
    route_weight, gate_weight, up_weight, down_weight,
):
    tokens, count, width = queries.shape
    nope, rank = absorb_weight.shape[1:]
    size = value_weight.shape[2]
    top = routes.shape[1]
    experts = 16
    capacity = max(2, tokens * top * 4 // (3 * experts))
    pages, page, entry = prefix_pool.shape
    groups, depth = prompt_cache.shape[:2]
    half = residual.shape[1]
    model = out_weight.shape[1]
    units = down_weight.shape[1]
    own_rows = pages * page + tokens
    bf16, f32 = jnp.bfloat16, jnp.float32
    dma = pltpu.SemaphoreType.DMA
    vmem = pl.BlockSpec(memory_space=pltpu.VMEM)
    smem = pl.BlockSpec(memory_space=pltpu.SMEM)
    anywhere = pl.BlockSpec(memory_space=pl.ANY)
    return pl.pallas_call(
        layer_kernel,
        out_shape=(jax.ShapeDtypeStruct((tokens, half), bf16),) * 2,
        in_specs=[smem] * 4 + [vmem] * 5 + [anywhere] * 9,
        out_specs=(vmem, vmem),
        scratch_shapes=[
            pltpu.VMEM((count, width, tokens), bf16),
            pltpu.VMEM((entry, tokens), bf16),
            pltpu.VMEM((own_rows + depth * 16, entry), bf16),
            pltpu.VMEM((count, nope, rank), bf16),
            pltpu.VMEM((count, rank, size), bf16),
            pltpu.VMEM((count * size, model), bf16),
            pltpu.VMEM((groups, depth * 16, entry), bf16),
            pltpu.VMEM((count, tokens, entry), bf16),
            pltpu.VMEM((count, tokens, own_rows), f32),
            pltpu.VMEM((1, pages * page + depth * 16), f32),
            pltpu.VMEM((tokens, count * size), bf16),
            pltpu.VMEM((16, 1, tokens), f32),
            pltpu.VMEM((16, 1, tokens), f32),
            pltpu.VMEM((tokens, half), f32),
            pltpu.VMEM((16, tokens, model), bf16),
            pltpu.VMEM((tokens, half), bf16),
            pltpu.VMEM((tokens, half), bf16),
            pltpu.VMEM((1, tokens), f32),
            pltpu.VMEM((1, tokens), f32),
            pltpu.VMEM((2, 1, half), f32),
            pltpu.VMEM((16, tokens), f32),
            pltpu.VMEM((16, tokens), f32),
            pltpu.VMEM((16, 1, tokens), f32),
            pltpu.VMEM((2, 16, capacity, tokens), bf16),
            pltpu.VMEM((4 * capacity, 128), f32),
            pltpu.VMEM((units, model), bf16),
            pltpu.VMEM((units, model), bf16),
            pltpu.VMEM((units, model), bf16),
            pltpu.VMEM((4 * capacity, model), bf16),
            pltpu.VMEM((4 * capacity, units), bf16),
            pltpu.VMEM((4, 4, capacity, model), bf16),
            pltpu.VMEM((4, 2, capacity, model), bf16),
            pltpu.VMEM((4, 2, tokens, model), bf16),
            pltpu.VMEM((4, tokens // 2, half), bf16),
            pltpu.VMEM((4, tokens // 2, half), bf16),
            pltpu.VMEM((4, tokens, half), bf16),
            pltpu.VMEM((4, tokens, half), bf16),
            pltpu.VMEM((4, tokens, half), bf16),
            dma((16,)),
            dma((16,)),
            dma((16,)),
            dma((16,)),
            dma((2,)),
            dma((2, 5)),
            dma((9,)),
            dma((2, 16)),
            dma((5, 32)),
            dma((2, 32)),
            dma((2, 9, 4)),
        ],
        compiler_params=pltpu.CompilerParams(
            collective_id=0, has_side_effects=True, vmem_limit_bytes=60 << 20
        ),
    )(
        page_table, prefix_len, prompt_len, group_ids,
        routes.T, route_weight.T, norm_gain[None, :], residual, prompt_cache,
        jnp.transpose(queries, (1, 2, 0)), stretch_cache.T, prefix_pool.reshape(pages * page, entry),
        absorb_weight, value_weight, out_weight,
        jnp.swapaxes(gate_weight[0], 0, 1), jnp.swapaxes(up_weight[0], 0, 1), down_weight[0],
    )


def solution(mesh):
    in_specs = (
        P("req", "tp", None),
        P("req", None),
        P("req", None, None),
        P("req", None),
        P(),
        P(None, "req", None),
        P(),
        P(),
        P("tp", None, None),
        P("tp", None, None),
        P("tp", None),
        P("req", "tp"),
        P("tp"),
        P("req", None),
        P("req", None),
        P("req", None, "tp"),
        P("req", None, "tp"),
        P("req", "tp", None),
    )
    out_specs = (P("req", "tp"), P("req", "tp"))
    body = on_block if mesh.shape["req"] == 16 and mesh.shape["tp"] == 2 else on_device
    return jax.shard_map(
        body, mesh=mesh, in_specs=in_specs, out_specs=out_specs, check_vma=False
    )
```

```python
import math

import jax
import jax.numpy as jnp
from jax import lax
from jax.experimental import pallas as pl
from jax.experimental.pallas import tpu as pltpu
from jax.sharding import PartitionSpec as P

NEGATIVE = -1e30
EPSILON = 1e-06


def on_device(
    queries, stretch_cache, prefix_pool, page_table, prefix_len, prompt_cache, prompt_len,
    group_ids, absorb_weight, value_weight, out_weight, residual, norm_gain, routes,
    route_weight, gate_weight, up_weight, down_weight,
):
    tokens = queries.shape[0]
    prompts = lax.all_gather(prompt_cache, "req", axis=1, tiled=True)
    projected = attend(
        queries, stretch_cache, prefix_pool, page_table, prefix_len, prompts, prompt_len,
        group_ids, absorb_weight, value_weight, out_weight,
    )
    attention_part = lax.psum_scatter(
        projected.astype(jnp.bfloat16), "tp", scatter_dimension=1, tiled=True
    ).astype(jnp.float32)
    attended = (residual.astype(jnp.float32) + attention_part).astype(jnp.bfloat16)
    stream = attended.astype(jnp.float32)
    squares = lax.psum(jnp.sum(stream * stream, axis=1), "tp")
    model_width = out_weight.shape[1]
    normed = (
        stream * lax.rsqrt(squares / model_width + EPSILON)[:, None] * norm_gain.astype(jnp.float32)
    ).astype(jnp.bfloat16)
    experts = lax.axis_size("req")
    top = routes.shape[1]
    capacity = max(2, tokens * top * 4 // (3 * experts))
    choice = routes[:, :, None] == jnp.arange(experts, dtype=jnp.int32)[None, None, :]
    share = jnp.sum(jnp.where(choice, route_weight[:, :, None], 0.0), axis=1).T
    named = share > 0.0
    before = jnp.arange(tokens)[:, None] <= jnp.arange(tokens)[None, :]
    slot = jnp.dot(
        named.astype(jnp.bfloat16), before.astype(jnp.bfloat16), preferred_element_type=jnp.float32
    ).astype(jnp.int32) - 1
    picks = (
        slot[:, None, :] == jnp.arange(capacity, dtype=jnp.int32)[None, :, None]
    ) & named[:, None, :]
    chooser = picks.astype(jnp.bfloat16).reshape(experts * capacity, tokens)
    level = jnp.sum(jnp.where(picks, share[:, None, :], 0.0), axis=2)
    whole = lax.all_gather(normed, "tp", axis=1, tiled=True)
    buffer = (
        jnp.dot(chooser, whole, preferred_element_type=jnp.float32)
        .astype(jnp.bfloat16)
        .reshape(experts, capacity, -1)
    )
    received = lax.all_to_all(buffer, "req", split_axis=0, concat_axis=0, tiled=True)
    gate = jnp.einsum("snd,df->snf", received, gate_weight[0], preferred_element_type=jnp.float32)
    up = jnp.einsum("snd,df->snf", received, up_weight[0], preferred_element_type=jnp.float32)
    hidden = (jax.nn.silu(gate) * up).astype(jnp.bfloat16)
    part_out = jnp.einsum(
        "snf,fd->snd", hidden, down_weight[0], preferred_element_type=jnp.float32
    ).astype(jnp.bfloat16)
    returned = lax.all_to_all(part_out, "req", split_axis=0, concat_axis=0, tiled=True)
    weighted = (returned.astype(jnp.float32) * level[:, :, None]).astype(jnp.bfloat16)
    combined = lax.dot_general(
        chooser, weighted.reshape(experts * capacity, -1), (((0,), (0,)), ((), ())),
        preferred_element_type=jnp.float32,
    )
    expert_part = lax.psum_scatter(
        combined.astype(jnp.bfloat16), "tp", scatter_dimension=1, tiled=True
    ).astype(jnp.float32)
    mixed = (stream + expert_part).astype(jnp.bfloat16)
    return (attended, mixed)


def attend(
    queries, stretch_cache, prefix_pool, page_table, prefix_len, prompts, prompt_len,
    group_ids, absorb_weight, value_weight, out_weight,
):
    tokens, heads, width = queries.shape
    nope, rank = absorb_weight.shape[1], value_weight.shape[1]
    me = lax.axis_index("req")
    requests = jnp.arange(group_ids.shape[0], dtype=jnp.int32) == me
    group = jnp.sum(jnp.where(requests, group_ids, 0))
    own_length = jnp.sum(jnp.where(requests, prefix_len, 0))
    prompt_length = jnp.where(group == 0, prompt_len[0], prompt_len[1])
    pages, page = prefix_pool.shape[:2]
    order = jnp.arange(pages, dtype=jnp.int32)
    logical = jnp.sum(
        jnp.where(page_table[0][None, :] == order[:, None], order[None, :], 0), axis=1
    )
    prefix_at = (logical[:, None] * page + jnp.arange(page, dtype=jnp.int32)[None, :]).reshape(-1)
    prompt = jnp.where(group == 0, prompts[0], prompts[1])
    keys = jnp.concatenate(
        [stretch_cache, prompt, prefix_pool.reshape(pages * page, -1)], axis=0
    )
    seen = jnp.concatenate(
        [jnp.arange(prompt.shape[0]) < prompt_length, prefix_at < own_length]
    )
    token = jnp.arange(tokens)
    visible = jnp.concatenate(
        [
            token[None, :] <= token[:, None],
            jnp.broadcast_to(seen[None, :], (tokens, seen.shape[0])),
        ],
        axis=1,
    )
    turned = jnp.transpose(queries, (1, 0, 2))
    absorbed = jnp.concatenate(
        [
            jnp.einsum(
                "htn,hnr->htr", turned[:, :, :nope], absorb_weight,
                preferred_element_type=jnp.float32,
            ).astype(jnp.bfloat16),
            turned[:, :, nope:],
        ],
        axis=2,
    )
    scores = jnp.einsum("htc,kc->htk", absorbed, keys, preferred_element_type=jnp.float32)
    scores = jnp.where(visible[None], scores * width ** (-0.5), NEGATIVE)
    weights = jnp.exp(scores - jnp.max(scores, axis=2, keepdims=True))
    weights = jnp.where(visible[None], weights, 0.0)
    totals = jnp.sum(weights, axis=2, keepdims=True)
    latent = jnp.einsum(
        "htk,kr->htr", weights.astype(jnp.bfloat16), keys[:, :rank],
        preferred_element_type=jnp.float32,
    )
    latent = (latent / totals).astype(jnp.bfloat16)
    heads_out = jnp.einsum(
        "htr,hrv->thv", latent, value_weight, preferred_element_type=jnp.float32
    ).astype(jnp.bfloat16)
    return jnp.dot(
        heads_out.reshape(tokens, -1), out_weight, preferred_element_type=jnp.float32
    )


MESH = pl.DeviceIdType.MESH


def coordinates():
    me = lax.axis_index("req")
    return me // 4, (me // 2) % 2, me % 2, lax.axis_index("tp")


def place(z, x, core, y):
    return {"req": (z * 2 + x) * 2 + core, "tp": y}


def greet():
    z, x, core, y = coordinates()
    me = lax.axis_index("req")
    barrier = pltpu.get_barrier_semaphore()
    for step in range(1, 16):
        pl.semaphore_signal(
            barrier, inc=1, device_id={"req": (me + step) % 16, "tp": y}, device_id_type=MESH
        )
    pl.semaphore_signal(barrier, inc=1, device_id=place(z, x, core, 1 - y), device_id_type=MESH)
    pl.semaphore_wait(barrier, 16)


def plane_at(place_in_turn):
    z = coordinates()[0]
    high = z // 2
    near = z + high * (3 - 2 * z)
    late = place_in_turn // 2
    odd = place_in_turn % 2
    first = (1 - odd) * (1 - late) * near + odd * (1 - late) * (1 - near) + late * place_in_turn
    return first + high * (3 - 2 * first)


def spread_tokens(whole, send, recv):
    z, x, core, y = coordinates()
    half_rows, half_cols = whole.shape[1] // 2, whole.shape[2] // 2

    def piece(zp, xp, yp, half, cp):
        return whole.at[
            (zp * 2 + xp) * 2 + cp,
            pl.ds(half * half_rows, half_rows),
            pl.ds(pl.multiple_of(yp * half_cols, half_cols), half_cols),
        ]

    def hop(zp, xp, yp, half, cp, kind, peer):
        slot = zp * 8 + xp * 4 + yp * 2 + half
        part = piece(zp, xp, yp, half, cp)
        return pltpu.make_async_remote_copy(
            part, part, send.at[kind, slot], recv.at[cp, slot], device_id=peer, device_id_type=MESH
        )

    up, down = place(z + 1, x, core, y), place(z - 1, x, core, y)
    over_x, over_y, other = place(z, 1 - x, core, y), place(z, x, core, 1 - y), place(z, x, 1 - core, y)

    def column(zp, finish, halves=(0, 1)):
        for half in halves:
            for go, kind, peer in (
                ((zp <= z) & (z < 3), 0, up), ((zp >= z) & (z > 0), 1, down)
            ):
                @pl.when(go)
                def _(kind=kind, peer=peer, half=half):
                    copy = hop(zp, x, y, half, core, kind, peer)
                    copy.wait_send() if finish else copy.start()
        for kind, peer, half in ((2, over_x, 0), (3, over_y, 1), (2, over_x, 1), (3, over_y, 0)):
            if half in halves:
                copy = hop(zp, x, y, half, core, kind, peer)
                copy.wait_send() if finish else copy.start()
        for half in halves:
            copy = hop(zp, x, y, half, core, 4, other)
            copy.wait_send() if finish else copy.start()

    def arrive(zp):
        for half in range(2):
            hop(zp, x, y, half, core, 0, over_x).wait_recv()
        column(zp, False)

    def beside(zp, finish):
        if not finish:
            for half in range(2):
                hop(zp, 1 - x, y, half, core, 2, over_x).wait_recv()
                hop(zp, x, 1 - y, half, core, 3, over_y).wait_recv()
        copies = [hop(zp, 1 - x, y, 0, core, 3, over_y), hop(zp, x, 1 - y, 1, core, 2, over_x)]
        for half in range(2):
            copies.append(hop(zp, 1 - x, y, half, core, 4, other))
            copies.append(hop(zp, x, 1 - y, half, core, 4, other))
        for copy in copies:
            copy.wait_send() if finish else copy.start()

    def diagonal(zp, finish):
        for half in range(2):
            copy = hop(zp, 1 - x, 1 - y, half, core, 4, other)
            if finish:
                copy.wait_send()
            else:
                hop(zp, 1 - x, 1 - y, half, core, 2, over_x).wait_recv()
                copy.start()

    def complete(zp):
        for xp in range(2):
            for yp in range(2):
                for half in range(2):
                    hop(zp, xp, yp, half, 1 - core, 4, other).wait_recv()

    def close(zp):
        column(zp, True)
        beside(zp, True)
        diagonal(zp, True)

    return column, arrive, beside, diagonal, complete, close


def return_sums(parts, part_in, chooser, acc, x_diag, y_diag, x_in, y_in, z_in, sems):
    z, x, core, y = coordinates()
    rows, half_cols = acc.shape[2], acc.shape[3] // 2
    half_rows = rows // 2
    over_x, over_y, other = place(z, 1 - x, core, y), place(z, x, core, 1 - y), place(z, x, 1 - core, y)
    mine = pl.ds(pl.multiple_of(y * half_cols, half_cols), half_cols)
    theirs = pl.ds(pl.multiple_of((1 - y) * half_cols, half_cols), half_cols)
    top, low = pl.ds(0, half_rows), pl.ds(half_rows, half_rows)

    def copy(source, target, kind, zp, peer):
        return pltpu.make_async_remote_copy(
            source, target, sems.at[0, kind, zp], sems.at[1, kind, zp],
            device_id=peer, device_id_type=MESH,
        )

    def core_copy(zp, xp):
        return copy(parts.at[zp, xp * 2 + 1 - core], part_in.at[zp, xp], xp, zp, other)

    def diag_copies(zp):
        far = acc.at[zp, 1 - x]
        return (
            copy(far.at[top, theirs], y_diag.at[zp], 2, zp, over_y),
            copy(far.at[low, theirs], x_diag.at[zp], 3, zp, over_x),
        )

    def free_copies(zp):
        return (
            copy(acc.at[zp, 1 - x].at[low, mine], x_in.at[zp, low], 4, zp, over_x),
            copy(acc.at[zp, x].at[top, theirs], y_in.at[zp, top], 5, zp, over_y),
        )

    def last_copies(zp):
        return (
            copy(acc.at[zp, 1 - x].at[top, mine], x_in.at[zp, top], 6, zp, over_x),
            copy(acc.at[zp, x].at[low, theirs], y_in.at[zp, low], 7, zp, over_y),
        )

    def plane_copy(zp):
        return pltpu.make_async_remote_copy(
            acc.at[zp, x].at[:, mine], z_in.at[z], sems.at[0, 8, zp], sems.at[1, 8, z],
            device_id=place(zp, x, core, y), device_id_type=MESH,
        )

    def plane_arrival(zp):
        return pltpu.make_async_remote_copy(
            acc.at[zp, x].at[:, mine], z_in.at[zp], sems.at[0, 8, zp], sems.at[1, 8, zp],
            device_id=place(zp, x, core, y), device_id_type=MESH,
        )

    def add(target, *terms):
        total = target[...].astype(jnp.float32)
        for term in terms:
            total = total + term[...].astype(jnp.float32)
        target[...] = total.astype(target.dtype)

    def cores(zp):
        down = (((0,), (0,)), ((), ()))
        for xp in range(2):
            core_copy(zp, xp).wait_recv()
            request = (zp * 2 + xp) * 2 + core
            total = lax.dot_general(
                chooser[0, request], parts[zp, xp * 2 + core], down,
                preferred_element_type=jnp.float32,
            ) + lax.dot_general(
                chooser[1, request], part_in[zp, xp], down, preferred_element_type=jnp.float32
            )
            acc[zp, xp] = total.astype(jnp.bfloat16)
        for item in diag_copies(zp) + free_copies(zp):
            item.start()

    def corners(zp):
        from_y, from_x = diag_copies(zp)
        over_x_copy, over_y_copy = last_copies(zp)
        from_y.wait_recv()
        add(acc.at[zp, 1 - x].at[top, mine], y_diag.at[zp])
        over_x_copy.start()
        from_x.wait_recv()
        add(acc.at[zp, x].at[low, theirs], x_diag.at[zp])
        over_y_copy.start()

    def arrivals(zp):
        for item in free_copies(zp) + last_copies(zp):
            item.wait_recv()

    def columns(zp):
        arrivals(zp)
        add(acc.at[zp, x].at[:, mine], x_in.at[zp], y_in.at[zp])
        plane_copy(zp).start()

    def final(result):
        arrivals(z)
        total = acc[z, x, :, mine].astype(jnp.float32)
        total = total + x_in[z].astype(jnp.float32) + y_in[z].astype(jnp.float32)
        for turn in range(1, 4):
            zp = plane_at(turn)
            plane_arrival(zp).wait_recv()
            total = total + z_in[zp].astype(jnp.float32)
        result[...] = total

    def close(zp):
        for xp in range(2):
            core_copy(zp, xp).wait_send()
        for item in diag_copies(zp) + free_copies(zp) + last_copies(zp):
            item.wait_send()

        @pl.when(zp != z)
        def _():
            plane_copy(zp).wait_send()

    return core_copy, cores, corners, columns, final, close


def choose(mine, chooser, which):
    requests, tokens = mine.shape
    capacity = chooser.shape[2]
    named = jnp.where(mine[...] > 0.0, 1.0, 0.0)
    rows = lax.broadcasted_iota(jnp.int32, (tokens, tokens), 0)
    columns = lax.broadcasted_iota(jnp.int32, (tokens, tokens), 1)
    before = jnp.where(rows <= columns, 1.0, 0.0).astype(jnp.bfloat16)
    slot = jnp.dot(named.astype(jnp.bfloat16), before, preferred_element_type=jnp.float32)
    wanted = jnp.where(named > 0.0, slot - 1.0, -1.0).astype(jnp.int32)
    places = lax.broadcasted_iota(jnp.int32, (capacity, tokens), 0)
    for request in range(requests):
        picks = jnp.where(wanted[request : request + 1, :] == places, 1.0, 0.0)
        chooser[which, request] = picks.astype(jnp.bfloat16)


def share_prompts(block_ref, share_ref, keys_ref, mine_ref, send, recv, send_w, recv_w, local):
    me = lax.axis_index("req")
    y = lax.axis_index("tp")
    depth = block_ref.shape[1]
    rows = pl.ds(pl.multiple_of(me * depth, depth), depth)
    core, other = me % 2, me + 1 - 2 * (me % 2)

    def block(source):
        return keys_ref.at[:, pl.ds(pl.multiple_of(source * depth, depth), depth), :]

    def shares(step):
        peer = (me + step) % 16
        return pltpu.make_async_remote_copy(
            share_ref.at[peer], mine_ref.at[me], send_w.at[step], recv_w.at[step],
            device_id={"req": peer, "tp": y}, device_id_type=MESH,
        )

    def direct(step):
        return pltpu.make_async_remote_copy(
            block_ref, keys_ref.at[:, rows, :], send.at[step], recv.at[step],
            device_id={"req": (me + 2 * step) % 16, "tp": y}, device_id_type=MESH,
        )

    def across(source, index):
        return pltpu.make_async_remote_copy(
            block(source), block(source), send.at[index], recv.at[index],
            device_id={"req": other, "tp": y}, device_id_type=MESH,
        )

    home = pltpu.make_async_remote_copy(
        block_ref, keys_ref.at[:, rows, :], send.at[8 + me // 2], recv.at[8 + me // 2],
        device_id={"req": other, "tp": y}, device_id_type=MESH,
    )
    own = pltpu.make_async_copy(block_ref, keys_ref.at[:, rows, :], local.at[0])
    own_share = pltpu.make_async_copy(share_ref.at[me], mine_ref.at[me], local.at[1])

    def start():
        for step in range(1, 8):
            direct(step).start()
        home.start()
        own.start()
        own_share.start()

        def send_share(step, carry):
            shares(step).start()
            return carry

        lax.fori_loop(1, 16, send_share, 0)

    def relay(step):
        source = (me + 2 * step) % 16
        across(source, 8 - step).wait_recv()
        across(source, 8 + source // 2).start()

    def finish():
        own.wait()
        for step in range(8):
            source = (me + 2 * step) % 16 + 1 - 2 * core
            across(source, 8 + source // 2).wait_recv()

    def finish_shares():
        own_share.wait()

        def wait_share(step, carry):
            shares(step).wait_recv()
            return carry

        lax.fori_loop(1, 16, wait_share, 0)

    def close():
        home.wait_send()
        for step in range(1, 8):
            direct(step).wait_send()
            source = (me + 2 * step) % 16
            across(source, 8 + source // 2).wait_send()

        def close_share(step, carry):
            shares(step).wait_send()
            return carry

        lax.fori_loop(1, 16, close_share, 0)

    return start, relay, finish, finish_shares, close


def layer_kernel(
    page_table, prefix_len, prompt_len, group_ids,
    routes, route_weight, gain, prompt_block,
    residual_hbm, query_hbm, stretch_hbm, pool_hbm, absorb_hbm, value_hbm, out_hbm, gate_hbm, up_hbm, down_hbm,
    attention_part, expert_part,
    query, residual, stretch, keys, absorb, value, out_w, prompts, absorbed, bests, totals, latents, bias,
    heads,
    share, share_in, projected,
    whole, outgoing, incoming, squares_out, squares_in, gains, mine_share, other_share, roots,
    chooser, level,
    gate_w, up_w, down_w, rows, hidden, parts, part_in, acc, x_diag, y_diag, x_in, y_in, z_in,
    prompt_send, prompt_recv, share_send, share_recv, local_sems,
    pair_sems, load_sems, root_sems, send, recv, sems,
):
    z, x, core, y = coordinates()
    me = lax.axis_index("req")
    tokens, half_cols = residual.shape
    half_rows = tokens // 2
    count, nope, rank = absorb.shape
    width = query.shape[1]
    pool_rows = pool_hbm.shape[0]
    own_rows = pool_rows + tokens
    loads = [
        pltpu.make_async_copy(source, target, load_sems.at[index])
        for index, (source, target) in enumerate(
            (
                (query_hbm, query), (absorb_hbm, absorb), (stretch_hbm, stretch),
                (pool_hbm, keys.at[pl.ds(0, pool_rows)]), (value_hbm, value), (out_hbm, out_w),
                (gate_hbm, gate_w), (up_hbm, up_w), (down_hbm, down_w), (residual_hbm, residual),
            )
        )
    ]
    for load in loads:
        load.start()
    mine = pl.ds(pl.multiple_of(y * half_cols, half_cols), half_cols)
    theirs = pl.ds(pl.multiple_of((1 - y) * half_cols, half_cols), half_cols)
    over_y, other = place(z, x, core, 1 - y), place(z, x, 1 - core, y)

    def pair(source, target, index, peer=over_y):
        return pltpu.make_async_remote_copy(
            source, target, pair_sems.at[0, index], pair_sems.at[1, index],
            device_id=peer, device_id_type=MESH,
        )

    def swap(half):
        lines = pl.ds(half * half_rows, half_rows)
        return pair(outgoing.at[lines], incoming.at[lines], half)

    squares = pair(squares_out, squares_in, 2)
    gain_copy = pair(gains.at[y], gains.at[y], 3)
    share_copy = pair(mine_share, other_share, 4, other)
    start_prompts, relay, finish_prompts, finish_shares, close_prompts = share_prompts(
        prompt_block, share, prompts, share_in, prompt_send, prompt_recv, share_send, share_recv,
        local_sems,
    )
    expert_of = lax.broadcasted_iota(jnp.int32, (16, tokens), 0)
    given = jnp.zeros((16, tokens), jnp.float32)
    for choice in range(routes.shape[0]):
        hit = routes[choice : choice + 1, :] == expert_of
        given = given + jnp.where(hit, route_weight[choice : choice + 1, :], 0.0)
    for expert in range(16):
        share[expert] = given[expert : expert + 1, :]
    gains[y] = gain[...].astype(jnp.float32)
    greet()
    start_prompts()
    gain_copy.start()
    group = group_ids[me]
    page = pool_rows // page_table.shape[1]
    lane = lax.broadcasted_iota(jnp.int32, (1, pool_rows), 1)
    logical = jnp.zeros((1, pool_rows), jnp.int32)
    for index in range(page_table.shape[1]):
        logical = jnp.where(lane // page == page_table[0, index], index, logical)
    prefix_at = logical * page + lane % page
    bias[:, pl.ds(0, pool_rows)] = jnp.where(prefix_at < prefix_len[me], 0.0, NEGATIVE)
    prompt_rows = prompts.shape[1]
    prompt_lane = lax.broadcasted_iota(jnp.int32, (1, prompt_rows), 1)
    bias[:, pl.ds(pool_rows, prompt_rows)] = jnp.where(prompt_lane < prompt_len[group], 0.0, NEGATIVE)
    loads[2].wait()
    keys[pl.ds(pool_rows, tokens), :] = stretch[...].T
    for index in (0, 1, 3):
        loads[index].wait()
    first = (((0,), (0,)), ((), ()))
    across = (((1,), (1,)), ((), ()))

    factor = width ** (-0.5) * math.log2(math.e)

    def own_keys(head):
        wide = lax.dot_general(
            query[head, pl.ds(0, nope), :], absorb[head], first, preferred_element_type=jnp.float32
        )
        absorbed[head, :, pl.ds(0, rank)] = wide.astype(jnp.bfloat16)
        absorbed[head, :, pl.ds(rank, width - nope)] = query[head, pl.ds(nope, width - nope), :].T
        found = lax.dot_general(
            absorbed[head], keys[pl.ds(0, own_rows), :], across, preferred_element_type=jnp.float32
        )
        later = lax.broadcasted_iota(jnp.int32, (tokens, tokens), 1) > lax.broadcasted_iota(
            jnp.int32, (tokens, tokens), 0
        )
        found = jnp.concatenate(
            [
                found[:, :pool_rows] + bias[:, pl.ds(0, pool_rows)],
                jnp.where(later, NEGATIVE, found[:, pool_rows:]),
            ],
            axis=1,
        )
        best = jnp.max(found, axis=1, keepdims=True)
        weights = jnp.exp2((found - best) * factor)
        bests[head] = best
        totals[head] = jnp.sum(weights, axis=1, keepdims=True)
        latents[head] = jnp.dot(
            weights.astype(jnp.bfloat16), keys[pl.ds(0, own_rows), pl.ds(0, rank)],
            preferred_element_type=jnp.float32,
        )

    def own_pair(index, carry):
        own_keys(2 * index)
        own_keys(2 * index + 1)

        @pl.when(index == 1)
        def _():
            for step in range(1, 4):
                relay(step)

        @pl.when(index == 2)
        def _():
            for step in range(4, 8):
                relay(step)

        return carry

    lax.fori_loop(0, count // 2, own_pair, 0)
    finish_prompts()
    keys[pl.ds(own_rows, prompt_rows), :] = prompts[group]
    loads[4].wait()
    loads[9].wait()
    size = value.shape[2]

    def prompt_keys(head, lines):
        found = lax.dot_general(
            absorbed[head, lines, :], keys[pl.ds(own_rows, prompt_rows), :], across,
            preferred_element_type=jnp.float32,
        ) + bias[:, pl.ds(pool_rows, prompt_rows)]
        held = bests[head, lines, :]
        best = jnp.maximum(jnp.max(found, axis=1, keepdims=True), held)
        keep = jnp.exp2((held - best) * factor)
        weights = jnp.exp2((found - best) * factor)
        total = totals[head, lines, :] * keep + jnp.sum(weights, axis=1, keepdims=True)
        latent = latents[head, lines, :] * keep + jnp.dot(
            weights.astype(jnp.bfloat16), keys[pl.ds(own_rows, prompt_rows), pl.ds(0, rank)],
            preferred_element_type=jnp.float32,
        )
        latent = (latent * (1.0 / total)).astype(jnp.bfloat16)
        heads[lines, pl.ds(pl.multiple_of(head * size, size), size)] = jnp.dot(
            latent, value[head], preferred_element_type=jnp.float32
        ).astype(jnp.bfloat16)

    for half in range(2):
        lines = pl.ds(half * half_rows, half_rows)

        def prompt_pair(index, carry, lines=lines):
            prompt_keys(2 * index, lines)
            prompt_keys(2 * index + 1, lines)
            return carry

        lax.fori_loop(0, count // 2, prompt_pair, 0)
        if half == 0:
            loads[5].wait()
        outgoing[lines, :] = jnp.dot(
            heads[lines, :], out_w[:, theirs], preferred_element_type=jnp.float32
        ).astype(jnp.bfloat16)
        swap(half).start()
    projected[...] = jnp.dot(heads[...], out_w[:, mine], preferred_element_type=jnp.float32)
    finish_shares()
    for request in range(16):
        mine_share[request : request + 1, :] = share_in[request]
    share_copy.start()
    choose(mine_share, chooser, 0)
    column, arrive, beside, diagonal, complete, close_spread = spread_tokens(whole, send, recv)
    diag = lax.broadcasted_iota(jnp.int32, (half_rows, tokens), 1) - lax.broadcasted_iota(
        jnp.int32, (half_rows, tokens), 0
    )
    sums = jnp.zeros((1, tokens), jnp.float32)
    for half in range(2):
        lines = pl.ds(half * half_rows, half_rows)
        swap(half).wait_recv()
        added = projected[lines, :] + incoming[lines, :].astype(jnp.float32)
        projected[lines, :] = added
        rounded = (residual[lines, :].astype(jnp.float32) + added).astype(jnp.bfloat16)
        whole[me, lines, mine] = rounded
        stream = rounded.astype(jnp.float32)
        line_sums = jnp.sum(stream * stream, axis=1, keepdims=True)
        sums = sums + jnp.sum(
            jnp.where(diag == half * half_rows, line_sums, 0.0), axis=0, keepdims=True
        )
        if half == 1:
            squares_out[...] = sums
            squares.start()
        column(z, False, (half,))
    part_out = pltpu.make_async_copy(projected, attention_part, load_sems.at[10])
    part_out.start()
    share_copy.wait_recv()
    choose(other_share, chooser, 1)

    def root_copy(step):
        peer = (me + step) % 16
        return pltpu.make_async_remote_copy(
            roots.at[me], roots.at[me], root_sems.at[0, peer], root_sems.at[1, me],
            device_id={"req": peer, "tp": y}, device_id_type=MESH,
        )

    def root_arrival(request):
        return pltpu.make_async_remote_copy(
            roots.at[request], roots.at[request], root_sems.at[0, request],
            root_sems.at[1, request], device_id=over_y, device_id_type=MESH,
        )

    arrive(plane_at(1))
    beside(z, False)
    squares.wait_recv()
    roots[me] = lax.rsqrt((squares_out[...] + squares_in[...]) / (2 * half_cols) + EPSILON)

    def send_root(step, carry):
        root_copy(step).start()
        return carry

    lax.fori_loop(1, 16, send_root, 0)
    gain_copy.wait_recv()
    for load in loads[6:9]:
        load.wait()
    capacity = chooser.shape[2]
    core_copy, cores, corners, columns, final, close_return = return_sums(
        parts, part_in, chooser, acc, x_diag, y_diag, x_in, y_in, z_in, sems
    )

    def compute(zp):
        for index in range(4):
            request = zp * 4 + index

            @pl.when(request != me)
            def _(request=request):
                root_arrival(request).wait_recv()

        for index in range(4):
            request = zp * 4 + index
            lines = pl.ds(index * capacity, capacity)
            picks = chooser[0, request]
            picked = jnp.dot(picks, whole[request], preferred_element_type=jnp.float32)
            wide = picks.astype(jnp.float32)
            picked = picked * jnp.sum(wide * roots[request], axis=1, keepdims=True)
            shared = jnp.sum(wide * share_in[request], axis=1, keepdims=True)
            level[lines, :] = jnp.broadcast_to(shared, (capacity, level.shape[1]))
            for side in range(2):
                span = pl.ds(side * half_cols, half_cols)
                scaled = picked[:, side * half_cols : (side + 1) * half_cols] * gains[side]
                rows[lines, span] = scaled.astype(jnp.bfloat16)
        gate = lax.dot_general(rows[...], gate_w[...], across, preferred_element_type=jnp.float32)
        up = lax.dot_general(rows[...], up_w[...], across, preferred_element_type=jnp.float32)
        hidden[...] = (gate / (1.0 + jnp.exp(-gate)) * up * level[:, :1]).astype(jnp.bfloat16)
        part = jnp.dot(hidden[...], down_w[...], preferred_element_type=jnp.float32)
        for index in range(4):
            parts[zp, index] = part[index * capacity : (index + 1) * capacity].astype(jnp.bfloat16)
        for xp in range(2):
            core_copy(zp, xp).start()

    def step(turn, carry):
        @pl.when(turn < 3)
        def _():
            arrive(plane_at(turn + 1))

        @pl.when(turn < 4)
        def _():
            beside(plane_at(turn), False)

        @pl.when((turn >= 4) & (turn < 8))
        def _():
            corners(plane_at((turn - 3) % 4))

        @pl.when((turn >= 3) & (turn < 7))
        def _():
            cores(plane_at((turn - 2) % 4))

        @pl.when(turn < 5)
        def _():
            zp = plane_at(turn - 1)
            diagonal(zp, False)
            complete(zp)
            compute(zp)

        @pl.when(turn >= 5)
        def _():
            columns(plane_at(turn - 4))

        return carry

    lax.fori_loop(1, 8, step, 0)
    final(expert_part)

    def close(zp, carry):
        close_spread(zp)
        close_return(zp)
        return carry

    lax.fori_loop(0, 4, close, 0)

    def close_root(step, carry):
        root_copy(step).wait_send()
        return carry

    lax.fori_loop(1, 16, close_root, 0)
    for item in (swap(0), swap(1), squares, gain_copy, share_copy):
        item.wait_send()
    close_prompts()
    part_out.wait()


def on_block(
    queries, stretch_cache, prefix_pool, page_table, prefix_len, prompt_cache, prompt_len,
    group_ids, absorb_weight, value_weight, out_weight, residual, norm_gain, routes,
    route_weight, gate_weight, up_weight, down_weight,
):
    tokens, count, width = queries.shape
    nope, rank = absorb_weight.shape[1:]
    size = value_weight.shape[2]
    top = routes.shape[1]
    experts = 16
    capacity = max(2, tokens * top * 4 // (3 * experts))
    pages, page, entry = prefix_pool.shape
    groups, depth = prompt_cache.shape[:2]
    half = residual.shape[1]
    model = out_weight.shape[1]
    units = down_weight.shape[1]
    own_rows = pages * page + tokens
    bf16, f32 = jnp.bfloat16, jnp.float32
    dma = pltpu.SemaphoreType.DMA
    vmem = pl.BlockSpec(memory_space=pltpu.VMEM)
    smem = pl.BlockSpec(memory_space=pltpu.SMEM)
    anywhere = pl.BlockSpec(memory_space=pl.ANY)
    attention_part, expert_part = pl.pallas_call(
        layer_kernel,
        out_shape=(jax.ShapeDtypeStruct((tokens, half), f32),) * 2,
        in_specs=[smem] * 4 + [vmem] * 4 + [anywhere] * 10,
        out_specs=(anywhere, vmem),
        scratch_shapes=[
            pltpu.VMEM((count, width, tokens), bf16),
            pltpu.VMEM((tokens, half), bf16),
            pltpu.VMEM((entry, tokens), bf16),
            pltpu.VMEM((own_rows + depth * 16, entry), bf16),
            pltpu.VMEM((count, nope, rank), bf16),
            pltpu.VMEM((count, rank, size), bf16),
            pltpu.VMEM((count * size, model), bf16),
            pltpu.VMEM((groups, depth * 16, entry), bf16),
            pltpu.VMEM((count, tokens, entry), bf16),
            pltpu.VMEM((count, tokens, 1), f32),
            pltpu.VMEM((count, tokens, 1), f32),
            pltpu.VMEM((count, tokens, rank), f32),
            pltpu.VMEM((1, pages * page + depth * 16), f32),
            pltpu.VMEM((tokens, count * size), bf16),
            pltpu.VMEM((16, 1, tokens), f32),
            pltpu.VMEM((16, 1, tokens), f32),
            pltpu.VMEM((tokens, half), f32),
            pltpu.VMEM((16, tokens, model), bf16),
            pltpu.VMEM((tokens, half), bf16),
            pltpu.VMEM((tokens, half), bf16),
            pltpu.VMEM((1, tokens), f32),
            pltpu.VMEM((1, tokens), f32),
            pltpu.VMEM((2, 1, half), f32),
            pltpu.VMEM((16, tokens), f32),
            pltpu.VMEM((16, tokens), f32),
            pltpu.VMEM((16, 1, tokens), f32),
            pltpu.VMEM((2, 16, capacity, tokens), bf16),
            pltpu.VMEM((4 * capacity, 128), f32),
            pltpu.VMEM((units, model), bf16),
            pltpu.VMEM((units, model), bf16),
            pltpu.VMEM((units, model), bf16),
            pltpu.VMEM((4 * capacity, model), bf16),
            pltpu.VMEM((4 * capacity, units), bf16),
            pltpu.VMEM((4, 4, capacity, model), bf16),
            pltpu.VMEM((4, 2, capacity, model), bf16),
            pltpu.VMEM((4, 2, tokens, model), bf16),
            pltpu.VMEM((4, tokens // 2, half), bf16),
            pltpu.VMEM((4, tokens // 2, half), bf16),
            pltpu.VMEM((4, tokens, half), bf16),
            pltpu.VMEM((4, tokens, half), bf16),
            pltpu.VMEM((4, tokens, half), bf16),
            dma((16,)),
            dma((16,)),
            dma((16,)),
            dma((16,)),
            dma((2,)),
            dma((2, 5)),
            dma((11,)),
            dma((2, 16)),
            dma((5, 32)),
            dma((2, 32)),
            dma((2, 9, 4)),
        ],
        compiler_params=pltpu.CompilerParams(
            collective_id=0, has_side_effects=True, vmem_limit_bytes=60 << 20
        ),
    )(
        page_table, prefix_len, prompt_len, group_ids,
        routes.T, route_weight.T, norm_gain[None, :], prompt_cache, residual,
        jnp.transpose(queries, (1, 2, 0)), stretch_cache.T, prefix_pool.reshape(pages * page, entry),
        absorb_weight, value_weight, out_weight,
        jnp.swapaxes(gate_weight[0], 0, 1), jnp.swapaxes(up_weight[0], 0, 1), down_weight[0],
    )
    attended = (residual.astype(f32) + attention_part).astype(bf16)
    return attended, (attended.astype(f32) + expert_part).astype(bf16)


def solution(mesh):
    in_specs = (
        P("req", "tp", None),
        P("req", None),
        P("req", None, None),
        P("req", None),
        P(),
        P(None, "req", None),
        P(),
        P(),
        P("tp", None, None),
        P("tp", None, None),
        P("tp", None),
        P("req", "tp"),
        P("tp"),
        P("req", None),
        P("req", None),
        P("req", None, "tp"),
        P("req", None, "tp"),
        P("req", "tp", None),
    )
    out_specs = (P("req", "tp"), P("req", "tp"))
    body = on_block if mesh.shape["req"] == 16 and mesh.shape["tp"] == 2 else on_device
    return jax.shard_map(
        body, mesh=mesh, in_specs=in_specs, out_specs=out_specs, check_vma=False
    )
```

```python
import math

import jax
import jax.numpy as jnp
from jax import lax
from jax.experimental import pallas as pl
from jax.experimental.pallas import tpu as pltpu
from jax.sharding import PartitionSpec as P

NEGATIVE = -1e30
EPSILON = 1e-06


def on_device(
    queries, stretch_cache, prefix_pool, page_table, prefix_len, prompt_cache, prompt_len,
    group_ids, absorb_weight, value_weight, out_weight, residual, norm_gain, routes,
    route_weight, gate_weight, up_weight, down_weight,
):
    tokens = queries.shape[0]
    prompts = lax.all_gather(prompt_cache, "req", axis=1, tiled=True)
    projected = attend(
        queries, stretch_cache, prefix_pool, page_table, prefix_len, prompts, prompt_len,
        group_ids, absorb_weight, value_weight, out_weight,
    )
    attention_part = lax.psum_scatter(
        projected.astype(jnp.bfloat16), "tp", scatter_dimension=1, tiled=True
    ).astype(jnp.float32)
    attended = (residual.astype(jnp.float32) + attention_part).astype(jnp.bfloat16)
    stream = attended.astype(jnp.float32)
    squares = lax.psum(jnp.sum(stream * stream, axis=1), "tp")
    model_width = out_weight.shape[1]
    normed = (
        stream * lax.rsqrt(squares / model_width + EPSILON)[:, None] * norm_gain.astype(jnp.float32)
    ).astype(jnp.bfloat16)
    experts = lax.axis_size("req")
    top = routes.shape[1]
    capacity = max(2, tokens * top * 4 // (3 * experts))
    choice = routes[:, :, None] == jnp.arange(experts, dtype=jnp.int32)[None, None, :]
    share = jnp.sum(jnp.where(choice, route_weight[:, :, None], 0.0), axis=1).T
    named = share > 0.0
    before = jnp.arange(tokens)[:, None] <= jnp.arange(tokens)[None, :]
    slot = jnp.dot(
        named.astype(jnp.bfloat16), before.astype(jnp.bfloat16), preferred_element_type=jnp.float32
    ).astype(jnp.int32) - 1
    picks = (
        slot[:, None, :] == jnp.arange(capacity, dtype=jnp.int32)[None, :, None]
    ) & named[:, None, :]
    chooser = picks.astype(jnp.bfloat16).reshape(experts * capacity, tokens)
    level = jnp.sum(jnp.where(picks, share[:, None, :], 0.0), axis=2)
    whole = lax.all_gather(normed, "tp", axis=1, tiled=True)
    buffer = (
        jnp.dot(chooser, whole, preferred_element_type=jnp.float32)
        .astype(jnp.bfloat16)
        .reshape(experts, capacity, -1)
    )
    received = lax.all_to_all(buffer, "req", split_axis=0, concat_axis=0, tiled=True)
    gate = jnp.einsum("snd,df->snf", received, gate_weight[0], preferred_element_type=jnp.float32)
    up = jnp.einsum("snd,df->snf", received, up_weight[0], preferred_element_type=jnp.float32)
    hidden = (jax.nn.silu(gate) * up).astype(jnp.bfloat16)
    part_out = jnp.einsum(
        "snf,fd->snd", hidden, down_weight[0], preferred_element_type=jnp.float32
    ).astype(jnp.bfloat16)
    returned = lax.all_to_all(part_out, "req", split_axis=0, concat_axis=0, tiled=True)
    weighted = (returned.astype(jnp.float32) * level[:, :, None]).astype(jnp.bfloat16)
    combined = lax.dot_general(
        chooser, weighted.reshape(experts * capacity, -1), (((0,), (0,)), ((), ())),
        preferred_element_type=jnp.float32,
    )
    expert_part = lax.psum_scatter(
        combined.astype(jnp.bfloat16), "tp", scatter_dimension=1, tiled=True
    ).astype(jnp.float32)
    mixed = (stream + expert_part).astype(jnp.bfloat16)
    return (attended, mixed)


def attend(
    queries, stretch_cache, prefix_pool, page_table, prefix_len, prompts, prompt_len,
    group_ids, absorb_weight, value_weight, out_weight,
):
    tokens, heads, width = queries.shape
    nope, rank = absorb_weight.shape[1], value_weight.shape[1]
    me = lax.axis_index("req")
    requests = jnp.arange(group_ids.shape[0], dtype=jnp.int32) == me
    group = jnp.sum(jnp.where(requests, group_ids, 0))
    own_length = jnp.sum(jnp.where(requests, prefix_len, 0))
    prompt_length = jnp.where(group == 0, prompt_len[0], prompt_len[1])
    pages, page = prefix_pool.shape[:2]
    order = jnp.arange(pages, dtype=jnp.int32)
    logical = jnp.sum(
        jnp.where(page_table[0][None, :] == order[:, None], order[None, :], 0), axis=1
    )
    prefix_at = (logical[:, None] * page + jnp.arange(page, dtype=jnp.int32)[None, :]).reshape(-1)
    prompt = jnp.where(group == 0, prompts[0], prompts[1])
    keys = jnp.concatenate(
        [stretch_cache, prompt, prefix_pool.reshape(pages * page, -1)], axis=0
    )
    seen = jnp.concatenate(
        [jnp.arange(prompt.shape[0]) < prompt_length, prefix_at < own_length]
    )
    token = jnp.arange(tokens)
    visible = jnp.concatenate(
        [
            token[None, :] <= token[:, None],
            jnp.broadcast_to(seen[None, :], (tokens, seen.shape[0])),
        ],
        axis=1,
    )
    turned = jnp.transpose(queries, (1, 0, 2))
    absorbed = jnp.concatenate(
        [
            jnp.einsum(
                "htn,hnr->htr", turned[:, :, :nope], absorb_weight,
                preferred_element_type=jnp.float32,
            ).astype(jnp.bfloat16),
            turned[:, :, nope:],
        ],
        axis=2,
    )
    scores = jnp.einsum("htc,kc->htk", absorbed, keys, preferred_element_type=jnp.float32)
    scores = jnp.where(visible[None], scores * width ** (-0.5), NEGATIVE)
    weights = jnp.exp(scores - jnp.max(scores, axis=2, keepdims=True))
    weights = jnp.where(visible[None], weights, 0.0)
    totals = jnp.sum(weights, axis=2, keepdims=True)
    latent = jnp.einsum(
        "htk,kr->htr", weights.astype(jnp.bfloat16), keys[:, :rank],
        preferred_element_type=jnp.float32,
    )
    latent = (latent / totals).astype(jnp.bfloat16)
    heads_out = jnp.einsum(
        "htr,hrv->thv", latent, value_weight, preferred_element_type=jnp.float32
    ).astype(jnp.bfloat16)
    return jnp.dot(
        heads_out.reshape(tokens, -1), out_weight, preferred_element_type=jnp.float32
    )


MESH = pl.DeviceIdType.MESH


def coordinates():
    me = lax.axis_index("req")
    return me // 4, (me // 2) % 2, me % 2, lax.axis_index("tp")


def place(z, x, core, y):
    return {"req": (z * 2 + x) * 2 + core, "tp": y}


def greet():
    z, x, core, y = coordinates()
    me = lax.axis_index("req")
    barrier = pltpu.get_barrier_semaphore()
    for step in range(1, 16):
        pl.semaphore_signal(
            barrier, inc=1, device_id={"req": (me + step) % 16, "tp": y}, device_id_type=MESH
        )
    pl.semaphore_signal(barrier, inc=1, device_id=place(z, x, core, 1 - y), device_id_type=MESH)
    pl.semaphore_wait(barrier, 16)


def plane_at(place_in_turn):
    z = coordinates()[0]
    high = z // 2
    near = z + high * (3 - 2 * z)
    late = place_in_turn // 2
    odd = place_in_turn % 2
    first = (1 - odd) * (1 - late) * near + odd * (1 - late) * (1 - near) + late * place_in_turn
    return first + high * (3 - 2 * first)


def spread_tokens(whole, send, recv):
    z, x, core, y = coordinates()
    quarter = whole.shape[2] // 4

    def piece(zp, xp, yp, half, cp):
        return whole.at[
            (zp * 2 + xp) * 2 + cp,
            :,
            pl.ds(pl.multiple_of((yp * 2 + half) * quarter, quarter), quarter),
        ]

    def hop(zp, xp, yp, half, cp, kind, peer):
        slot = zp * 8 + xp * 4 + yp * 2 + half
        part = piece(zp, xp, yp, half, cp)
        return pltpu.make_async_remote_copy(
            part, part, send.at[kind, slot], recv.at[cp, slot], device_id=peer, device_id_type=MESH
        )

    up, down = place(z + 1, x, core, y), place(z - 1, x, core, y)
    over_x, over_y, other = place(z, 1 - x, core, y), place(z, x, core, 1 - y), place(z, x, 1 - core, y)

    def column(zp, finish, halves=(0, 1)):
        for half in halves:
            for go, kind, peer in (
                ((zp <= z) & (z < 3), 0, up), ((zp >= z) & (z > 0), 1, down)
            ):
                @pl.when(go)
                def _(kind=kind, peer=peer, half=half):
                    copy = hop(zp, x, y, half, core, kind, peer)
                    copy.wait_send() if finish else copy.start()
        for kind, peer, half in ((2, over_x, 0), (3, over_y, 1), (2, over_x, 1), (3, over_y, 0)):
            if half in halves:
                copy = hop(zp, x, y, half, core, kind, peer)
                copy.wait_send() if finish else copy.start()
        for half in halves:
            copy = hop(zp, x, y, half, core, 4, other)
            copy.wait_send() if finish else copy.start()

    def arrive(zp):
        for half in range(2):
            hop(zp, x, y, half, core, 0, over_x).wait_recv()
        column(zp, False)

    def beside(zp, finish):
        if not finish:
            for half in range(2):
                hop(zp, 1 - x, y, half, core, 2, over_x).wait_recv()
                hop(zp, x, 1 - y, half, core, 3, over_y).wait_recv()
        copies = [hop(zp, 1 - x, y, 0, core, 3, over_y), hop(zp, x, 1 - y, 1, core, 2, over_x)]
        for half in range(2):
            copies.append(hop(zp, 1 - x, y, half, core, 4, other))
            copies.append(hop(zp, x, 1 - y, half, core, 4, other))
        for copy in copies:
            copy.wait_send() if finish else copy.start()

    def diagonal(zp, finish):
        for half in range(2):
            copy = hop(zp, 1 - x, 1 - y, half, core, 4, other)
            if finish:
                copy.wait_send()
            else:
                hop(zp, 1 - x, 1 - y, half, core, 2, over_x).wait_recv()
                copy.start()

    def complete(zp):
        for xp in range(2):
            for yp in range(2):
                for half in range(2):
                    hop(zp, xp, yp, half, 1 - core, 4, other).wait_recv()

    def close(zp):
        column(zp, True)
        beside(zp, True)
        diagonal(zp, True)

    return column, arrive, beside, diagonal, complete, close


def return_sums(parts, part_in, chooser, acc, x_diag, y_diag, x_in, y_in, z_in, sems):
    z, x, core, y = coordinates()
    rows, half_cols = acc.shape[2], acc.shape[3] // 2
    half_rows = rows // 2
    over_x, over_y, other = place(z, 1 - x, core, y), place(z, x, core, 1 - y), place(z, x, 1 - core, y)
    mine = pl.ds(pl.multiple_of(y * half_cols, half_cols), half_cols)
    theirs = pl.ds(pl.multiple_of((1 - y) * half_cols, half_cols), half_cols)
    top, low = pl.ds(0, half_rows), pl.ds(half_rows, half_rows)

    def copy(source, target, kind, zp, peer):
        return pltpu.make_async_remote_copy(
            source, target, sems.at[0, kind, zp], sems.at[1, kind, zp],
            device_id=peer, device_id_type=MESH,
        )

    def core_copy(zp, xp):
        return copy(parts.at[zp, xp * 2 + 1 - core], part_in.at[zp, xp], xp, zp, other)

    def diag_copies(zp):
        far = acc.at[zp, 1 - x]
        return (
            copy(far.at[top, theirs], y_diag.at[zp], 2, zp, over_y),
            copy(far.at[low, theirs], x_diag.at[zp], 3, zp, over_x),
        )

    def free_copies(zp):
        return (
            copy(acc.at[zp, 1 - x].at[low, mine], x_in.at[zp, low], 4, zp, over_x),
            copy(acc.at[zp, x].at[top, theirs], y_in.at[zp, top], 5, zp, over_y),
        )

    def last_copies(zp):
        return (
            copy(acc.at[zp, 1 - x].at[top, mine], x_in.at[zp, top], 6, zp, over_x),
            copy(acc.at[zp, x].at[low, theirs], y_in.at[zp, low], 7, zp, over_y),
        )

    def plane_copy(zp):
        return pltpu.make_async_remote_copy(
            acc.at[zp, x].at[:, mine], z_in.at[z], sems.at[0, 8, zp], sems.at[1, 8, z],
            device_id=place(zp, x, core, y), device_id_type=MESH,
        )

    def plane_arrival(zp):
        return pltpu.make_async_remote_copy(
            acc.at[zp, x].at[:, mine], z_in.at[zp], sems.at[0, 8, zp], sems.at[1, 8, zp],
            device_id=place(zp, x, core, y), device_id_type=MESH,
        )

    def add(target, *terms):
        total = target[...].astype(jnp.float32)
        for term in terms:
            total = total + term[...].astype(jnp.float32)
        target[...] = total.astype(target.dtype)

    def cores(zp):
        down = (((0,), (0,)), ((), ()))
        for xp in range(2):
            core_copy(zp, xp).wait_recv()
            request = (zp * 2 + xp) * 2 + core
            total = lax.dot_general(
                chooser[0, request], parts[zp, xp * 2 + core], down,
                preferred_element_type=jnp.float32,
            ) + lax.dot_general(
                chooser[1, request], part_in[zp, xp], down, preferred_element_type=jnp.float32
            )
            acc[zp, xp] = total.astype(jnp.bfloat16)
        for item in diag_copies(zp) + free_copies(zp):
            item.start()

    def corners(zp):
        from_y, from_x = diag_copies(zp)
        over_x_copy, over_y_copy = last_copies(zp)
        from_y.wait_recv()
        add(acc.at[zp, 1 - x].at[top, mine], y_diag.at[zp])
        over_x_copy.start()
        from_x.wait_recv()
        add(acc.at[zp, x].at[low, theirs], x_diag.at[zp])
        over_y_copy.start()

    def arrivals(zp):
        for item in free_copies(zp) + last_copies(zp):
            item.wait_recv()

    def columns(zp):
        arrivals(zp)
        add(acc.at[zp, x].at[:, mine], x_in.at[zp], y_in.at[zp])
        plane_copy(zp).start()

    def final(result):
        arrivals(z)
        total = acc[z, x, :, mine].astype(jnp.float32)
        total = total + x_in[z].astype(jnp.float32) + y_in[z].astype(jnp.float32)
        for turn in range(1, 4):
            zp = plane_at(turn)
            plane_arrival(zp).wait_recv()
            total = total + z_in[zp].astype(jnp.float32)
        result[...] = total

    def close(zp):
        for xp in range(2):
            core_copy(zp, xp).wait_send()
        for item in diag_copies(zp) + free_copies(zp) + last_copies(zp):
            item.wait_send()

        @pl.when(zp != z)
        def _():
            plane_copy(zp).wait_send()

    return core_copy, cores, corners, columns, final, close


def choose(mine, chooser, which):
    requests, tokens = mine.shape
    capacity = chooser.shape[2]
    named = jnp.where(mine[...] > 0.0, 1.0, 0.0)
    rows = lax.broadcasted_iota(jnp.int32, (tokens, tokens), 0)
    columns = lax.broadcasted_iota(jnp.int32, (tokens, tokens), 1)
    before = jnp.where(rows <= columns, 1.0, 0.0).astype(jnp.bfloat16)
    slot = jnp.dot(named.astype(jnp.bfloat16), before, preferred_element_type=jnp.float32)
    wanted = jnp.where(named > 0.0, slot - 1.0, -1.0).astype(jnp.int32)
    places = lax.broadcasted_iota(jnp.int32, (capacity, tokens), 0)
    for request in range(requests):
        picks = jnp.where(wanted[request : request + 1, :] == places, 1.0, 0.0)
        chooser[which, request] = picks.astype(jnp.bfloat16)


def share_prompts(block_ref, share_ref, keys_ref, mine_ref, send, recv, send_w, recv_w, local):
    me = lax.axis_index("req")
    y = lax.axis_index("tp")
    depth = block_ref.shape[1]
    rows = pl.ds(pl.multiple_of(me * depth, depth), depth)
    core, other = me % 2, me + 1 - 2 * (me % 2)

    def block(source):
        return keys_ref.at[:, pl.ds(pl.multiple_of(source * depth, depth), depth), :]

    def shares(step):
        peer = (me + step) % 16
        return pltpu.make_async_remote_copy(
            share_ref.at[peer], mine_ref.at[me], send_w.at[step], recv_w.at[step],
            device_id={"req": peer, "tp": y}, device_id_type=MESH,
        )

    def direct(step):
        return pltpu.make_async_remote_copy(
            block_ref, keys_ref.at[:, rows, :], send.at[step], recv.at[step],
            device_id={"req": (me + 2 * step) % 16, "tp": y}, device_id_type=MESH,
        )

    def across(source, index):
        return pltpu.make_async_remote_copy(
            block(source), block(source), send.at[index], recv.at[index],
            device_id={"req": other, "tp": y}, device_id_type=MESH,
        )

    home = pltpu.make_async_remote_copy(
        block_ref, keys_ref.at[:, rows, :], send.at[8 + me // 2], recv.at[8 + me // 2],
        device_id={"req": other, "tp": y}, device_id_type=MESH,
    )
    own = pltpu.make_async_copy(block_ref, keys_ref.at[:, rows, :], local.at[0])
    own_share = pltpu.make_async_copy(share_ref.at[me], mine_ref.at[me], local.at[1])

    def start():
        for step in range(1, 8):
            direct(step).start()
        home.start()
        own.start()
        own_share.start()

        def send_share(step, carry):
            shares(step).start()
            return carry

        lax.fori_loop(1, 16, send_share, 0)

    def relay(step):
        source = (me + 2 * step) % 16
        across(source, 8 - step).wait_recv()
        across(source, 8 + source // 2).start()

    def finish():
        own.wait()
        for step in range(8):
            source = (me + 2 * step) % 16 + 1 - 2 * core
            across(source, 8 + source // 2).wait_recv()

    def finish_shares():
        own_share.wait()

        def wait_share(step, carry):
            shares(step).wait_recv()
            return carry

        lax.fori_loop(1, 16, wait_share, 0)

    def close():
        home.wait_send()
        for step in range(1, 8):
            direct(step).wait_send()
            source = (me + 2 * step) % 16
            across(source, 8 + source // 2).wait_send()

        def close_share(step, carry):
            shares(step).wait_send()
            return carry

        lax.fori_loop(1, 16, close_share, 0)

    return start, relay, finish, finish_shares, close


def layer_kernel(
    page_table, prefix_len, prompt_len, group_ids,
    routes, route_weight, gain, prompt_block,
    residual_hbm, query_hbm, stretch_hbm, pool_hbm, absorb_hbm, value_hbm, out_hbm, gate_hbm, up_hbm, down_hbm,
    attention_part, expert_part,
    query, residual, stretch, keys, absorb, value, out_w, prompts, absorbed, bests, totals, latents, bias,
    heads,
    share, share_in, projected,
    whole, outgoing, incoming, squares_out, squares_in, gains, mine_share, other_share, roots,
    chooser, level,
    gate_w, up_w, down_w, rows, hidden, parts, part_in, acc, x_diag, y_diag, x_in, y_in, z_in,
    prompt_send, prompt_recv, share_send, share_recv, local_sems,
    pair_sems, load_sems, root_sems, send, recv, sems,
):
    z, x, core, y = coordinates()
    me = lax.axis_index("req")
    tokens, half_cols = residual.shape
    quarter = half_cols // 2
    count, nope, rank = absorb.shape
    width = query.shape[1]
    pool_rows = pool_hbm.shape[0]
    own_rows = pool_rows + tokens
    loads = [
        pltpu.make_async_copy(source, target, load_sems.at[index])
        for index, (source, target) in enumerate(
            (
                (query_hbm, query), (absorb_hbm, absorb), (stretch_hbm, stretch),
                (pool_hbm, keys.at[pl.ds(0, pool_rows)]), (value_hbm, value), (out_hbm, out_w),
                (gate_hbm, gate_w), (up_hbm, up_w), (down_hbm, down_w), (residual_hbm, residual),
            )
        )
    ]
    for load in loads:
        load.start()
    mine = pl.ds(pl.multiple_of(y * half_cols, half_cols), half_cols)
    theirs = pl.ds(pl.multiple_of((1 - y) * half_cols, half_cols), half_cols)
    over_y, other = place(z, x, core, 1 - y), place(z, x, 1 - core, y)

    def pair(source, target, index, peer=over_y):
        return pltpu.make_async_remote_copy(
            source, target, pair_sems.at[0, index], pair_sems.at[1, index],
            device_id=peer, device_id_type=MESH,
        )

    def swap(half):
        span = pl.ds(half * quarter, quarter)
        return pair(outgoing.at[:, span], incoming.at[:, span], half)

    squares = pair(squares_out, squares_in, 2)
    gain_copy = pair(gains.at[y], gains.at[y], 3)
    share_copy = pair(mine_share, other_share, 4, other)
    start_prompts, relay, finish_prompts, finish_shares, close_prompts = share_prompts(
        prompt_block, share, prompts, share_in, prompt_send, prompt_recv, share_send, share_recv,
        local_sems,
    )
    expert_of = lax.broadcasted_iota(jnp.int32, (16, tokens), 0)
    given = jnp.zeros((16, tokens), jnp.float32)
    for choice in range(routes.shape[0]):
        hit = routes[choice : choice + 1, :] == expert_of
        given = given + jnp.where(hit, route_weight[choice : choice + 1, :], 0.0)
    for expert in range(16):
        share[expert] = given[expert : expert + 1, :]
    for row in range(gain.shape[0]):
        gains[y, :, pl.ds(row * gain.shape[1], gain.shape[1])] = gain[row : row + 1, :].astype(
            jnp.float32
        )
    greet()
    start_prompts()
    gain_copy.start()
    group = group_ids[me]
    page = pool_rows // page_table.shape[1]
    lane = lax.broadcasted_iota(jnp.int32, (1, pool_rows), 1)
    logical = jnp.zeros((1, pool_rows), jnp.int32)
    for index in range(page_table.shape[1]):
        logical = jnp.where(lane // page == page_table[0, index], index, logical)
    prefix_at = logical * page + lane % page
    bias[:, pl.ds(0, pool_rows)] = jnp.where(prefix_at < prefix_len[me], 0.0, NEGATIVE)
    prompt_rows = prompts.shape[1]
    prompt_lane = lax.broadcasted_iota(jnp.int32, (1, prompt_rows), 1)
    bias[:, pl.ds(pool_rows, prompt_rows)] = jnp.where(prompt_lane < prompt_len[group], 0.0, NEGATIVE)
    loads[2].wait()
    keys[pl.ds(pool_rows, tokens), :] = stretch[...].T
    for index in (0, 1, 3):
        loads[index].wait()
    first = (((0,), (0,)), ((), ()))
    across = (((1,), (1,)), ((), ()))

    factor = width ** (-0.5) * math.log2(math.e)

    batch = count // 2
    deep = batch * tokens

    def own_keys(index, carry):
        lines = pl.ds(pl.multiple_of(index * deep, deep), deep)
        for turn in range(batch):
            head = index * batch + turn
            own = pl.ds(pl.multiple_of(head * tokens, tokens), tokens)
            wide = lax.dot_general(
                query[head, pl.ds(0, nope), :], absorb[head], first,
                preferred_element_type=jnp.float32,
            )
            absorbed[own, pl.ds(0, rank)] = wide.astype(jnp.bfloat16)
            absorbed[own, pl.ds(rank, width - nope)] = query[head, pl.ds(nope, width - nope), :].T
        found = lax.dot_general(
            absorbed[lines, :], keys[pl.ds(0, own_rows), :], across,
            preferred_element_type=jnp.float32,
        )
        token = lax.rem(lax.broadcasted_iota(jnp.int32, (deep, tokens), 0), tokens)
        later = lax.broadcasted_iota(jnp.int32, (deep, tokens), 1) > token
        found = jnp.concatenate(
            [
                found[:, :pool_rows] + bias[:, pl.ds(0, pool_rows)],
                jnp.where(later, NEGATIVE, found[:, pool_rows:]),
            ],
            axis=1,
        )
        best = jnp.max(found, axis=1, keepdims=True)
        weights = jnp.exp2((found - best) * factor)
        bests[lines, :] = best
        totals[lines, :] = jnp.sum(weights, axis=1, keepdims=True)
        latents[lines, :] = jnp.dot(
            weights.astype(jnp.bfloat16), keys[pl.ds(0, own_rows), pl.ds(0, rank)],
            preferred_element_type=jnp.float32,
        )

        @pl.when(index == 0)
        def _():
            for step in range(1, 8):
                relay(step)

        return carry

    lax.fori_loop(0, 2, own_keys, 0)
    finish_prompts()
    keys[pl.ds(own_rows, prompt_rows), :] = prompts[group]
    loads[4].wait()
    loads[9].wait()
    size = value.shape[2]

    def prompt_keys(index, carry):
        lines = pl.ds(pl.multiple_of(index * deep, deep), deep)
        found = lax.dot_general(
            absorbed[lines, :], keys[pl.ds(own_rows, prompt_rows), :], across,
            preferred_element_type=jnp.float32,
        ) + bias[:, pl.ds(pool_rows, prompt_rows)]
        held = bests[lines, :]
        best = jnp.maximum(jnp.max(found, axis=1, keepdims=True), held)
        keep = jnp.exp2((held - best) * factor)
        weights = jnp.exp2((found - best) * factor)
        total = totals[lines, :] * keep + jnp.sum(weights, axis=1, keepdims=True)
        latent = latents[lines, :] * keep + jnp.dot(
            weights.astype(jnp.bfloat16), keys[pl.ds(own_rows, prompt_rows), pl.ds(0, rank)],
            preferred_element_type=jnp.float32,
        )
        latent = (latent * (1.0 / total)).astype(jnp.bfloat16)
        for turn in range(batch):
            head = index * batch + turn
            heads[:, pl.ds(pl.multiple_of(head * size, size), size)] = jnp.dot(
                latent[turn * tokens : (turn + 1) * tokens], value[head],
                preferred_element_type=jnp.float32,
            ).astype(jnp.bfloat16)
        return carry

    lax.fori_loop(0, 2, prompt_keys, 0)
    loads[5].wait()
    for half in range(2):
        across_cols = pl.ds(
            pl.multiple_of((1 - y) * half_cols + half * quarter, quarter), quarter
        )
        outgoing[:, pl.ds(half * quarter, quarter)] = jnp.dot(
            heads[...], out_w[:, across_cols], preferred_element_type=jnp.float32
        ).astype(jnp.bfloat16)
        swap(half).start()
    for half in range(2):
        own_cols = pl.ds(pl.multiple_of(y * half_cols + half * quarter, quarter), quarter)
        projected[:, pl.ds(half * quarter, quarter)] = jnp.dot(
            heads[...], out_w[:, own_cols], preferred_element_type=jnp.float32
        )
    finish_shares()
    for request in range(16):
        mine_share[request : request + 1, :] = share_in[request]
    share_copy.start()
    choose(mine_share, chooser, 0)
    column, arrive, beside, diagonal, complete, close_spread = spread_tokens(whole, send, recv)
    sums = jnp.zeros((tokens, 1), jnp.float32)
    for half in range(2):
        span = pl.ds(half * quarter, quarter)
        swap(half).wait_recv()
        added = projected[:, span] + incoming[:, span].astype(jnp.float32)
        projected[:, span] = added
        rounded = (residual[:, span].astype(jnp.float32) + added).astype(jnp.bfloat16)
        whole[me, :, pl.ds(pl.multiple_of(y * half_cols + half * quarter, quarter), quarter)] = rounded
        stream = rounded.astype(jnp.float32)
        sums = sums + jnp.sum(stream * stream, axis=1, keepdims=True)
        if half == 1:
            diag = lax.broadcasted_iota(jnp.int32, (tokens, tokens), 1) == (
                lax.broadcasted_iota(jnp.int32, (tokens, tokens), 0)
            )
            squares_out[...] = jnp.sum(jnp.where(diag, sums, 0.0), axis=0, keepdims=True)
            squares.start()
        column(z, False, (half,))
    part_out = pltpu.make_async_copy(projected, attention_part, load_sems.at[10])
    part_out.start()
    share_copy.wait_recv()
    choose(other_share, chooser, 1)

    def root_copy(step):
        peer = (me + step) % 16
        return pltpu.make_async_remote_copy(
            roots.at[me], roots.at[me], root_sems.at[0, peer], root_sems.at[1, me],
            device_id={"req": peer, "tp": y}, device_id_type=MESH,
        )

    def root_arrival(request):
        return pltpu.make_async_remote_copy(
            roots.at[request], roots.at[request], root_sems.at[0, request],
            root_sems.at[1, request], device_id=over_y, device_id_type=MESH,
        )

    arrive(plane_at(1))
    beside(z, False)
    squares.wait_recv()
    roots[me] = lax.rsqrt((squares_out[...] + squares_in[...]) / (2 * half_cols) + EPSILON)

    def send_root(step, carry):
        root_copy(step).start()
        return carry

    lax.fori_loop(1, 16, send_root, 0)
    gain_copy.wait_recv()
    for load in loads[6:9]:
        load.wait()
    capacity = chooser.shape[2]
    core_copy, cores, corners, columns, final, close_return = return_sums(
        parts, part_in, chooser, acc, x_diag, y_diag, x_in, y_in, z_in, sems
    )

    def compute(zp):
        for index in range(4):
            request = zp * 4 + index

            @pl.when(request != me)
            def _(request=request):
                root_arrival(request).wait_recv()

        for index in range(4):
            request = zp * 4 + index
            lines = pl.ds(index * capacity, capacity)
            picks = chooser[0, request]
            picked = jnp.dot(picks, whole[request], preferred_element_type=jnp.float32)
            wide = picks.astype(jnp.float32)
            picked = picked * jnp.sum(wide * roots[request], axis=1, keepdims=True)
            shared = jnp.sum(wide * share_in[request], axis=1, keepdims=True)
            level[lines, :] = jnp.broadcast_to(shared, (capacity, level.shape[1]))
            for side in range(2):
                span = pl.ds(side * half_cols, half_cols)
                scaled = picked[:, side * half_cols : (side + 1) * half_cols] * gains[side]
                rows[lines, span] = scaled.astype(jnp.bfloat16)
        gate = lax.dot_general(rows[...], gate_w[...], across, preferred_element_type=jnp.float32)
        up = lax.dot_general(rows[...], up_w[...], across, preferred_element_type=jnp.float32)
        hidden[...] = (gate / (1.0 + jnp.exp(-gate)) * up * level[:, :1]).astype(jnp.bfloat16)
        part = jnp.dot(hidden[...], down_w[...], preferred_element_type=jnp.float32)
        for index in range(4):
            parts[zp, index] = part[index * capacity : (index + 1) * capacity].astype(jnp.bfloat16)
        for xp in range(2):
            core_copy(zp, xp).start()

    def step(turn, carry):
        @pl.when(turn < 3)
        def _():
            arrive(plane_at(turn + 1))

        @pl.when(turn < 4)
        def _():
            beside(plane_at(turn), False)

        @pl.when((turn >= 4) & (turn < 8))
        def _():
            corners(plane_at((turn - 3) % 4))

        @pl.when((turn >= 3) & (turn < 7))
        def _():
            cores(plane_at((turn - 2) % 4))

        @pl.when(turn < 5)
        def _():
            zp = plane_at(turn - 1)
            diagonal(zp, False)
            complete(zp)
            compute(zp)

        @pl.when(turn >= 5)
        def _():
            columns(plane_at(turn - 4))

        return carry

    lax.fori_loop(1, 8, step, 0)
    final(expert_part)

    def close(zp, carry):
        close_spread(zp)
        close_return(zp)
        return carry

    lax.fori_loop(0, 4, close, 0)

    def close_root(step, carry):
        root_copy(step).wait_send()
        return carry

    lax.fori_loop(1, 16, close_root, 0)
    for item in (swap(0), swap(1), squares, gain_copy, share_copy):
        item.wait_send()
    close_prompts()
    part_out.wait()


def on_block(
    queries, stretch_cache, prefix_pool, page_table, prefix_len, prompt_cache, prompt_len,
    group_ids, absorb_weight, value_weight, out_weight, residual, norm_gain, routes,
    route_weight, gate_weight, up_weight, down_weight,
):
    tokens, count, width = queries.shape
    nope, rank = absorb_weight.shape[1:]
    size = value_weight.shape[2]
    top = routes.shape[1]
    experts = 16
    capacity = max(2, tokens * top * 4 // (3 * experts))
    pages, page, entry = prefix_pool.shape
    groups, depth = prompt_cache.shape[:2]
    half = residual.shape[1]
    model = out_weight.shape[1]
    units = down_weight.shape[1]
    own_rows = pages * page + tokens
    bf16, f32 = jnp.bfloat16, jnp.float32
    dma = pltpu.SemaphoreType.DMA
    vmem = pl.BlockSpec(memory_space=pltpu.VMEM)
    smem = pl.BlockSpec(memory_space=pltpu.SMEM)
    anywhere = pl.BlockSpec(memory_space=pl.ANY)
    attention_part, expert_part = pl.pallas_call(
        layer_kernel,
        out_shape=(jax.ShapeDtypeStruct((tokens, half), f32),) * 2,
        in_specs=[smem] * 4 + [vmem] * 4 + [anywhere] * 10,
        out_specs=(anywhere, vmem),
        scratch_shapes=[
            pltpu.VMEM((count, width, tokens), bf16),
            pltpu.VMEM((tokens, half), bf16),
            pltpu.VMEM((entry, tokens), bf16),
            pltpu.VMEM((own_rows + depth * 16, entry), bf16),
            pltpu.VMEM((count, nope, rank), bf16),
            pltpu.VMEM((count, rank, size), bf16),
            pltpu.VMEM((count * size, model), bf16),
            pltpu.VMEM((groups, depth * 16, entry), bf16),
            pltpu.VMEM((count * tokens, entry), bf16),
            pltpu.VMEM((count * tokens, 1), f32),
            pltpu.VMEM((count * tokens, 1), f32),
            pltpu.VMEM((count * tokens, rank), f32),
            pltpu.VMEM((1, pages * page + depth * 16), f32),
            pltpu.VMEM((tokens, count * size), bf16),
            pltpu.VMEM((16, 1, tokens), f32),
            pltpu.VMEM((16, 1, tokens), f32),
            pltpu.VMEM((tokens, half), f32),
            pltpu.VMEM((16, tokens, model), bf16),
            pltpu.VMEM((tokens, half), bf16),
            pltpu.VMEM((tokens, half), bf16),
            pltpu.VMEM((1, tokens), f32),
            pltpu.VMEM((1, tokens), f32),
            pltpu.VMEM((2, 1, half), f32),
            pltpu.VMEM((16, tokens), f32),
            pltpu.VMEM((16, tokens), f32),
            pltpu.VMEM((16, 1, tokens), f32),
            pltpu.VMEM((2, 16, capacity, tokens), bf16),
            pltpu.VMEM((4 * capacity, 128), f32),
            pltpu.VMEM((units, model), bf16),
            pltpu.VMEM((units, model), bf16),
            pltpu.VMEM((units, model), bf16),
            pltpu.VMEM((4 * capacity, model), bf16),
            pltpu.VMEM((4 * capacity, units), bf16),
            pltpu.VMEM((4, 4, capacity, model), bf16),
            pltpu.VMEM((4, 2, capacity, model), bf16),
            pltpu.VMEM((4, 2, tokens, model), bf16),
            pltpu.VMEM((4, tokens // 2, half), bf16),
            pltpu.VMEM((4, tokens // 2, half), bf16),
            pltpu.VMEM((4, tokens, half), bf16),
            pltpu.VMEM((4, tokens, half), bf16),
            pltpu.VMEM((4, tokens, half), bf16),
            dma((16,)),
            dma((16,)),
            dma((16,)),
            dma((16,)),
            dma((2,)),
            dma((2, 5)),
            dma((11,)),
            dma((2, 16)),
            dma((5, 32)),
            dma((2, 32)),
            dma((2, 9, 4)),
        ],
        compiler_params=pltpu.CompilerParams(
            collective_id=0, has_side_effects=True, vmem_limit_bytes=60 << 20
        ),
    )(
        page_table, prefix_len, prompt_len, group_ids,
        routes.T, route_weight.T, norm_gain.reshape(-1, 128), prompt_cache, residual,
        jnp.transpose(queries, (1, 2, 0)), stretch_cache.T, prefix_pool.reshape(pages * page, entry),
        absorb_weight, value_weight, out_weight,
        jnp.swapaxes(gate_weight[0], 0, 1), jnp.swapaxes(up_weight[0], 0, 1), down_weight[0],
    )
    attended = (residual.astype(f32) + attention_part).astype(bf16)
    return attended, (attended.astype(f32) + expert_part).astype(bf16)


def solution(mesh):
    in_specs = (
        P("req", "tp", None),
        P("req", None),
        P("req", None, None),
        P("req", None),
        P(),
        P(None, "req", None),
        P(),
        P(),
        P("tp", None, None),
        P("tp", None, None),
        P("tp", None),
        P("req", "tp"),
        P("tp"),
        P("req", None),
        P("req", None),
        P("req", None, "tp"),
        P("req", None, "tp"),
        P("req", "tp", None),
    )
    out_specs = (P("req", "tp"), P("req", "tp"))
    body = on_block if mesh.shape["req"] == 16 and mesh.shape["tp"] == 2 else on_device
    return jax.shard_map(
        body, mesh=mesh, in_specs=in_specs, out_specs=out_specs, check_vma=False
    )
```

```python
import math

import jax
import jax.numpy as jnp
from jax import lax
from jax.experimental import pallas as pl
from jax.experimental.pallas import tpu as pltpu
from jax.sharding import PartitionSpec as P

NEGATIVE = -1e30
EPSILON = 1e-06


def on_device(
    queries, stretch_cache, prefix_pool, page_table, prefix_len, prompt_cache, prompt_len,
    group_ids, absorb_weight, value_weight, out_weight, residual, norm_gain, routes,
    route_weight, gate_weight, up_weight, down_weight,
):
    tokens = queries.shape[0]
    prompts = lax.all_gather(prompt_cache, "req", axis=1, tiled=True)
    projected = attend(
        queries, stretch_cache, prefix_pool, page_table, prefix_len, prompts, prompt_len,
        group_ids, absorb_weight, value_weight, out_weight,
    )
    attention_part = lax.psum_scatter(
        projected.astype(jnp.bfloat16), "tp", scatter_dimension=1, tiled=True
    ).astype(jnp.float32)
    attended = (residual.astype(jnp.float32) + attention_part).astype(jnp.bfloat16)
    stream = attended.astype(jnp.float32)
    squares = lax.psum(jnp.sum(stream * stream, axis=1), "tp")
    model_width = out_weight.shape[1]
    normed = (
        stream * lax.rsqrt(squares / model_width + EPSILON)[:, None] * norm_gain.astype(jnp.float32)
    ).astype(jnp.bfloat16)
    experts = lax.axis_size("req")
    top = routes.shape[1]
    capacity = max(2, tokens * top * 4 // (3 * experts))
    choice = routes[:, :, None] == jnp.arange(experts, dtype=jnp.int32)[None, None, :]
    share = jnp.sum(jnp.where(choice, route_weight[:, :, None], 0.0), axis=1).T
    named = share > 0.0
    before = jnp.arange(tokens)[:, None] <= jnp.arange(tokens)[None, :]
    slot = jnp.dot(
        named.astype(jnp.bfloat16), before.astype(jnp.bfloat16), preferred_element_type=jnp.float32
    ).astype(jnp.int32) - 1
    picks = (
        slot[:, None, :] == jnp.arange(capacity, dtype=jnp.int32)[None, :, None]
    ) & named[:, None, :]
    chooser = picks.astype(jnp.bfloat16).reshape(experts * capacity, tokens)
    level = jnp.sum(jnp.where(picks, share[:, None, :], 0.0), axis=2)
    whole = lax.all_gather(normed, "tp", axis=1, tiled=True)
    buffer = (
        jnp.dot(chooser, whole, preferred_element_type=jnp.float32)
        .astype(jnp.bfloat16)
        .reshape(experts, capacity, -1)
    )
    received = lax.all_to_all(buffer, "req", split_axis=0, concat_axis=0, tiled=True)
    gate = jnp.einsum("snd,df->snf", received, gate_weight[0], preferred_element_type=jnp.float32)
    up = jnp.einsum("snd,df->snf", received, up_weight[0], preferred_element_type=jnp.float32)
    hidden = (jax.nn.silu(gate) * up).astype(jnp.bfloat16)
    part_out = jnp.einsum(
        "snf,fd->snd", hidden, down_weight[0], preferred_element_type=jnp.float32
    ).astype(jnp.bfloat16)
    returned = lax.all_to_all(part_out, "req", split_axis=0, concat_axis=0, tiled=True)
    weighted = (returned.astype(jnp.float32) * level[:, :, None]).astype(jnp.bfloat16)
    combined = lax.dot_general(
        chooser, weighted.reshape(experts * capacity, -1), (((0,), (0,)), ((), ())),
        preferred_element_type=jnp.float32,
    )
    expert_part = lax.psum_scatter(
        combined.astype(jnp.bfloat16), "tp", scatter_dimension=1, tiled=True
    ).astype(jnp.float32)
    mixed = (stream + expert_part).astype(jnp.bfloat16)
    return (attended, mixed)


def attend(
    queries, stretch_cache, prefix_pool, page_table, prefix_len, prompts, prompt_len,
    group_ids, absorb_weight, value_weight, out_weight,
):
    tokens, heads, width = queries.shape
    nope, rank = absorb_weight.shape[1], value_weight.shape[1]
    me = lax.axis_index("req")
    requests = jnp.arange(group_ids.shape[0], dtype=jnp.int32) == me
    group = jnp.sum(jnp.where(requests, group_ids, 0))
    own_length = jnp.sum(jnp.where(requests, prefix_len, 0))
    prompt_length = jnp.where(group == 0, prompt_len[0], prompt_len[1])
    pages, page = prefix_pool.shape[:2]
    order = jnp.arange(pages, dtype=jnp.int32)
    logical = jnp.sum(
        jnp.where(page_table[0][None, :] == order[:, None], order[None, :], 0), axis=1
    )
    prefix_at = (logical[:, None] * page + jnp.arange(page, dtype=jnp.int32)[None, :]).reshape(-1)
    prompt = jnp.where(group == 0, prompts[0], prompts[1])
    keys = jnp.concatenate(
        [stretch_cache, prompt, prefix_pool.reshape(pages * page, -1)], axis=0
    )
    seen = jnp.concatenate(
        [jnp.arange(prompt.shape[0]) < prompt_length, prefix_at < own_length]
    )
    token = jnp.arange(tokens)
    visible = jnp.concatenate(
        [
            token[None, :] <= token[:, None],
            jnp.broadcast_to(seen[None, :], (tokens, seen.shape[0])),
        ],
        axis=1,
    )
    turned = jnp.transpose(queries, (1, 0, 2))
    absorbed = jnp.concatenate(
        [
            jnp.einsum(
                "htn,hnr->htr", turned[:, :, :nope], absorb_weight,
                preferred_element_type=jnp.float32,
            ).astype(jnp.bfloat16),
            turned[:, :, nope:],
        ],
        axis=2,
    )
    scores = jnp.einsum("htc,kc->htk", absorbed, keys, preferred_element_type=jnp.float32)
    scores = jnp.where(visible[None], scores * width ** (-0.5), NEGATIVE)
    weights = jnp.exp(scores - jnp.max(scores, axis=2, keepdims=True))
    weights = jnp.where(visible[None], weights, 0.0)
    totals = jnp.sum(weights, axis=2, keepdims=True)
    latent = jnp.einsum(
        "htk,kr->htr", weights.astype(jnp.bfloat16), keys[:, :rank],
        preferred_element_type=jnp.float32,
    )
    latent = (latent / totals).astype(jnp.bfloat16)
    heads_out = jnp.einsum(
        "htr,hrv->thv", latent, value_weight, preferred_element_type=jnp.float32
    ).astype(jnp.bfloat16)
    return jnp.dot(
        heads_out.reshape(tokens, -1), out_weight, preferred_element_type=jnp.float32
    )


MESH = pl.DeviceIdType.MESH


def coordinates():
    me = lax.axis_index("req")
    return me // 4, (me // 2) % 2, me % 2, lax.axis_index("tp")


def place(z, x, core, y):
    return {"req": (z * 2 + x) * 2 + core, "tp": y}


def greet():
    z, x, core, y = coordinates()
    me = lax.axis_index("req")
    barrier = pltpu.get_barrier_semaphore()
    for step in range(1, 16):
        pl.semaphore_signal(
            barrier, inc=1, device_id={"req": (me + step) % 16, "tp": y}, device_id_type=MESH
        )
    pl.semaphore_signal(barrier, inc=1, device_id=place(z, x, core, 1 - y), device_id_type=MESH)
    pl.semaphore_wait(barrier, 16)


def plane_at(place_in_turn):
    z = coordinates()[0]
    high = z // 2
    near = z + high * (3 - 2 * z)
    late = place_in_turn // 2
    odd = place_in_turn % 2
    first = (1 - odd) * (1 - late) * near + odd * (1 - late) * (1 - near) + late * place_in_turn
    return first + high * (3 - 2 * first)


def spread_tokens(whole, send, recv, mid_send, mid_recv):
    z, x, core, y = coordinates()
    quarter = whole.shape[2] // 4

    def piece(zp, xp, yp, half, cp):
        return whole.at[
            (zp * 2 + xp) * 2 + cp,
            :,
            pl.ds(pl.multiple_of((yp * 2 + half) * quarter, quarter), quarter),
        ]

    def hop(zp, xp, yp, half, cp, kind, peer):
        slot = zp * 8 + xp * 4 + yp * 2 + half
        part = piece(zp, xp, yp, half, cp)
        return pltpu.make_async_remote_copy(
            part, part, send.at[kind, slot], recv.at[cp, slot], device_id=peer, device_id_type=MESH
        )

    def edge(zp, xp, yp, side, kind, peer):
        slot = zp * 8 + xp * 4 + yp * 2 + side
        narrow = quarter // 2
        part = whole.at[
            (zp * 2 + xp) * 2 + core,
            :,
            pl.ds(pl.multiple_of(yp * 2 * quarter + side * 3 * narrow, narrow), narrow),
        ]
        return pltpu.make_async_remote_copy(
            part, part, send.at[kind, slot], recv.at[core, slot], device_id=peer, device_id_type=MESH
        )

    def middle(zp, way, peer):
        narrow = quarter // 2
        part = whole.at[
            (zp * 2 + 1 - x) * 2 + core,
            :,
            pl.ds(pl.multiple_of((1 - y) * 2 * quarter + narrow, narrow), quarter),
        ]
        return pltpu.make_async_remote_copy(
            part, part, mid_send.at[way, zp], mid_recv.at[zp], device_id=peer, device_id_type=MESH
        )

    up, down = place(z + 1, x, core, y), place(z - 1, x, core, y)
    over_x, over_y, other = place(z, 1 - x, core, y), place(z, x, core, 1 - y), place(z, x, 1 - core, y)
    between = z * (3 - z)

    def pass_middle(zp, finish):
        @pl.when((zp <= z) & (z < 3))
        def _():
            copy = middle(zp, 0, up)
            copy.wait_send() if finish else copy.start()

        @pl.when((zp >= z) & (z > 0))
        def _():
            copy = middle(zp, 1, down)
            copy.wait_send() if finish else copy.start()

    def relay_middle(zp):
        @pl.when(between > 0)
        def _():
            middle(zp, 0, over_x).wait_recv()
            pass_middle(zp, False)

    def column(zp, finish, halves=(0, 1), ways=(True, True)):
        for half in halves if ways[0] else ():
            for go, kind, peer in (
                ((zp <= z) & (z < 3), 0, up), ((zp >= z) & (z > 0), 1, down)
            ):
                @pl.when(go)
                def _(kind=kind, peer=peer, half=half):
                    copy = hop(zp, x, y, half, core, kind, peer)
                    copy.wait_send() if finish else copy.start()
        for kind, peer, half in ((2, over_x, 0), (3, over_y, 1), (2, over_x, 1), (3, over_y, 0)):
            if half in halves and ways[1]:
                copy = hop(zp, x, y, half, core, kind, peer)
                copy.wait_send() if finish else copy.start()
        for half in halves if ways[1] else ():
            copy = hop(zp, x, y, half, core, 4, other)
            copy.wait_send() if finish else copy.start()

    def forward(zp):
        @pl.when(between > 0)
        def _():
            for half in range(2):
                hop(zp, x, y, half, core, 0, over_x).wait_recv()
                column(zp, False, (half,), (True, False))

    def arrive(zp):
        @pl.when(between == 0)
        def _():
            for half in range(2):
                hop(zp, x, y, half, core, 0, over_x).wait_recv()

        column(zp, False, (0, 1), (False, True))

    def beside(zp, finish, own):
        if not finish:
            for half in range(2):
                hop(zp, 1 - x, y, half, core, 2, over_x).wait_recv()
                hop(zp, x, 1 - y, half, core, 3, over_y).wait_recv()
        if own:
            copies = [hop(zp, 1 - x, y, 0, core, 3, over_y), hop(zp, x, 1 - y, 1, core, 2, over_x)]
        else:
            copies = [edge(zp, 1 - x, y, 0, 3, over_y), edge(zp, x, 1 - y, 1, 2, over_x)]
        for half in range(2):
            copies.append(hop(zp, 1 - x, y, half, core, 4, other))
            copies.append(hop(zp, x, 1 - y, half, core, 4, other))
        for copy in copies:
            copy.wait_send() if finish else copy.start()

    def diagonal(zp, finish):
        if not finish:
            @pl.when(zp == z)
            def _():
                for half in range(2):
                    hop(zp, 1 - x, 1 - y, half, core, 2, over_x).wait_recv()
                pass_middle(zp, False)

            @pl.when(zp != z)
            def _():
                for side in range(2):
                    edge(zp, 1 - x, 1 - y, side, 2, over_x).wait_recv()

            @pl.when((zp != z) & (between == 0))
            def _():
                middle(zp, 0, over_x).wait_recv()

        for half in range(2):
            copy = hop(zp, 1 - x, 1 - y, half, core, 4, other)
            copy.wait_send() if finish else copy.start()

    def complete(zp):
        for xp in range(2):
            for yp in range(2):
                for half in range(2):
                    hop(zp, xp, yp, half, 1 - core, 4, other).wait_recv()

    def close(zp):
        column(zp, True)

        @pl.when(zp == z)
        def _():
            beside(zp, True, True)

        @pl.when(zp != z)
        def _():
            beside(zp, True, False)

        diagonal(zp, True)
        pass_middle(zp, True)

    return column, forward, arrive, beside, relay_middle, diagonal, complete, close


def return_sums(parts, part_in, chooser, acc, x_diag, y_diag, x_in, y_in, z_in, sems):
    z, x, core, y = coordinates()
    rows, half_cols = acc.shape[2], acc.shape[3] // 2
    half_rows = rows // 2
    over_x, over_y, other = place(z, 1 - x, core, y), place(z, x, core, 1 - y), place(z, x, 1 - core, y)
    mine = pl.ds(pl.multiple_of(y * half_cols, half_cols), half_cols)
    theirs = pl.ds(pl.multiple_of((1 - y) * half_cols, half_cols), half_cols)
    top, low = pl.ds(0, half_rows), pl.ds(half_rows, half_rows)

    def copy(source, target, kind, zp, peer):
        return pltpu.make_async_remote_copy(
            source, target, sems.at[0, kind, zp], sems.at[1, kind, zp],
            device_id=peer, device_id_type=MESH,
        )

    def core_copy(zp, xp):
        return copy(parts.at[zp, xp * 2 + 1 - core], part_in.at[zp, xp], xp, zp, other)

    def diag_copies(zp):
        far = acc.at[zp, 1 - x]
        return (
            copy(far.at[top, theirs], y_diag.at[zp], 2, zp, over_y),
            copy(far.at[low, theirs], x_diag.at[zp], 3, zp, over_x),
        )

    def free_copies(zp):
        return (
            copy(acc.at[zp, 1 - x].at[low, mine], x_in.at[zp, low], 4, zp, over_x),
            copy(acc.at[zp, x].at[top, theirs], y_in.at[zp, top], 5, zp, over_y),
        )

    def last_copies(zp):
        return (
            copy(acc.at[zp, 1 - x].at[top, mine], x_in.at[zp, top], 6, zp, over_x),
            copy(acc.at[zp, x].at[low, theirs], y_in.at[zp, low], 7, zp, over_y),
        )

    def plane_copy(zp):
        return pltpu.make_async_remote_copy(
            acc.at[zp, x].at[:, mine], z_in.at[z], sems.at[0, 8, zp], sems.at[1, 8, z],
            device_id=place(zp, x, core, y), device_id_type=MESH,
        )

    def plane_arrival(zp):
        return pltpu.make_async_remote_copy(
            acc.at[zp, x].at[:, mine], z_in.at[zp], sems.at[0, 8, zp], sems.at[1, 8, zp],
            device_id=place(zp, x, core, y), device_id_type=MESH,
        )

    def add(target, *terms):
        total = target[...].astype(jnp.float32)
        for term in terms:
            total = total + term[...].astype(jnp.float32)
        target[...] = total.astype(target.dtype)

    def cores(zp):
        down = (((0,), (0,)), ((), ()))
        for xp in range(2):
            core_copy(zp, xp).wait_recv()
            request = (zp * 2 + xp) * 2 + core
            total = lax.dot_general(
                chooser[0, request], parts[zp, xp * 2 + core], down,
                preferred_element_type=jnp.float32,
            ) + lax.dot_general(
                chooser[1, request], part_in[zp, xp], down, preferred_element_type=jnp.float32
            )
            acc[zp, xp] = total.astype(jnp.bfloat16)
        for item in diag_copies(zp) + free_copies(zp):
            item.start()

    def corners(zp):
        from_y, from_x = diag_copies(zp)
        over_x_copy, over_y_copy = last_copies(zp)
        from_y.wait_recv()
        add(acc.at[zp, 1 - x].at[top, mine], y_diag.at[zp])
        over_x_copy.start()
        from_x.wait_recv()
        add(acc.at[zp, x].at[low, theirs], x_diag.at[zp])
        over_y_copy.start()

    def arrivals(zp):
        for item in free_copies(zp) + last_copies(zp):
            item.wait_recv()

    def columns(zp):
        arrivals(zp)
        add(acc.at[zp, x].at[:, mine], x_in.at[zp], y_in.at[zp])
        plane_copy(zp).start()

    def final(result):
        arrivals(z)
        total = acc[z, x, :, mine].astype(jnp.float32)
        total = total + x_in[z].astype(jnp.float32) + y_in[z].astype(jnp.float32)
        for turn in range(1, 4):
            zp = plane_at(turn)
            plane_arrival(zp).wait_recv()
            total = total + z_in[zp].astype(jnp.float32)
        result[...] = total

    def close(zp):
        for xp in range(2):
            core_copy(zp, xp).wait_send()
        for item in diag_copies(zp) + free_copies(zp) + last_copies(zp):
            item.wait_send()

        @pl.when(zp != z)
        def _():
            plane_copy(zp).wait_send()

    return core_copy, cores, corners, columns, final, close


def choose(mine, chooser, which):
    requests, tokens = mine.shape
    capacity = chooser.shape[2]
    named = jnp.where(mine[...] > 0.0, 1.0, 0.0)
    rows = lax.broadcasted_iota(jnp.int32, (tokens, tokens), 0)
    columns = lax.broadcasted_iota(jnp.int32, (tokens, tokens), 1)
    before = jnp.where(rows <= columns, 1.0, 0.0).astype(jnp.bfloat16)
    slot = jnp.dot(named.astype(jnp.bfloat16), before, preferred_element_type=jnp.float32)
    wanted = jnp.where(named > 0.0, slot - 1.0, -1.0).astype(jnp.int32)
    places = lax.broadcasted_iota(jnp.int32, (capacity, tokens), 0)
    for request in range(requests):
        picks = jnp.where(wanted[request : request + 1, :] == places, 1.0, 0.0)
        chooser[which, request] = picks.astype(jnp.bfloat16)


def share_prompts(block_ref, share_ref, keys_ref, mine_ref, send, recv, send_w, recv_w, local):
    me = lax.axis_index("req")
    y = lax.axis_index("tp")
    depth = block_ref.shape[1]
    rows = pl.ds(pl.multiple_of(me * depth, depth), depth)
    core, other = me % 2, me + 1 - 2 * (me % 2)

    def block(source):
        return keys_ref.at[:, pl.ds(pl.multiple_of(source * depth, depth), depth), :]

    def shares(step):
        peer = (me + step) % 16
        return pltpu.make_async_remote_copy(
            share_ref.at[peer], mine_ref.at[me], send_w.at[step], recv_w.at[step],
            device_id={"req": peer, "tp": y}, device_id_type=MESH,
        )

    def direct(step):
        return pltpu.make_async_remote_copy(
            block_ref, keys_ref.at[:, rows, :], send.at[step], recv.at[step],
            device_id={"req": (me + 2 * step) % 16, "tp": y}, device_id_type=MESH,
        )

    def across(source, index):
        return pltpu.make_async_remote_copy(
            block(source), block(source), send.at[index], recv.at[index],
            device_id={"req": other, "tp": y}, device_id_type=MESH,
        )

    home = pltpu.make_async_remote_copy(
        block_ref, keys_ref.at[:, rows, :], send.at[8 + me // 2], recv.at[8 + me // 2],
        device_id={"req": other, "tp": y}, device_id_type=MESH,
    )
    own = pltpu.make_async_copy(block_ref, keys_ref.at[:, rows, :], local.at[0])
    own_share = pltpu.make_async_copy(share_ref.at[me], mine_ref.at[me], local.at[1])

    def start():
        for step in range(1, 8):
            direct(step).start()
        home.start()
        own.start()
        own_share.start()

        def send_share(step, carry):
            shares(step).start()
            return carry

        lax.fori_loop(1, 16, send_share, 0)

    def relay(step):
        source = (me + 2 * step) % 16
        across(source, 8 - step).wait_recv()
        across(source, 8 + source // 2).start()

    def finish():
        own.wait()
        for step in range(8):
            source = (me + 2 * step) % 16 + 1 - 2 * core
            across(source, 8 + source // 2).wait_recv()

    def finish_shares():
        own_share.wait()

        def wait_share(step, carry):
            shares(step).wait_recv()
            return carry

        lax.fori_loop(1, 16, wait_share, 0)

    def close():
        home.wait_send()
        for step in range(1, 8):
            direct(step).wait_send()
            source = (me + 2 * step) % 16
            across(source, 8 + source // 2).wait_send()

        def close_share(step, carry):
            shares(step).wait_send()
            return carry

        lax.fori_loop(1, 16, close_share, 0)

    return start, relay, finish, finish_shares, close


def layer_kernel(
    page_table, prefix_len, prompt_len, group_ids,
    routes, route_weight, gain, prompt_block,
    residual_hbm, query_hbm, stretch_hbm, pool_hbm, absorb_hbm, value_hbm, out_hbm, gate_hbm, up_hbm, down_hbm,
    attention_part, expert_part,
    query, residual, stretch, keys, absorb, value, out_w, prompts, absorbed, bests, totals, latents, bias,
    heads,
    share, share_in, projected,
    whole, outgoing, incoming, squares_out, squares_in, gains, mine_share, other_share, roots,
    chooser, level,
    gate_w, up_w, down_w, rows, hidden, parts, part_in, acc, x_diag, y_diag, x_in, y_in, z_in,
    prompt_send, prompt_recv, share_send, share_recv, local_sems,
    pair_sems, load_sems, root_sems, send, recv, mid_send, mid_recv, sems,
):
    z, x, core, y = coordinates()
    me = lax.axis_index("req")
    tokens, half_cols = residual.shape
    quarter = half_cols // 2
    count, nope, rank = absorb.shape
    width = query.shape[1]
    pool_rows = pool_hbm.shape[0]
    own_rows = pool_rows + tokens
    loads = [
        pltpu.make_async_copy(source, target, load_sems.at[index])
        for index, (source, target) in enumerate(
            (
                (query_hbm, query), (absorb_hbm, absorb), (stretch_hbm, stretch),
                (pool_hbm, keys.at[pl.ds(0, pool_rows)]), (value_hbm, value), (out_hbm, out_w),
                (gate_hbm, gate_w), (up_hbm, up_w), (down_hbm, down_w), (residual_hbm, residual),
            )
        )
    ]
    for load in loads:
        load.start()
    mine = pl.ds(pl.multiple_of(y * half_cols, half_cols), half_cols)
    theirs = pl.ds(pl.multiple_of((1 - y) * half_cols, half_cols), half_cols)
    over_y, other = place(z, x, core, 1 - y), place(z, x, 1 - core, y)

    def pair(source, target, index, peer=over_y):
        return pltpu.make_async_remote_copy(
            source, target, pair_sems.at[0, index], pair_sems.at[1, index],
            device_id=peer, device_id_type=MESH,
        )

    def swap(half):
        span = pl.ds(half * quarter, quarter)
        return pair(outgoing.at[:, span], incoming.at[:, span], half)

    squares = pair(squares_out, squares_in, 2)
    gain_copy = pair(gains.at[y], gains.at[y], 3)
    share_copy = pair(mine_share, other_share, 4, other)
    start_prompts, relay, finish_prompts, finish_shares, close_prompts = share_prompts(
        prompt_block, share, prompts, share_in, prompt_send, prompt_recv, share_send, share_recv,
        local_sems,
    )
    expert_of = lax.broadcasted_iota(jnp.int32, (16, tokens), 0)
    given = jnp.zeros((16, tokens), jnp.float32)
    for choice in range(routes.shape[0]):
        hit = routes[choice : choice + 1, :] == expert_of
        given = given + jnp.where(hit, route_weight[choice : choice + 1, :], 0.0)
    for expert in range(16):
        share[expert] = given[expert : expert + 1, :]
    for row in range(gain.shape[0]):
        gains[y, :, pl.ds(row * gain.shape[1], gain.shape[1])] = gain[row : row + 1, :].astype(
            jnp.float32
        )
    greet()
    start_prompts()
    gain_copy.start()
    group = group_ids[me]
    page = pool_rows // page_table.shape[1]
    lane = lax.broadcasted_iota(jnp.int32, (1, pool_rows), 1)
    logical = jnp.zeros((1, pool_rows), jnp.int32)
    for index in range(page_table.shape[1]):
        logical = jnp.where(lane // page == page_table[0, index], index, logical)
    prefix_at = logical * page + lane % page
    bias[:, pl.ds(0, pool_rows)] = jnp.where(prefix_at < prefix_len[me], 0.0, NEGATIVE)
    prompt_rows = prompts.shape[1]
    prompt_lane = lax.broadcasted_iota(jnp.int32, (1, prompt_rows), 1)
    bias[:, pl.ds(pool_rows, prompt_rows)] = jnp.where(prompt_lane < prompt_len[group], 0.0, NEGATIVE)
    loads[2].wait()
    keys[pl.ds(pool_rows, tokens), :] = stretch[...].T
    for index in (0, 1, 3):
        loads[index].wait()
    first = (((0,), (0,)), ((), ()))
    across = (((1,), (1,)), ((), ()))

    factor = width ** (-0.5) * math.log2(math.e)

    batch = count // 2
    deep = batch * tokens

    def own_keys(index, carry):
        lines = pl.ds(pl.multiple_of(index * deep, deep), deep)
        for turn in range(batch):
            head = index * batch + turn
            own = pl.ds(pl.multiple_of(head * tokens, tokens), tokens)
            wide = lax.dot_general(
                query[head, pl.ds(0, nope), :], absorb[head], first,
                preferred_element_type=jnp.float32,
            )
            absorbed[own, pl.ds(0, rank)] = wide.astype(jnp.bfloat16)
            absorbed[own, pl.ds(rank, width - nope)] = query[head, pl.ds(nope, width - nope), :].T
        found = lax.dot_general(
            absorbed[lines, :], keys[pl.ds(0, own_rows), :], across,
            preferred_element_type=jnp.float32,
        )
        token = lax.rem(lax.broadcasted_iota(jnp.int32, (deep, tokens), 0), tokens)
        later = lax.broadcasted_iota(jnp.int32, (deep, tokens), 1) > token
        found = jnp.concatenate(
            [
                found[:, :pool_rows] + bias[:, pl.ds(0, pool_rows)],
                jnp.where(later, NEGATIVE, found[:, pool_rows:]),
            ],
            axis=1,
        )
        best = jnp.max(found, axis=1, keepdims=True)
        weights = jnp.exp2((found - best) * factor)
        bests[lines, :] = best
        totals[lines, :] = jnp.sum(weights, axis=1, keepdims=True)
        latents[lines, :] = jnp.dot(
            weights.astype(jnp.bfloat16), keys[pl.ds(0, own_rows), pl.ds(0, rank)],
            preferred_element_type=jnp.float32,
        )

        @pl.when(index == 0)
        def _():
            for step in range(1, 8):
                relay(step)

        return carry

    lax.fori_loop(0, 2, own_keys, 0)
    finish_prompts()
    keys[pl.ds(own_rows, prompt_rows), :] = prompts[group]
    loads[4].wait()
    loads[9].wait()
    size = value.shape[2]

    def prompt_keys(index, carry):
        lines = pl.ds(pl.multiple_of(index * deep, deep), deep)
        found = lax.dot_general(
            absorbed[lines, :], keys[pl.ds(own_rows, prompt_rows), :], across,
            preferred_element_type=jnp.float32,
        ) + bias[:, pl.ds(pool_rows, prompt_rows)]
        held = bests[lines, :]
        best = jnp.maximum(jnp.max(found, axis=1, keepdims=True), held)
        keep = jnp.exp2((held - best) * factor)
        weights = jnp.exp2((found - best) * factor)
        total = totals[lines, :] * keep + jnp.sum(weights, axis=1, keepdims=True)
        latent = latents[lines, :] * keep + jnp.dot(
            weights.astype(jnp.bfloat16), keys[pl.ds(own_rows, prompt_rows), pl.ds(0, rank)],
            preferred_element_type=jnp.float32,
        )
        latent = (latent * (1.0 / total)).astype(jnp.bfloat16)
        for turn in range(batch):
            head = index * batch + turn
            heads[:, pl.ds(pl.multiple_of(head * size, size), size)] = jnp.dot(
                latent[turn * tokens : (turn + 1) * tokens], value[head],
                preferred_element_type=jnp.float32,
            ).astype(jnp.bfloat16)
        return carry

    lax.fori_loop(0, 2, prompt_keys, 0)
    loads[5].wait()
    for half in range(2):
        across_cols = pl.ds(
            pl.multiple_of((1 - y) * half_cols + half * quarter, quarter), quarter
        )
        outgoing[:, pl.ds(half * quarter, quarter)] = jnp.dot(
            heads[...], out_w[:, across_cols], preferred_element_type=jnp.float32
        ).astype(jnp.bfloat16)
        swap(half).start()
    for half in range(2):
        own_cols = pl.ds(pl.multiple_of(y * half_cols + half * quarter, quarter), quarter)
        projected[:, pl.ds(half * quarter, quarter)] = jnp.dot(
            heads[...], out_w[:, own_cols], preferred_element_type=jnp.float32
        )
    finish_shares()
    for request in range(16):
        mine_share[request : request + 1, :] = share_in[request]
    share_copy.start()
    choose(mine_share, chooser, 0)
    (
        column, forward, arrive, beside, relay_middle, diagonal, complete, close_spread,
    ) = spread_tokens(
        whole, send, recv, mid_send, mid_recv
    )
    sums = jnp.zeros((tokens, 1), jnp.float32)
    for half in range(2):
        span = pl.ds(half * quarter, quarter)
        swap(half).wait_recv()
        added = projected[:, span] + incoming[:, span].astype(jnp.float32)
        projected[:, span] = added
        rounded = (residual[:, span].astype(jnp.float32) + added).astype(jnp.bfloat16)
        whole[me, :, pl.ds(pl.multiple_of(y * half_cols + half * quarter, quarter), quarter)] = rounded
        stream = rounded.astype(jnp.float32)
        sums = sums + jnp.sum(stream * stream, axis=1, keepdims=True)
        if half == 1:
            diag = lax.broadcasted_iota(jnp.int32, (tokens, tokens), 1) == (
                lax.broadcasted_iota(jnp.int32, (tokens, tokens), 0)
            )
            squares_out[...] = jnp.sum(jnp.where(diag, sums, 0.0), axis=0, keepdims=True)
            squares.start()
        column(z, False, (half,))
    part_out = pltpu.make_async_copy(projected, attention_part, load_sems.at[10])
    part_out.start()
    share_copy.wait_recv()
    choose(other_share, chooser, 1)

    def root_copy(step):
        peer = (me + step) % 16
        return pltpu.make_async_remote_copy(
            roots.at[me], roots.at[me], root_sems.at[0, peer], root_sems.at[1, me],
            device_id={"req": peer, "tp": y}, device_id_type=MESH,
        )

    def root_arrival(request):
        return pltpu.make_async_remote_copy(
            roots.at[request], roots.at[request], root_sems.at[0, request],
            root_sems.at[1, request], device_id=over_y, device_id_type=MESH,
        )

    forward(plane_at(1))
    arrive(plane_at(1))
    forward(plane_at(2))
    beside(z, False, True)
    squares.wait_recv()
    roots[me] = lax.rsqrt((squares_out[...] + squares_in[...]) / (2 * half_cols) + EPSILON)

    def send_root(step, carry):
        root_copy(step).start()
        return carry

    lax.fori_loop(1, 16, send_root, 0)
    gain_copy.wait_recv()
    for load in loads[6:9]:
        load.wait()
    capacity = chooser.shape[2]
    core_copy, cores, corners, columns, final, close_return = return_sums(
        parts, part_in, chooser, acc, x_diag, y_diag, x_in, y_in, z_in, sems
    )

    def compute(zp):
        for index in range(4):
            request = zp * 4 + index

            @pl.when(request != me)
            def _(request=request):
                root_arrival(request).wait_recv()

        for index in range(4):
            request = zp * 4 + index
            lines = pl.ds(index * capacity, capacity)
            picks = chooser[0, request]
            picked = jnp.dot(picks, whole[request], preferred_element_type=jnp.float32)
            wide = picks.astype(jnp.float32)
            picked = picked * jnp.sum(wide * roots[request], axis=1, keepdims=True)
            shared = jnp.sum(wide * share_in[request], axis=1, keepdims=True)
            level[lines, :] = jnp.broadcast_to(shared, (capacity, level.shape[1]))
            for side in range(2):
                span = pl.ds(side * half_cols, half_cols)
                scaled = picked[:, side * half_cols : (side + 1) * half_cols] * gains[side]
                rows[lines, span] = scaled.astype(jnp.bfloat16)
        gate = lax.dot_general(rows[...], gate_w[...], across, preferred_element_type=jnp.float32)
        up = lax.dot_general(rows[...], up_w[...], across, preferred_element_type=jnp.float32)
        hidden[...] = (gate / (1.0 + jnp.exp(-gate)) * up * level[:, :1]).astype(jnp.bfloat16)
        part = jnp.dot(hidden[...], down_w[...], preferred_element_type=jnp.float32)
        for index in range(4):
            parts[zp, index] = part[index * capacity : (index + 1) * capacity].astype(jnp.bfloat16)
        for xp in range(2):
            core_copy(zp, xp).start()

    def step(turn, carry):
        @pl.when(turn < 3)
        def _():
            arrive(plane_at(turn + 1))

        @pl.when(turn == 1)
        def _():
            forward(plane_at(3))

        @pl.when(turn == 2)
        def _():
            relay_middle(plane_at(1))
            relay_middle(plane_at(2))

        @pl.when(turn < 4)
        def _():
            beside(plane_at(turn), False, False)

        @pl.when(turn == 2)
        def _():
            relay_middle(plane_at(3))

        @pl.when(turn >= 5)
        def _():
            columns(plane_at(turn - 4))

        @pl.when(turn >= 4)
        def _():
            corners(plane_at((turn - 3) % 4))

        @pl.when((turn >= 3) & (turn < 7))
        def _():
            cores(plane_at((turn - 2) % 4))

        @pl.when(turn < 5)
        def _():
            zp = plane_at(turn - 1)
            diagonal(zp, False)
            complete(zp)
            compute(zp)

        return carry

    lax.fori_loop(1, 8, step, 0)
    final(expert_part)

    def close(zp, carry):
        close_spread(zp)
        close_return(zp)
        return carry

    lax.fori_loop(0, 4, close, 0)

    def close_root(step, carry):
        root_copy(step).wait_send()
        return carry

    lax.fori_loop(1, 16, close_root, 0)
    for item in (swap(0), swap(1), squares, gain_copy, share_copy):
        item.wait_send()
    close_prompts()
    part_out.wait()


def on_block(
    queries, stretch_cache, prefix_pool, page_table, prefix_len, prompt_cache, prompt_len,
    group_ids, absorb_weight, value_weight, out_weight, residual, norm_gain, routes,
    route_weight, gate_weight, up_weight, down_weight,
):
    tokens, count, width = queries.shape
    nope, rank = absorb_weight.shape[1:]
    size = value_weight.shape[2]
    top = routes.shape[1]
    experts = 16
    capacity = max(2, tokens * top * 4 // (3 * experts))
    pages, page, entry = prefix_pool.shape
    groups, depth = prompt_cache.shape[:2]
    half = residual.shape[1]
    model = out_weight.shape[1]
    units = down_weight.shape[1]
    own_rows = pages * page + tokens
    bf16, f32 = jnp.bfloat16, jnp.float32
    dma = pltpu.SemaphoreType.DMA
    vmem = pl.BlockSpec(memory_space=pltpu.VMEM)
    smem = pl.BlockSpec(memory_space=pltpu.SMEM)
    anywhere = pl.BlockSpec(memory_space=pl.ANY)
    attention_part, expert_part = pl.pallas_call(
        layer_kernel,
        out_shape=(jax.ShapeDtypeStruct((tokens, half), f32),) * 2,
        in_specs=[smem] * 4 + [vmem] * 4 + [anywhere] * 10,
        out_specs=(anywhere, vmem),
        scratch_shapes=[
            pltpu.VMEM((count, width, tokens), bf16),
            pltpu.VMEM((tokens, half), bf16),
            pltpu.VMEM((entry, tokens), bf16),
            pltpu.VMEM((own_rows + depth * 16, entry), bf16),
            pltpu.VMEM((count, nope, rank), bf16),
            pltpu.VMEM((count, rank, size), bf16),
            pltpu.VMEM((count * size, model), bf16),
            pltpu.VMEM((groups, depth * 16, entry), bf16),
            pltpu.VMEM((count * tokens, entry), bf16),
            pltpu.VMEM((count * tokens, 1), f32),
            pltpu.VMEM((count * tokens, 1), f32),
            pltpu.VMEM((count * tokens, rank), f32),
            pltpu.VMEM((1, pages * page + depth * 16), f32),
            pltpu.VMEM((tokens, count * size), bf16),
            pltpu.VMEM((16, 1, tokens), f32),
            pltpu.VMEM((16, 1, tokens), f32),
            pltpu.VMEM((tokens, half), f32),
            pltpu.VMEM((16, tokens, model), bf16),
            pltpu.VMEM((tokens, half), bf16),
            pltpu.VMEM((tokens, half), bf16),
            pltpu.VMEM((1, tokens), f32),
            pltpu.VMEM((1, tokens), f32),
            pltpu.VMEM((2, 1, half), f32),
            pltpu.VMEM((16, tokens), f32),
            pltpu.VMEM((16, tokens), f32),
            pltpu.VMEM((16, 1, tokens), f32),
            pltpu.VMEM((2, 16, capacity, tokens), bf16),
            pltpu.VMEM((4 * capacity, 128), f32),
            pltpu.VMEM((units, model), bf16),
            pltpu.VMEM((units, model), bf16),
            pltpu.VMEM((units, model), bf16),
            pltpu.VMEM((4 * capacity, model), bf16),
            pltpu.VMEM((4 * capacity, units), bf16),
            pltpu.VMEM((4, 4, capacity, model), bf16),
            pltpu.VMEM((4, 2, capacity, model), bf16),
            pltpu.VMEM((4, 2, tokens, model), bf16),
            pltpu.VMEM((4, tokens // 2, half), bf16),
            pltpu.VMEM((4, tokens // 2, half), bf16),
            pltpu.VMEM((4, tokens, half), bf16),
            pltpu.VMEM((4, tokens, half), bf16),
            pltpu.VMEM((4, tokens, half), bf16),
            dma((16,)),
            dma((16,)),
            dma((16,)),
            dma((16,)),
            dma((2,)),
            dma((2, 5)),
            dma((11,)),
            dma((2, 16)),
            dma((5, 32)),
            dma((2, 32)),
            dma((2, 4)),
            dma((4,)),
            dma((2, 9, 4)),
        ],
        compiler_params=pltpu.CompilerParams(
            collective_id=0, has_side_effects=True, vmem_limit_bytes=60 << 20
        ),
    )(
        page_table, prefix_len, prompt_len, group_ids,
        routes.T, route_weight.T, norm_gain.reshape(-1, 128), prompt_cache, residual,
        jnp.transpose(queries, (1, 2, 0)), stretch_cache.T, prefix_pool.reshape(pages * page, entry),
        absorb_weight, value_weight, out_weight,
        jnp.swapaxes(gate_weight[0], 0, 1), jnp.swapaxes(up_weight[0], 0, 1), down_weight[0],
    )
    attended = (residual.astype(f32) + attention_part).astype(bf16)
    return attended, (attended.astype(f32) + expert_part).astype(bf16)


def solution(mesh):
    in_specs = (
        P("req", "tp", None),
        P("req", None),
        P("req", None, None),
        P("req", None),
        P(),
        P(None, "req", None),
        P(),
        P(),
        P("tp", None, None),
        P("tp", None, None),
        P("tp", None),
        P("req", "tp"),
        P("tp"),
        P("req", None),
        P("req", None),
        P("req", None, "tp"),
        P("req", None, "tp"),
        P("req", "tp", None),
    )
    out_specs = (P("req", "tp"), P("req", "tp"))
    body = on_block if mesh.shape["req"] == 16 and mesh.shape["tp"] == 2 else on_device
    return jax.shard_map(
        body, mesh=mesh, in_specs=in_specs, out_specs=out_specs, check_vma=False
    )
```

```python
import math

import jax
import jax.numpy as jnp
from jax import lax
from jax.experimental import pallas as pl
from jax.experimental.pallas import tpu as pltpu
from jax.sharding import PartitionSpec as P

NEGATIVE = -1e30
EPSILON = 1e-06


def on_device(
    queries, stretch_cache, prefix_pool, page_table, prefix_len, prompt_cache, prompt_len,
    group_ids, absorb_weight, value_weight, out_weight, residual, norm_gain, routes,
    route_weight, gate_weight, up_weight, down_weight,
):
    tokens = queries.shape[0]
    prompts = lax.all_gather(prompt_cache, "req", axis=1, tiled=True)
    projected = attend(
        queries, stretch_cache, prefix_pool, page_table, prefix_len, prompts, prompt_len,
        group_ids, absorb_weight, value_weight, out_weight,
    )
    attention_part = lax.psum_scatter(
        projected.astype(jnp.bfloat16), "tp", scatter_dimension=1, tiled=True
    ).astype(jnp.float32)
    attended = (residual.astype(jnp.float32) + attention_part).astype(jnp.bfloat16)
    stream = attended.astype(jnp.float32)
    squares = lax.psum(jnp.sum(stream * stream, axis=1), "tp")
    model_width = out_weight.shape[1]
    normed = (
        stream * lax.rsqrt(squares / model_width + EPSILON)[:, None] * norm_gain.astype(jnp.float32)
    ).astype(jnp.bfloat16)
    experts = lax.axis_size("req")
    top = routes.shape[1]
    capacity = max(2, tokens * top * 4 // (3 * experts))
    choice = routes[:, :, None] == jnp.arange(experts, dtype=jnp.int32)[None, None, :]
    share = jnp.sum(jnp.where(choice, route_weight[:, :, None], 0.0), axis=1).T
    named = share > 0.0
    before = jnp.arange(tokens)[:, None] <= jnp.arange(tokens)[None, :]
    slot = jnp.dot(
        named.astype(jnp.bfloat16), before.astype(jnp.bfloat16), preferred_element_type=jnp.float32
    ).astype(jnp.int32) - 1
    picks = (
        slot[:, None, :] == jnp.arange(capacity, dtype=jnp.int32)[None, :, None]
    ) & named[:, None, :]
    chooser = picks.astype(jnp.bfloat16).reshape(experts * capacity, tokens)
    level = jnp.sum(jnp.where(picks, share[:, None, :], 0.0), axis=2)
    whole = lax.all_gather(normed, "tp", axis=1, tiled=True)
    buffer = (
        jnp.dot(chooser, whole, preferred_element_type=jnp.float32)
        .astype(jnp.bfloat16)
        .reshape(experts, capacity, -1)
    )
    received = lax.all_to_all(buffer, "req", split_axis=0, concat_axis=0, tiled=True)
    gate = jnp.einsum("snd,df->snf", received, gate_weight[0], preferred_element_type=jnp.float32)
    up = jnp.einsum("snd,df->snf", received, up_weight[0], preferred_element_type=jnp.float32)
    hidden = (jax.nn.silu(gate) * up).astype(jnp.bfloat16)
    part_out = jnp.einsum(
        "snf,fd->snd", hidden, down_weight[0], preferred_element_type=jnp.float32
    ).astype(jnp.bfloat16)
    returned = lax.all_to_all(part_out, "req", split_axis=0, concat_axis=0, tiled=True)
    weighted = (returned.astype(jnp.float32) * level[:, :, None]).astype(jnp.bfloat16)
    combined = lax.dot_general(
        chooser, weighted.reshape(experts * capacity, -1), (((0,), (0,)), ((), ())),
        preferred_element_type=jnp.float32,
    )
    expert_part = lax.psum_scatter(
        combined.astype(jnp.bfloat16), "tp", scatter_dimension=1, tiled=True
    ).astype(jnp.float32)
    mixed = (stream + expert_part).astype(jnp.bfloat16)
    return (attended, mixed)


def attend(
    queries, stretch_cache, prefix_pool, page_table, prefix_len, prompts, prompt_len,
    group_ids, absorb_weight, value_weight, out_weight,
):
    tokens, heads, width = queries.shape
    nope, rank = absorb_weight.shape[1], value_weight.shape[1]
    me = lax.axis_index("req")
    requests = jnp.arange(group_ids.shape[0], dtype=jnp.int32) == me
    group = jnp.sum(jnp.where(requests, group_ids, 0))
    own_length = jnp.sum(jnp.where(requests, prefix_len, 0))
    prompt_length = jnp.where(group == 0, prompt_len[0], prompt_len[1])
    pages, page = prefix_pool.shape[:2]
    order = jnp.arange(pages, dtype=jnp.int32)
    logical = jnp.sum(
        jnp.where(page_table[0][None, :] == order[:, None], order[None, :], 0), axis=1
    )
    prefix_at = (logical[:, None] * page + jnp.arange(page, dtype=jnp.int32)[None, :]).reshape(-1)
    prompt = jnp.where(group == 0, prompts[0], prompts[1])
    keys = jnp.concatenate(
        [stretch_cache, prompt, prefix_pool.reshape(pages * page, -1)], axis=0
    )
    seen = jnp.concatenate(
        [jnp.arange(prompt.shape[0]) < prompt_length, prefix_at < own_length]
    )
    token = jnp.arange(tokens)
    visible = jnp.concatenate(
        [
            token[None, :] <= token[:, None],
            jnp.broadcast_to(seen[None, :], (tokens, seen.shape[0])),
        ],
        axis=1,
    )
    turned = jnp.transpose(queries, (1, 0, 2))
    absorbed = jnp.concatenate(
        [
            jnp.einsum(
                "htn,hnr->htr", turned[:, :, :nope], absorb_weight,
                preferred_element_type=jnp.float32,
            ).astype(jnp.bfloat16),
            turned[:, :, nope:],
        ],
        axis=2,
    )
    scores = jnp.einsum("htc,kc->htk", absorbed, keys, preferred_element_type=jnp.float32)
    scores = jnp.where(visible[None], scores * width ** (-0.5), NEGATIVE)
    weights = jnp.exp(scores - jnp.max(scores, axis=2, keepdims=True))
    weights = jnp.where(visible[None], weights, 0.0)
    totals = jnp.sum(weights, axis=2, keepdims=True)
    latent = jnp.einsum(
        "htk,kr->htr", weights.astype(jnp.bfloat16), keys[:, :rank],
        preferred_element_type=jnp.float32,
    )
    latent = (latent / totals).astype(jnp.bfloat16)
    heads_out = jnp.einsum(
        "htr,hrv->thv", latent, value_weight, preferred_element_type=jnp.float32
    ).astype(jnp.bfloat16)
    return jnp.dot(
        heads_out.reshape(tokens, -1), out_weight, preferred_element_type=jnp.float32
    )


MESH = pl.DeviceIdType.MESH


def coordinates():
    me = lax.axis_index("req")
    return me // 4, (me // 2) % 2, me % 2, lax.axis_index("tp")


def place(z, x, core, y):
    return {"req": (z * 2 + x) * 2 + core, "tp": y}


def greet():
    z, x, core, y = coordinates()
    me = lax.axis_index("req")
    barrier = pltpu.get_barrier_semaphore()
    for step in range(1, 16):
        pl.semaphore_signal(
            barrier, inc=1, device_id={"req": (me + step) % 16, "tp": y}, device_id_type=MESH
        )
    pl.semaphore_signal(barrier, inc=1, device_id=place(z, x, core, 1 - y), device_id_type=MESH)
    pl.semaphore_wait(barrier, 16)


def plane_at(place_in_turn):
    z = coordinates()[0]
    high = z // 2
    near = z + high * (3 - 2 * z)
    late = place_in_turn // 2
    odd = place_in_turn % 2
    first = (1 - odd) * (1 - late) * near + odd * (1 - late) * (1 - near) + late * place_in_turn
    return first + high * (3 - 2 * first)


def spread_tokens(whole, send, recv, mid_send, mid_recv):
    z, x, core, y = coordinates()
    quarter = whole.shape[2] // 4

    def piece(zp, xp, yp, half, cp):
        return whole.at[
            (zp * 2 + xp) * 2 + cp,
            :,
            pl.ds(pl.multiple_of((yp * 2 + half) * quarter, quarter), quarter),
        ]

    def hop(zp, xp, yp, half, cp, kind, peer):
        slot = zp * 8 + xp * 4 + yp * 2 + half
        part = piece(zp, xp, yp, half, cp)
        return pltpu.make_async_remote_copy(
            part, part, send.at[kind, slot], recv.at[cp, slot], device_id=peer, device_id_type=MESH
        )

    def edge(zp, xp, yp, side, kind, peer):
        slot = zp * 8 + xp * 4 + yp * 2 + side
        narrow = quarter // 2
        part = whole.at[
            (zp * 2 + xp) * 2 + core,
            :,
            pl.ds(pl.multiple_of(yp * 2 * quarter + side * 3 * narrow, narrow), narrow),
        ]
        return pltpu.make_async_remote_copy(
            part, part, send.at[kind, slot], recv.at[core, slot], device_id=peer, device_id_type=MESH
        )

    def middle(zp, way, peer):
        narrow = quarter // 2
        part = whole.at[
            (zp * 2 + 1 - x) * 2 + core,
            :,
            pl.ds(pl.multiple_of((1 - y) * 2 * quarter + narrow, narrow), quarter),
        ]
        return pltpu.make_async_remote_copy(
            part, part, mid_send.at[way, zp], mid_recv.at[zp], device_id=peer, device_id_type=MESH
        )

    up, down = place(z + 1, x, core, y), place(z - 1, x, core, y)
    over_x, over_y, other = place(z, 1 - x, core, y), place(z, x, core, 1 - y), place(z, x, 1 - core, y)
    between = z * (3 - z)

    def pass_middle(zp, finish):
        @pl.when((zp <= z) & (z < 3))
        def _():
            copy = middle(zp, 0, up)
            copy.wait_send() if finish else copy.start()

        @pl.when((zp >= z) & (z > 0))
        def _():
            copy = middle(zp, 1, down)
            copy.wait_send() if finish else copy.start()

    def relay_middle(zp):
        @pl.when(between > 0)
        def _():
            middle(zp, 0, over_x).wait_recv()
            pass_middle(zp, False)

    def column(zp, finish, halves=(0, 1), ways=(True, True)):
        for half in halves if ways[0] else ():
            for go, kind, peer in (
                ((zp <= z) & (z < 3), 0, up), ((zp >= z) & (z > 0), 1, down)
            ):
                @pl.when(go)
                def _(kind=kind, peer=peer, half=half):
                    copy = hop(zp, x, y, half, core, kind, peer)
                    copy.wait_send() if finish else copy.start()
        for kind, peer, half in ((2, over_x, 0), (3, over_y, 1), (2, over_x, 1), (3, over_y, 0)):
            if half in halves and ways[1]:
                copy = hop(zp, x, y, half, core, kind, peer)
                copy.wait_send() if finish else copy.start()
        for half in halves if ways[1] else ():
            copy = hop(zp, x, y, half, core, 4, other)
            copy.wait_send() if finish else copy.start()

    def forward(zp):
        @pl.when(between > 0)
        def _():
            for half in range(2):
                hop(zp, x, y, half, core, 0, over_x).wait_recv()
                column(zp, False, (half,), (True, False))

    def arrive(zp):
        @pl.when(between == 0)
        def _():
            for half in range(2):
                hop(zp, x, y, half, core, 0, over_x).wait_recv()

        column(zp, False, (0, 1), (False, True))

    def beside(zp, finish, own):
        if not finish:
            for half in range(2):
                hop(zp, 1 - x, y, half, core, 2, over_x).wait_recv()
                hop(zp, x, 1 - y, half, core, 3, over_y).wait_recv()
        if own:
            copies = [hop(zp, 1 - x, y, 0, core, 3, over_y), hop(zp, x, 1 - y, 1, core, 2, over_x)]
        else:
            copies = [edge(zp, 1 - x, y, 0, 3, over_y), edge(zp, x, 1 - y, 1, 2, over_x)]
        for half in range(2):
            copies.append(hop(zp, 1 - x, y, half, core, 4, other))
            copies.append(hop(zp, x, 1 - y, half, core, 4, other))
        for copy in copies:
            copy.wait_send() if finish else copy.start()

    def diagonal(zp, finish):
        if not finish:
            @pl.when(zp == z)
            def _():
                for half in range(2):
                    hop(zp, 1 - x, 1 - y, half, core, 2, over_x).wait_recv()
                pass_middle(zp, False)

            @pl.when(zp != z)
            def _():
                for side in range(2):
                    edge(zp, 1 - x, 1 - y, side, 2, over_x).wait_recv()

            @pl.when((zp != z) & (between == 0))
            def _():
                middle(zp, 0, over_x).wait_recv()

        for half in range(2):
            copy = hop(zp, 1 - x, 1 - y, half, core, 4, other)
            copy.wait_send() if finish else copy.start()

    def complete(zp):
        for xp in range(2):
            for yp in range(2):
                for half in range(2):
                    hop(zp, xp, yp, half, 1 - core, 4, other).wait_recv()

    def close(zp):
        column(zp, True)

        @pl.when(zp == z)
        def _():
            beside(zp, True, True)

        @pl.when(zp != z)
        def _():
            beside(zp, True, False)

        diagonal(zp, True)
        pass_middle(zp, True)

    return column, forward, arrive, beside, relay_middle, diagonal, complete, close


def return_sums(
    parts, part_in, chooser, acc, x_diag, y_diag, x_in, y_in, z_in, mid_in, center_in, sems, mid_sems,
    center_sems,
):
    z, x, core, y = coordinates()
    rows, half_cols = acc.shape[2], acc.shape[3] // 2
    half_rows = rows // 2
    over_x, over_y, other = place(z, 1 - x, core, y), place(z, x, core, 1 - y), place(z, x, 1 - core, y)
    mine = pl.ds(pl.multiple_of(y * half_cols, half_cols), half_cols)
    theirs = pl.ds(pl.multiple_of((1 - y) * half_cols, half_cols), half_cols)

    def copy(source, target, kind, zp, peer):
        return pltpu.make_async_remote_copy(
            source, target, sems.at[0, kind, zp], sems.at[1, kind, zp],
            device_id=peer, device_id_type=MESH,
        )

    def core_copy(zp, xp):
        return copy(parts.at[zp, xp * 2 + 1 - core], part_in.at[zp, xp], xp, zp, other)

    def split(own):
        return half_rows if own else half_rows // 2

    def diag_copies(zp, own):
        far, edge = acc.at[zp, 1 - x], split(own)
        over, under = pl.ds(0, edge), pl.ds(rows - edge, edge)
        return (
            copy(far.at[over, theirs], y_diag.at[zp, over], 2, zp, over_y),
            copy(far.at[under, theirs], x_diag.at[zp, over], 3, zp, over_x),
        )

    def free_copies(zp, own):
        edge = split(own)
        after, ahead = pl.ds(edge, rows - edge), pl.ds(0, rows - edge)
        return (
            copy(acc.at[zp, 1 - x].at[after, mine], x_in.at[zp, after], 4, zp, over_x),
            copy(acc.at[zp, x].at[ahead, theirs], y_in.at[zp, ahead], 5, zp, over_y),
        )

    def last_copies(zp, own):
        edge = split(own)
        over, under = pl.ds(0, edge), pl.ds(rows - edge, edge)
        return (
            copy(acc.at[zp, 1 - x].at[over, mine], x_in.at[zp, over], 6, zp, over_x),
            copy(acc.at[zp, x].at[under, theirs], y_in.at[zp, under], 7, zp, over_y),
        )

    center = pl.ds(half_rows // 2, half_rows)

    def center_copy(zp):
        return pltpu.make_async_remote_copy(
            acc.at[zp, 1 - x].at[center, theirs], center_in.at[z],
            center_sems.at[0, zp], center_sems.at[1, z],
            device_id=place(zp, x, core, y), device_id_type=MESH,
        )

    def center_arrival(zp):
        return pltpu.make_async_remote_copy(
            acc.at[zp, 1 - x].at[center, theirs], center_in.at[zp],
            center_sems.at[0, zp], center_sems.at[1, zp],
            device_id=place(near, x, core, y), device_id_type=MESH,
        )

    def plane_copy(zp):
        return pltpu.make_async_remote_copy(
            acc.at[zp, x].at[:, mine], z_in.at[z], sems.at[0, 8, zp], sems.at[1, 8, z],
            device_id=place(zp, x, core, y), device_id_type=MESH,
        )

    between = z * (3 - z)
    near = plane_at(1)

    def plane_arrival(zp):
        return pltpu.make_async_remote_copy(
            acc.at[zp, x].at[:, mine], z_in.at[zp], sems.at[0, 8, zp], sems.at[1, 8, zp],
            device_id=place(near, x, core, y), device_id_type=MESH,
        )

    def gather_copy(zp, half):
        lines = pl.ds(half * half_rows, half_rows)
        return pltpu.make_async_remote_copy(
            acc.at[zp, x].at[lines, mine], mid_in.at[zp, lines],
            mid_sems.at[0, half, zp], mid_sems.at[1, half, zp],
            device_id=place(near, x, core, y), device_id_type=MESH,
        )

    def joint_copy(zp, half):
        lines = pl.ds(half * half_rows, half_rows)
        return pltpu.make_async_remote_copy(
            acc.at[zp, x].at[lines, mine], z_in.at[z, lines],
            mid_sems.at[2, half, zp], mid_sems.at[3, half, z],
            device_id=place(zp, x, core, y), device_id_type=MESH,
        )

    def joint_arrival(zp, half):
        lines = pl.ds(half * half_rows, half_rows)
        return pltpu.make_async_remote_copy(
            acc.at[zp, x].at[lines, mine], z_in.at[zp, lines],
            mid_sems.at[2, half, zp], mid_sems.at[3, half, zp],
            device_id=place(near, x, core, y), device_id_type=MESH,
        )

    def add(target, *terms):
        total = target[...].astype(jnp.float32)
        for term in terms:
            total = total + term[...].astype(jnp.float32)
        target[...] = total.astype(target.dtype)

    def cores(zp, own):
        down = (((0,), (0,)), ((), ()))
        for xp in range(2):
            core_copy(zp, xp).wait_recv()
            request = (zp * 2 + xp) * 2 + core
            total = lax.dot_general(
                chooser[0, request], parts[zp, xp * 2 + core], down,
                preferred_element_type=jnp.float32,
            ) + lax.dot_general(
                chooser[1, request], part_in[zp, xp], down, preferred_element_type=jnp.float32
            )
            acc[zp, xp] = total.astype(jnp.bfloat16)
        if own:
            for item in free_copies(zp, own):
                item.start()
            others = [plane_at(turn) for turn in range(1, 4)]
            for source in others:
                center_arrival(source).wait_recv()
            add(
                acc.at[zp, 1 - x].at[center, theirs],
                *[center_in.at[source] for source in others],
            )
            for item in diag_copies(zp, own):
                item.start()
        else:
            for item in diag_copies(zp, own) + free_copies(zp, own):
                item.start()
            center_copy(zp).start()

    def corners(zp, own):
        edge = split(own)
        over, under = pl.ds(0, edge), pl.ds(rows - edge, edge)
        from_y, from_x = diag_copies(zp, own)
        over_x_copy, over_y_copy = last_copies(zp, own)
        from_y.wait_recv()
        add(acc.at[zp, 1 - x].at[over, mine], y_diag.at[zp, over])
        over_x_copy.start()
        from_x.wait_recv()
        add(acc.at[zp, x].at[under, theirs], x_diag.at[zp, over])
        over_y_copy.start()

    def arrivals(zp, own):
        for item in free_copies(zp, own) + last_copies(zp, own):
            item.wait_recv()

    def columns(zp):
        arrivals(zp, False)
        add(acc.at[zp, x].at[:, mine], x_in.at[zp], y_in.at[zp])

        @pl.when(zp == near)
        def _():
            plane_copy(zp).start()

        @pl.when((zp != near) & (between == 0))
        def _():
            for half in range(2):
                gather_copy(zp, half).start()

    def joints(zp):
        @pl.when(between > 0)
        def _():
            for half in range(2):
                lines = pl.ds(half * half_rows, half_rows)
                gather_copy(zp, half).wait_recv()
                add(acc.at[zp, x].at[lines, mine], mid_in.at[zp, lines])
                joint_copy(zp, half).start()

    def final(result):
        arrivals(z, True)
        total = acc[z, x, :, mine].astype(jnp.float32)
        total = total + x_in[z].astype(jnp.float32) + y_in[z].astype(jnp.float32)
        plane_arrival(near).wait_recv()
        total = total + z_in[near].astype(jnp.float32)
        far = plane_at(2)
        for half in range(2):
            joint_arrival(far, half).wait_recv()
        result[...] = total + z_in[far].astype(jnp.float32)

    def close(zp):
        for xp in range(2):
            core_copy(zp, xp).wait_send()

        def sent(own):
            for item in diag_copies(zp, own) + free_copies(zp, own) + last_copies(zp, own):
                item.wait_send()
            if not own:
                center_copy(zp).wait_send()

        pl.when(zp == z)(lambda: sent(True))
        pl.when(zp != z)(lambda: sent(False))

        @pl.when(zp == near)
        def _():
            plane_copy(zp).wait_send()

        @pl.when((zp != near) & (zp != z) & (between == 0))
        def _():
            for half in range(2):
                gather_copy(zp, half).wait_send()

        @pl.when((zp != near) & (zp != z) & (between > 0))
        def _():
            for half in range(2):
                joint_copy(zp, half).wait_send()

    return core_copy, cores, corners, columns, joints, final, close


def choose(mine, chooser, which):
    requests, tokens = mine.shape
    capacity = chooser.shape[2]
    named = jnp.where(mine[...] > 0.0, 1.0, 0.0)
    rows = lax.broadcasted_iota(jnp.int32, (tokens, tokens), 0)
    columns = lax.broadcasted_iota(jnp.int32, (tokens, tokens), 1)
    before = jnp.where(rows <= columns, 1.0, 0.0).astype(jnp.bfloat16)
    slot = jnp.dot(named.astype(jnp.bfloat16), before, preferred_element_type=jnp.float32)
    wanted = jnp.where(named > 0.0, slot - 1.0, -1.0).astype(jnp.int32)
    places = lax.broadcasted_iota(jnp.int32, (capacity, tokens), 0)
    for request in range(requests):
        picks = jnp.where(wanted[request : request + 1, :] == places, 1.0, 0.0)
        chooser[which, request] = picks.astype(jnp.bfloat16)


def share_prompts(block_ref, share_ref, keys_ref, mine_ref, send, recv, send_w, recv_w, local):
    me = lax.axis_index("req")
    y = lax.axis_index("tp")
    depth = block_ref.shape[1]
    rows = pl.ds(pl.multiple_of(me * depth, depth), depth)
    core, other = me % 2, me + 1 - 2 * (me % 2)

    def block(source):
        return keys_ref.at[:, pl.ds(pl.multiple_of(source * depth, depth), depth), :]

    def shares(step):
        peer = (me + step) % 16
        return pltpu.make_async_remote_copy(
            share_ref.at[peer], mine_ref.at[me], send_w.at[step], recv_w.at[step],
            device_id={"req": peer, "tp": y}, device_id_type=MESH,
        )

    def direct(step):
        return pltpu.make_async_remote_copy(
            block_ref, keys_ref.at[:, rows, :], send.at[step], recv.at[step],
            device_id={"req": (me + 2 * step) % 16, "tp": y}, device_id_type=MESH,
        )

    def across(source, index):
        return pltpu.make_async_remote_copy(
            block(source), block(source), send.at[index], recv.at[index],
            device_id={"req": other, "tp": y}, device_id_type=MESH,
        )

    home = pltpu.make_async_remote_copy(
        block_ref, keys_ref.at[:, rows, :], send.at[8 + me // 2], recv.at[8 + me // 2],
        device_id={"req": other, "tp": y}, device_id_type=MESH,
    )
    own = pltpu.make_async_copy(block_ref, keys_ref.at[:, rows, :], local.at[0])
    own_share = pltpu.make_async_copy(share_ref.at[me], mine_ref.at[me], local.at[1])

    def start():
        for step in range(1, 8):
            direct(step).start()
        home.start()
        own.start()
        own_share.start()

        def send_share(step, carry):
            shares(step).start()
            return carry

        lax.fori_loop(1, 16, send_share, 0)

    def relay(step):
        source = (me + 2 * step) % 16
        across(source, 8 - step).wait_recv()
        across(source, 8 + source // 2).start()

    def finish():
        own.wait()
        for step in range(8):
            source = (me + 2 * step) % 16 + 1 - 2 * core
            across(source, 8 + source // 2).wait_recv()

    def finish_shares():
        own_share.wait()

        def wait_share(step, carry):
            shares(step).wait_recv()
            return carry

        lax.fori_loop(1, 16, wait_share, 0)

    def close():
        home.wait_send()
        for step in range(1, 8):
            direct(step).wait_send()
            source = (me + 2 * step) % 16
            across(source, 8 + source // 2).wait_send()

        def close_share(step, carry):
            shares(step).wait_send()
            return carry

        lax.fori_loop(1, 16, close_share, 0)

    return start, relay, finish, finish_shares, close


def layer_kernel(
    page_table, prefix_len, prompt_len, group_ids,
    routes, route_weight, gain, prompt_block,
    residual_hbm, query_hbm, stretch_hbm, pool_hbm, absorb_hbm, value_hbm, out_hbm, gate_hbm, up_hbm, down_hbm,
    attention_part, expert_part,
    query, residual, stretch, keys, absorb, value, out_w, prompts, absorbed, bests, totals, latents, bias,
    heads,
    share, share_in, projected,
    whole, outgoing, incoming, squares_out, squares_in, gains, mine_share, other_share, roots,
    chooser, level,
    gate_w, up_w, down_w, rows, hidden, parts, part_in, acc, x_diag, y_diag, x_in, y_in, z_in, mid_in,
    center_in, prompt_send, prompt_recv, share_send, share_recv, local_sems,
    pair_sems, load_sems, root_sems, send, recv, mid_send, mid_recv, sems, mid_sems, center_sems,
):
    z, x, core, y = coordinates()
    me = lax.axis_index("req")
    tokens, half_cols = residual.shape
    quarter = half_cols // 2
    count, nope, rank = absorb.shape
    width = query.shape[1]
    pool_rows = pool_hbm.shape[0]
    own_rows = pool_rows + tokens
    loads = [
        pltpu.make_async_copy(source, target, load_sems.at[index])
        for index, (source, target) in enumerate(
            (
                (query_hbm, query), (absorb_hbm, absorb), (stretch_hbm, stretch),
                (pool_hbm, keys.at[pl.ds(0, pool_rows)]), (value_hbm, value), (out_hbm, out_w),
                (gate_hbm, gate_w), (up_hbm, up_w), (down_hbm, down_w), (residual_hbm, residual),
            )
        )
    ]
    for load in loads:
        load.start()
    mine = pl.ds(pl.multiple_of(y * half_cols, half_cols), half_cols)
    theirs = pl.ds(pl.multiple_of((1 - y) * half_cols, half_cols), half_cols)
    over_y, other = place(z, x, core, 1 - y), place(z, x, 1 - core, y)

    def pair(source, target, index, peer=over_y):
        return pltpu.make_async_remote_copy(
            source, target, pair_sems.at[0, index], pair_sems.at[1, index],
            device_id=peer, device_id_type=MESH,
        )

    def swap(half):
        span = pl.ds(half * quarter, quarter)
        return pair(outgoing.at[:, span], incoming.at[:, span], half)

    squares = pair(squares_out, squares_in, 2)
    gain_copy = pair(gains.at[y], gains.at[y], 3)
    share_copy = pair(mine_share, other_share, 4, other)
    start_prompts, relay, finish_prompts, finish_shares, close_prompts = share_prompts(
        prompt_block, share, prompts, share_in, prompt_send, prompt_recv, share_send, share_recv,
        local_sems,
    )
    expert_of = lax.broadcasted_iota(jnp.int32, (16, tokens), 0)
    given = jnp.zeros((16, tokens), jnp.float32)
    for choice in range(routes.shape[0]):
        hit = routes[choice : choice + 1, :] == expert_of
        given = given + jnp.where(hit, route_weight[choice : choice + 1, :], 0.0)
    for expert in range(16):
        share[expert] = given[expert : expert + 1, :]
    for row in range(gain.shape[0]):
        gains[y, :, pl.ds(row * gain.shape[1], gain.shape[1])] = gain[row : row + 1, :].astype(
            jnp.float32
        )
    greet()
    start_prompts()
    gain_copy.start()
    group = group_ids[me]
    page = pool_rows // page_table.shape[1]
    lane = lax.broadcasted_iota(jnp.int32, (1, pool_rows), 1)
    logical = jnp.zeros((1, pool_rows), jnp.int32)
    for index in range(page_table.shape[1]):
        logical = jnp.where(lane // page == page_table[0, index], index, logical)
    prefix_at = logical * page + lane % page
    bias[:, pl.ds(0, pool_rows)] = jnp.where(prefix_at < prefix_len[me], 0.0, NEGATIVE)
    prompt_rows = prompts.shape[1]
    prompt_lane = lax.broadcasted_iota(jnp.int32, (1, prompt_rows), 1)
    bias[:, pl.ds(pool_rows, prompt_rows)] = jnp.where(prompt_lane < prompt_len[group], 0.0, NEGATIVE)
    loads[2].wait()
    keys[pl.ds(pool_rows, tokens), :] = stretch[...].T
    for index in (0, 1, 3):
        loads[index].wait()
    first = (((0,), (0,)), ((), ()))
    across = (((1,), (1,)), ((), ()))

    factor = width ** (-0.5) * math.log2(math.e)

    batch = count // 2
    deep = batch * tokens

    def own_keys(index, carry):
        lines = pl.ds(pl.multiple_of(index * deep, deep), deep)
        for turn in range(batch):
            head = index * batch + turn
            own = pl.ds(pl.multiple_of(head * tokens, tokens), tokens)
            wide = lax.dot_general(
                query[head, pl.ds(0, nope), :], absorb[head], first,
                preferred_element_type=jnp.float32,
            )
            absorbed[own, pl.ds(0, rank)] = wide.astype(jnp.bfloat16)
            absorbed[own, pl.ds(rank, width - nope)] = query[head, pl.ds(nope, width - nope), :].T
        found = lax.dot_general(
            absorbed[lines, :], keys[pl.ds(0, own_rows), :], across,
            preferred_element_type=jnp.float32,
        )
        token = lax.rem(lax.broadcasted_iota(jnp.int32, (deep, tokens), 0), tokens)
        later = lax.broadcasted_iota(jnp.int32, (deep, tokens), 1) > token
        found = jnp.concatenate(
            [
                found[:, :pool_rows] + bias[:, pl.ds(0, pool_rows)],
                jnp.where(later, NEGATIVE, found[:, pool_rows:]),
            ],
            axis=1,
        )
        best = jnp.max(found, axis=1, keepdims=True)
        weights = jnp.exp2((found - best) * factor)
        bests[lines, :] = best
        totals[lines, :] = jnp.sum(weights, axis=1, keepdims=True)
        latents[lines, :] = jnp.dot(
            weights.astype(jnp.bfloat16), keys[pl.ds(0, own_rows), pl.ds(0, rank)],
            preferred_element_type=jnp.float32,
        )

        @pl.when(index == 0)
        def _():
            for step in range(1, 8):
                relay(step)

        return carry

    lax.fori_loop(0, 2, own_keys, 0)
    finish_prompts()
    keys[pl.ds(own_rows, prompt_rows), :] = prompts[group]
    loads[4].wait()
    loads[9].wait()
    size = value.shape[2]

    def prompt_keys(index, carry):
        lines = pl.ds(pl.multiple_of(index * deep, deep), deep)
        found = lax.dot_general(
            absorbed[lines, :], keys[pl.ds(own_rows, prompt_rows), :], across,
            preferred_element_type=jnp.float32,
        ) + bias[:, pl.ds(pool_rows, prompt_rows)]
        held = bests[lines, :]
        best = jnp.maximum(jnp.max(found, axis=1, keepdims=True), held)
        keep = jnp.exp2((held - best) * factor)
        weights = jnp.exp2((found - best) * factor)
        total = totals[lines, :] * keep + jnp.sum(weights, axis=1, keepdims=True)
        latent = latents[lines, :] * keep + jnp.dot(
            weights.astype(jnp.bfloat16), keys[pl.ds(own_rows, prompt_rows), pl.ds(0, rank)],
            preferred_element_type=jnp.float32,
        )
        latent = (latent * (1.0 / total)).astype(jnp.bfloat16)
        for turn in range(batch):
            head = index * batch + turn
            heads[:, pl.ds(pl.multiple_of(head * size, size), size)] = jnp.dot(
                latent[turn * tokens : (turn + 1) * tokens], value[head],
                preferred_element_type=jnp.float32,
            ).astype(jnp.bfloat16)
        return carry

    lax.fori_loop(0, 2, prompt_keys, 0)
    loads[5].wait()
    for half in range(2):
        across_cols = pl.ds(
            pl.multiple_of((1 - y) * half_cols + half * quarter, quarter), quarter
        )
        outgoing[:, pl.ds(half * quarter, quarter)] = jnp.dot(
            heads[...], out_w[:, across_cols], preferred_element_type=jnp.float32
        ).astype(jnp.bfloat16)
        swap(half).start()
    for half in range(2):
        own_cols = pl.ds(pl.multiple_of(y * half_cols + half * quarter, quarter), quarter)
        projected[:, pl.ds(half * quarter, quarter)] = jnp.dot(
            heads[...], out_w[:, own_cols], preferred_element_type=jnp.float32
        )
    finish_shares()
    for request in range(16):
        mine_share[request : request + 1, :] = share_in[request]
    share_copy.start()
    choose(mine_share, chooser, 0)
    (
        column, forward, arrive, beside, relay_middle, diagonal, complete, close_spread,
    ) = spread_tokens(
        whole, send, recv, mid_send, mid_recv
    )
    sums = jnp.zeros((tokens, 1), jnp.float32)
    for half in range(2):
        span = pl.ds(half * quarter, quarter)
        swap(half).wait_recv()
        added = projected[:, span] + incoming[:, span].astype(jnp.float32)
        projected[:, span] = added
        rounded = (residual[:, span].astype(jnp.float32) + added).astype(jnp.bfloat16)
        whole[me, :, pl.ds(pl.multiple_of(y * half_cols + half * quarter, quarter), quarter)] = rounded
        stream = rounded.astype(jnp.float32)
        sums = sums + jnp.sum(stream * stream, axis=1, keepdims=True)
        if half == 1:
            diag = lax.broadcasted_iota(jnp.int32, (tokens, tokens), 1) == (
                lax.broadcasted_iota(jnp.int32, (tokens, tokens), 0)
            )
            squares_out[...] = jnp.sum(jnp.where(diag, sums, 0.0), axis=0, keepdims=True)
            squares.start()
        column(z, False, (half,))
    part_out = pltpu.make_async_copy(projected, attention_part, load_sems.at[10])
    part_out.start()
    share_copy.wait_recv()
    choose(other_share, chooser, 1)

    def root_copy(step):
        peer = (me + step) % 16
        return pltpu.make_async_remote_copy(
            roots.at[me], roots.at[me], root_sems.at[0, peer], root_sems.at[1, me],
            device_id={"req": peer, "tp": y}, device_id_type=MESH,
        )

    def root_arrival(request):
        return pltpu.make_async_remote_copy(
            roots.at[request], roots.at[request], root_sems.at[0, request],
            root_sems.at[1, request], device_id=over_y, device_id_type=MESH,
        )

    forward(plane_at(1))
    arrive(plane_at(1))
    forward(plane_at(2))
    beside(z, False, True)
    squares.wait_recv()
    roots[me] = lax.rsqrt((squares_out[...] + squares_in[...]) / (2 * half_cols) + EPSILON)

    def send_root(step, carry):
        root_copy(step).start()
        return carry

    lax.fori_loop(1, 16, send_root, 0)
    gain_copy.wait_recv()
    for load in loads[6:9]:
        load.wait()
    capacity = chooser.shape[2]
    core_copy, cores, corners, columns, joints, final, close_return = return_sums(
        parts, part_in, chooser, acc, x_diag, y_diag, x_in, y_in, z_in, mid_in, center_in, sems, mid_sems,
        center_sems,
    )

    def compute(zp):
        for index in range(4):
            request = zp * 4 + index

            @pl.when(request != me)
            def _(request=request):
                root_arrival(request).wait_recv()

        for index in range(4):
            request = zp * 4 + index
            lines = pl.ds(index * capacity, capacity)
            picks = chooser[0, request]
            picked = jnp.dot(picks, whole[request], preferred_element_type=jnp.float32)
            wide = picks.astype(jnp.float32)
            picked = picked * jnp.sum(wide * roots[request], axis=1, keepdims=True)
            shared = jnp.sum(wide * share_in[request], axis=1, keepdims=True)
            level[lines, :] = jnp.broadcast_to(shared, (capacity, level.shape[1]))
            for side in range(2):
                span = pl.ds(side * half_cols, half_cols)
                scaled = picked[:, side * half_cols : (side + 1) * half_cols] * gains[side]
                rows[lines, span] = scaled.astype(jnp.bfloat16)
        gate = lax.dot_general(rows[...], gate_w[...], across, preferred_element_type=jnp.float32)
        up = lax.dot_general(rows[...], up_w[...], across, preferred_element_type=jnp.float32)
        hidden[...] = (gate / (1.0 + jnp.exp(-gate)) * up * level[:, :1]).astype(jnp.bfloat16)
        part = jnp.dot(hidden[...], down_w[...], preferred_element_type=jnp.float32)
        for index in range(4):
            parts[zp, index] = part[index * capacity : (index + 1) * capacity].astype(jnp.bfloat16)
        for xp in range(2):
            core_copy(zp, xp).start()

    def step(turn, carry):
        @pl.when(turn < 3)
        def _():
            arrive(plane_at(turn + 1))

        @pl.when(turn == 1)
        def _():
            forward(plane_at(3))

        @pl.when(turn == 2)
        def _():
            relay_middle(plane_at(1))
            relay_middle(plane_at(2))

        @pl.when(turn < 4)
        def _():
            beside(plane_at(turn), False, False)

        @pl.when(turn == 2)
        def _():
            relay_middle(plane_at(3))

        @pl.when(turn >= 5)
        def _():
            columns(plane_at(turn - 4))

        @pl.when(turn == 7)
        def _():
            joints(plane_at(2))

        @pl.when((turn >= 4) & (turn < 7))
        def _():
            corners(plane_at(turn - 3), False)

        @pl.when((turn >= 3) & (turn < 6))
        def _():
            cores(plane_at(turn - 2), False)

        @pl.when(turn == 6)
        def _():
            cores(z, True)

        @pl.when(turn < 5)
        def _():
            zp = plane_at(turn - 1)
            diagonal(zp, False)
            complete(zp)
            compute(zp)

        return carry

    lax.fori_loop(1, 8, step, 0)
    corners(z, True)
    joints(plane_at(3))
    final(expert_part)

    def close(zp, carry):
        close_spread(zp)
        close_return(zp)
        return carry

    lax.fori_loop(0, 4, close, 0)

    def close_root(step, carry):
        root_copy(step).wait_send()
        return carry

    lax.fori_loop(1, 16, close_root, 0)
    for item in (swap(0), swap(1), squares, gain_copy, share_copy):
        item.wait_send()
    close_prompts()
    part_out.wait()


def on_block(
    queries, stretch_cache, prefix_pool, page_table, prefix_len, prompt_cache, prompt_len,
    group_ids, absorb_weight, value_weight, out_weight, residual, norm_gain, routes,
    route_weight, gate_weight, up_weight, down_weight,
):
    tokens, count, width = queries.shape
    nope, rank = absorb_weight.shape[1:]
    size = value_weight.shape[2]
    top = routes.shape[1]
    experts = 16
    capacity = max(2, tokens * top * 4 // (3 * experts))
    pages, page, entry = prefix_pool.shape
    groups, depth = prompt_cache.shape[:2]
    half = residual.shape[1]
    model = out_weight.shape[1]
    units = down_weight.shape[1]
    own_rows = pages * page + tokens
    bf16, f32 = jnp.bfloat16, jnp.float32
    dma = pltpu.SemaphoreType.DMA
    vmem = pl.BlockSpec(memory_space=pltpu.VMEM)
    smem = pl.BlockSpec(memory_space=pltpu.SMEM)
    anywhere = pl.BlockSpec(memory_space=pl.ANY)
    attention_part, expert_part = pl.pallas_call(
        layer_kernel,
        out_shape=(jax.ShapeDtypeStruct((tokens, half), f32),) * 2,
        in_specs=[smem] * 4 + [vmem] * 4 + [anywhere] * 10,
        out_specs=(anywhere, vmem),
        scratch_shapes=[
            pltpu.VMEM((count, width, tokens), bf16),
            pltpu.VMEM((tokens, half), bf16),
            pltpu.VMEM((entry, tokens), bf16),
            pltpu.VMEM((own_rows + depth * 16, entry), bf16),
            pltpu.VMEM((count, nope, rank), bf16),
            pltpu.VMEM((count, rank, size), bf16),
            pltpu.VMEM((count * size, model), bf16),
            pltpu.VMEM((groups, depth * 16, entry), bf16),
            pltpu.VMEM((count * tokens, entry), bf16),
            pltpu.VMEM((count * tokens, 1), f32),
            pltpu.VMEM((count * tokens, 1), f32),
            pltpu.VMEM((count * tokens, rank), f32),
            pltpu.VMEM((1, pages * page + depth * 16), f32),
            pltpu.VMEM((tokens, count * size), bf16),
            pltpu.VMEM((16, 1, tokens), f32),
            pltpu.VMEM((16, 1, tokens), f32),
            pltpu.VMEM((tokens, half), f32),
            pltpu.VMEM((16, tokens, model), bf16),
            pltpu.VMEM((tokens, half), bf16),
            pltpu.VMEM((tokens, half), bf16),
            pltpu.VMEM((1, tokens), f32),
            pltpu.VMEM((1, tokens), f32),
            pltpu.VMEM((2, 1, half), f32),
            pltpu.VMEM((16, tokens), f32),
            pltpu.VMEM((16, tokens), f32),
            pltpu.VMEM((16, 1, tokens), f32),
            pltpu.VMEM((2, 16, capacity, tokens), bf16),
            pltpu.VMEM((4 * capacity, 128), f32),
            pltpu.VMEM((units, model), bf16),
            pltpu.VMEM((units, model), bf16),
            pltpu.VMEM((units, model), bf16),
            pltpu.VMEM((4 * capacity, model), bf16),
            pltpu.VMEM((4 * capacity, units), bf16),
            pltpu.VMEM((4, 4, capacity, model), bf16),
            pltpu.VMEM((4, 2, capacity, model), bf16),
            pltpu.VMEM((4, 2, tokens, model), bf16),
            pltpu.VMEM((4, tokens // 2, half), bf16),
            pltpu.VMEM((4, tokens // 2, half), bf16),
            pltpu.VMEM((4, tokens, half), bf16),
            pltpu.VMEM((4, tokens, half), bf16),
            pltpu.VMEM((4, tokens, half), bf16),
            pltpu.VMEM((4, tokens, half), bf16),
            pltpu.VMEM((4, tokens // 2, half), bf16),
            dma((16,)),
            dma((16,)),
            dma((16,)),
            dma((16,)),
            dma((2,)),
            dma((2, 5)),
            dma((11,)),
            dma((2, 16)),
            dma((5, 32)),
            dma((2, 32)),
            dma((2, 4)),
            dma((4,)),
            dma((2, 9, 4)),
            dma((4, 2, 4)),
            dma((2, 4)),
        ],
        compiler_params=pltpu.CompilerParams(
            collective_id=0, has_side_effects=True, vmem_limit_bytes=60 << 20
        ),
    )(
        page_table, prefix_len, prompt_len, group_ids,
        routes.T, route_weight.T, norm_gain.reshape(-1, 128), prompt_cache, residual,
        jnp.transpose(queries, (1, 2, 0)), stretch_cache.T, prefix_pool.reshape(pages * page, entry),
        absorb_weight, value_weight, out_weight,
        jnp.swapaxes(gate_weight[0], 0, 1), jnp.swapaxes(up_weight[0], 0, 1), down_weight[0],
    )
    attended = (residual.astype(f32) + attention_part).astype(bf16)
    return attended, (attended.astype(f32) + expert_part).astype(bf16)


def solution(mesh):
    in_specs = (
        P("req", "tp", None),
        P("req", None),
        P("req", None, None),
        P("req", None),
        P(),
        P(None, "req", None),
        P(),
        P(),
        P("tp", None, None),
        P("tp", None, None),
        P("tp", None),
        P("req", "tp"),
        P("tp"),
        P("req", None),
        P("req", None),
        P("req", None, "tp"),
        P("req", None, "tp"),
        P("req", "tp", None),
    )
    out_specs = (P("req", "tp"), P("req", "tp"))
    body = on_block if mesh.shape["req"] == 16 and mesh.shape["tp"] == 2 else on_device
    return jax.shard_map(
        body, mesh=mesh, in_specs=in_specs, out_specs=out_specs, check_vma=False
    )
```

```python
import math

import jax
import jax.numpy as jnp
from jax import lax
from jax.experimental import pallas as pl
from jax.experimental.pallas import tpu as pltpu
from jax.sharding import PartitionSpec as P

NEGATIVE = -1e30
EPSILON = 1e-06


def on_device(
    queries, stretch_cache, prefix_pool, page_table, prefix_len, prompt_cache, prompt_len,
    group_ids, absorb_weight, value_weight, out_weight, residual, norm_gain, routes,
    route_weight, gate_weight, up_weight, down_weight,
):
    tokens = queries.shape[0]
    prompts = lax.all_gather(prompt_cache, "req", axis=1, tiled=True)
    projected = attend(
        queries, stretch_cache, prefix_pool, page_table, prefix_len, prompts, prompt_len,
        group_ids, absorb_weight, value_weight, out_weight,
    )
    attention_part = lax.psum_scatter(
        projected.astype(jnp.bfloat16), "tp", scatter_dimension=1, tiled=True
    ).astype(jnp.float32)
    attended = (residual.astype(jnp.float32) + attention_part).astype(jnp.bfloat16)
    stream = attended.astype(jnp.float32)
    squares = lax.psum(jnp.sum(stream * stream, axis=1), "tp")
    model_width = out_weight.shape[1]
    normed = (
        stream * lax.rsqrt(squares / model_width + EPSILON)[:, None] * norm_gain.astype(jnp.float32)
    ).astype(jnp.bfloat16)
    experts = lax.axis_size("req")
    top = routes.shape[1]
    capacity = max(2, tokens * top * 4 // (3 * experts))
    choice = routes[:, :, None] == jnp.arange(experts, dtype=jnp.int32)[None, None, :]
    share = jnp.sum(jnp.where(choice, route_weight[:, :, None], 0.0), axis=1).T
    named = share > 0.0
    before = jnp.arange(tokens)[:, None] <= jnp.arange(tokens)[None, :]
    slot = jnp.dot(
        named.astype(jnp.bfloat16), before.astype(jnp.bfloat16), preferred_element_type=jnp.float32
    ).astype(jnp.int32) - 1
    picks = (
        slot[:, None, :] == jnp.arange(capacity, dtype=jnp.int32)[None, :, None]
    ) & named[:, None, :]
    chooser = picks.astype(jnp.bfloat16).reshape(experts * capacity, tokens)
    level = jnp.sum(jnp.where(picks, share[:, None, :], 0.0), axis=2)
    whole = lax.all_gather(normed, "tp", axis=1, tiled=True)
    buffer = (
        jnp.dot(chooser, whole, preferred_element_type=jnp.float32)
        .astype(jnp.bfloat16)
        .reshape(experts, capacity, -1)
    )
    received = lax.all_to_all(buffer, "req", split_axis=0, concat_axis=0, tiled=True)
    gate = jnp.einsum("snd,df->snf", received, gate_weight[0], preferred_element_type=jnp.float32)
    up = jnp.einsum("snd,df->snf", received, up_weight[0], preferred_element_type=jnp.float32)
    hidden = (jax.nn.silu(gate) * up).astype(jnp.bfloat16)
    part_out = jnp.einsum(
        "snf,fd->snd", hidden, down_weight[0], preferred_element_type=jnp.float32
    ).astype(jnp.bfloat16)
    returned = lax.all_to_all(part_out, "req", split_axis=0, concat_axis=0, tiled=True)
    weighted = (returned.astype(jnp.float32) * level[:, :, None]).astype(jnp.bfloat16)
    combined = lax.dot_general(
        chooser, weighted.reshape(experts * capacity, -1), (((0,), (0,)), ((), ())),
        preferred_element_type=jnp.float32,
    )
    expert_part = lax.psum_scatter(
        combined.astype(jnp.bfloat16), "tp", scatter_dimension=1, tiled=True
    ).astype(jnp.float32)
    mixed = (stream + expert_part).astype(jnp.bfloat16)
    return (attended, mixed)


def attend(
    queries, stretch_cache, prefix_pool, page_table, prefix_len, prompts, prompt_len,
    group_ids, absorb_weight, value_weight, out_weight,
):
    tokens, heads, width = queries.shape
    nope, rank = absorb_weight.shape[1], value_weight.shape[1]
    me = lax.axis_index("req")
    requests = jnp.arange(group_ids.shape[0], dtype=jnp.int32) == me
    group = jnp.sum(jnp.where(requests, group_ids, 0))
    own_length = jnp.sum(jnp.where(requests, prefix_len, 0))
    prompt_length = jnp.where(group == 0, prompt_len[0], prompt_len[1])
    pages, page = prefix_pool.shape[:2]
    order = jnp.arange(pages, dtype=jnp.int32)
    logical = jnp.sum(
        jnp.where(page_table[0][None, :] == order[:, None], order[None, :], 0), axis=1
    )
    prefix_at = (logical[:, None] * page + jnp.arange(page, dtype=jnp.int32)[None, :]).reshape(-1)
    prompt = jnp.where(group == 0, prompts[0], prompts[1])
    keys = jnp.concatenate(
        [stretch_cache, prompt, prefix_pool.reshape(pages * page, -1)], axis=0
    )
    seen = jnp.concatenate(
        [jnp.arange(prompt.shape[0]) < prompt_length, prefix_at < own_length]
    )
    token = jnp.arange(tokens)
    visible = jnp.concatenate(
        [
            token[None, :] <= token[:, None],
            jnp.broadcast_to(seen[None, :], (tokens, seen.shape[0])),
        ],
        axis=1,
    )
    turned = jnp.transpose(queries, (1, 0, 2))
    absorbed = jnp.concatenate(
        [
            jnp.einsum(
                "htn,hnr->htr", turned[:, :, :nope], absorb_weight,
                preferred_element_type=jnp.float32,
            ).astype(jnp.bfloat16),
            turned[:, :, nope:],
        ],
        axis=2,
    )
    scores = jnp.einsum("htc,kc->htk", absorbed, keys, preferred_element_type=jnp.float32)
    scores = jnp.where(visible[None], scores * width ** (-0.5), NEGATIVE)
    weights = jnp.exp(scores - jnp.max(scores, axis=2, keepdims=True))
    weights = jnp.where(visible[None], weights, 0.0)
    totals = jnp.sum(weights, axis=2, keepdims=True)
    latent = jnp.einsum(
        "htk,kr->htr", weights.astype(jnp.bfloat16), keys[:, :rank],
        preferred_element_type=jnp.float32,
    )
    latent = (latent / totals).astype(jnp.bfloat16)
    heads_out = jnp.einsum(
        "htr,hrv->thv", latent, value_weight, preferred_element_type=jnp.float32
    ).astype(jnp.bfloat16)
    return jnp.dot(
        heads_out.reshape(tokens, -1), out_weight, preferred_element_type=jnp.float32
    )


MESH = pl.DeviceIdType.MESH


def coordinates():
    me = lax.axis_index("req")
    return me // 4, (me // 2) % 2, me % 2, lax.axis_index("tp")


def place(z, x, core, y):
    return {"req": (z * 2 + x) * 2 + core, "tp": y}


def greet():
    z, x, core, y = coordinates()
    me = lax.axis_index("req")
    barrier = pltpu.get_barrier_semaphore()
    for step in range(1, 16):
        pl.semaphore_signal(
            barrier, inc=1, device_id={"req": (me + step) % 16, "tp": y}, device_id_type=MESH
        )
    pl.semaphore_signal(barrier, inc=1, device_id=place(z, x, core, 1 - y), device_id_type=MESH)


def plane_at(place_in_turn):
    z = coordinates()[0]
    high = z // 2
    near = z + high * (3 - 2 * z)
    late = place_in_turn // 2
    odd = place_in_turn % 2
    first = (1 - odd) * (1 - late) * near + odd * (1 - late) * (1 - near) + late * place_in_turn
    return first + high * (3 - 2 * first)


def spread_tokens(whole, send, recv, mid_send, mid_recv):
    z, x, core, y = coordinates()
    quarter = whole.shape[2] // 4

    def piece(zp, xp, yp, half, cp):
        return whole.at[
            (zp * 2 + xp) * 2 + cp,
            :,
            pl.ds(pl.multiple_of((yp * 2 + half) * quarter, quarter), quarter),
        ]

    def hop(zp, xp, yp, half, cp, kind, peer):
        slot = zp * 8 + xp * 4 + yp * 2 + half
        part = piece(zp, xp, yp, half, cp)
        return pltpu.make_async_remote_copy(
            part, part, send.at[kind, slot], recv.at[cp, slot], device_id=peer, device_id_type=MESH
        )

    def edge(zp, xp, yp, side, kind, peer):
        slot = zp * 8 + xp * 4 + yp * 2 + side
        narrow = quarter // 2
        part = whole.at[
            (zp * 2 + xp) * 2 + core,
            :,
            pl.ds(pl.multiple_of(yp * 2 * quarter + side * 3 * narrow, narrow), narrow),
        ]
        return pltpu.make_async_remote_copy(
            part, part, send.at[kind, slot], recv.at[core, slot], device_id=peer, device_id_type=MESH
        )

    def middle(zp, way, peer):
        narrow = quarter // 2
        part = whole.at[
            (zp * 2 + 1 - x) * 2 + core,
            :,
            pl.ds(pl.multiple_of((1 - y) * 2 * quarter + narrow, narrow), quarter),
        ]
        return pltpu.make_async_remote_copy(
            part, part, mid_send.at[way, zp], mid_recv.at[zp], device_id=peer, device_id_type=MESH
        )

    up, down = place(z + 1, x, core, y), place(z - 1, x, core, y)
    over_x, over_y, other = place(z, 1 - x, core, y), place(z, x, core, 1 - y), place(z, x, 1 - core, y)
    between = z * (3 - z)

    def pass_middle(zp, finish):
        @pl.when((zp <= z) & (z < 3))
        def _():
            copy = middle(zp, 0, up)
            copy.wait_send() if finish else copy.start()

        @pl.when((zp >= z) & (z > 0))
        def _():
            copy = middle(zp, 1, down)
            copy.wait_send() if finish else copy.start()

    def relay_middle(zp):
        @pl.when(between > 0)
        def _():
            middle(zp, 0, over_x).wait_recv()
            pass_middle(zp, False)

    def column(zp, finish, halves=(0, 1), ways=(True, True)):
        for half in halves if ways[0] else ():
            for go, kind, peer in (
                ((zp <= z) & (z < 3), 0, up), ((zp >= z) & (z > 0), 1, down)
            ):
                @pl.when(go)
                def _(kind=kind, peer=peer, half=half):
                    copy = hop(zp, x, y, half, core, kind, peer)
                    copy.wait_send() if finish else copy.start()
        for kind, peer, half in ((2, over_x, 0), (3, over_y, 1), (2, over_x, 1), (3, over_y, 0)):
            if half in halves and ways[1]:
                copy = hop(zp, x, y, half, core, kind, peer)
                copy.wait_send() if finish else copy.start()
        for half in halves if ways[1] else ():
            copy = hop(zp, x, y, half, core, 4, other)
            copy.wait_send() if finish else copy.start()

    def forward(zp):
        @pl.when(between > 0)
        def _():
            for half in range(2):
                hop(zp, x, y, half, core, 0, over_x).wait_recv()
                column(zp, False, (half,), (True, False))

    def arrive(zp):
        @pl.when(between == 0)
        def _():
            for half in range(2):
                hop(zp, x, y, half, core, 0, over_x).wait_recv()

        column(zp, False, (0, 1), (False, True))

    def beside(zp, finish, own):
        if not finish:
            for half in range(2):
                hop(zp, 1 - x, y, half, core, 2, over_x).wait_recv()
                hop(zp, x, 1 - y, half, core, 3, over_y).wait_recv()
        if own:
            copies = [hop(zp, 1 - x, y, 0, core, 3, over_y), hop(zp, x, 1 - y, 1, core, 2, over_x)]
        else:
            copies = [edge(zp, 1 - x, y, 0, 3, over_y), edge(zp, x, 1 - y, 1, 2, over_x)]
        for half in range(2):
            copies.append(hop(zp, 1 - x, y, half, core, 4, other))
            copies.append(hop(zp, x, 1 - y, half, core, 4, other))
        for copy in copies:
            copy.wait_send() if finish else copy.start()

    def diagonal(zp, finish):
        if not finish:
            @pl.when(zp == z)
            def _():
                for half in range(2):
                    hop(zp, 1 - x, 1 - y, half, core, 2, over_x).wait_recv()
                pass_middle(zp, False)

            @pl.when(zp != z)
            def _():
                for side in range(2):
                    edge(zp, 1 - x, 1 - y, side, 2, over_x).wait_recv()

            @pl.when((zp != z) & (between == 0))
            def _():
                middle(zp, 0, over_x).wait_recv()

        for half in range(2):
            copy = hop(zp, 1 - x, 1 - y, half, core, 4, other)
            copy.wait_send() if finish else copy.start()

    def complete(zp):
        for xp in range(2):
            for yp in range(2):
                for half in range(2):
                    hop(zp, xp, yp, half, 1 - core, 4, other).wait_recv()

    def close(zp):
        column(zp, True)

        @pl.when(zp == z)
        def _():
            beside(zp, True, True)

        @pl.when(zp != z)
        def _():
            beside(zp, True, False)

        diagonal(zp, True)
        pass_middle(zp, True)

    return column, forward, arrive, beside, relay_middle, diagonal, complete, close


def return_sums(
    parts, part_in, chooser, acc, x_diag, y_diag, x_in, y_in, z_in, mid_in, center_in, sems, mid_sems,
    center_sems,
):
    z, x, core, y = coordinates()
    rows, half_cols = acc.shape[2], acc.shape[3] // 2
    half_rows = rows // 2
    over_x, over_y, other = place(z, 1 - x, core, y), place(z, x, core, 1 - y), place(z, x, 1 - core, y)
    mine = pl.ds(pl.multiple_of(y * half_cols, half_cols), half_cols)
    theirs = pl.ds(pl.multiple_of((1 - y) * half_cols, half_cols), half_cols)

    def copy(source, target, kind, zp, peer):
        return pltpu.make_async_remote_copy(
            source, target, sems.at[0, kind, zp], sems.at[1, kind, zp],
            device_id=peer, device_id_type=MESH,
        )

    def core_copy(zp, xp):
        return copy(parts.at[zp, xp * 2 + 1 - core], part_in.at[zp, xp], xp, zp, other)

    def split(own):
        return half_rows if own else half_rows // 2

    def diag_copies(zp, own):
        far, edge = acc.at[zp, 1 - x], split(own)
        over, under = pl.ds(0, edge), pl.ds(rows - edge, edge)
        return (
            copy(far.at[over, theirs], y_diag.at[zp, over], 2, zp, over_y),
            copy(far.at[under, theirs], x_diag.at[zp, over], 3, zp, over_x),
        )

    def free_copies(zp, own):
        edge = split(own)
        after, ahead = pl.ds(edge, rows - edge), pl.ds(0, rows - edge)
        return (
            copy(acc.at[zp, 1 - x].at[after, mine], x_in.at[zp, after], 4, zp, over_x),
            copy(acc.at[zp, x].at[ahead, theirs], y_in.at[zp, ahead], 5, zp, over_y),
        )

    def last_copies(zp, own):
        edge = split(own)
        over, under = pl.ds(0, edge), pl.ds(rows - edge, edge)
        return (
            copy(acc.at[zp, 1 - x].at[over, mine], x_in.at[zp, over], 6, zp, over_x),
            copy(acc.at[zp, x].at[under, theirs], y_in.at[zp, under], 7, zp, over_y),
        )

    center = pl.ds(half_rows // 2, half_rows)

    def center_copy(zp):
        return pltpu.make_async_remote_copy(
            acc.at[zp, 1 - x].at[center, theirs], center_in.at[z],
            center_sems.at[0, zp], center_sems.at[1, z],
            device_id=place(zp, x, core, y), device_id_type=MESH,
        )

    def center_arrival(zp):
        return pltpu.make_async_remote_copy(
            acc.at[zp, 1 - x].at[center, theirs], center_in.at[zp],
            center_sems.at[0, zp], center_sems.at[1, zp],
            device_id=place(near, x, core, y), device_id_type=MESH,
        )

    def plane_copy(zp):
        return pltpu.make_async_remote_copy(
            acc.at[zp, x].at[:, mine], z_in.at[z], sems.at[0, 8, zp], sems.at[1, 8, z],
            device_id=place(zp, x, core, y), device_id_type=MESH,
        )

    between = z * (3 - z)
    near = plane_at(1)

    def plane_arrival(zp):
        return pltpu.make_async_remote_copy(
            acc.at[zp, x].at[:, mine], z_in.at[zp], sems.at[0, 8, zp], sems.at[1, 8, zp],
            device_id=place(near, x, core, y), device_id_type=MESH,
        )

    def gather_copy(zp, half):
        lines = pl.ds(half * half_rows, half_rows)
        return pltpu.make_async_remote_copy(
            acc.at[zp, x].at[lines, mine], mid_in.at[zp, lines],
            mid_sems.at[0, half, zp], mid_sems.at[1, half, zp],
            device_id=place(near, x, core, y), device_id_type=MESH,
        )

    def joint_copy(zp, half):
        lines = pl.ds(half * half_rows, half_rows)
        return pltpu.make_async_remote_copy(
            acc.at[zp, x].at[lines, mine], z_in.at[z, lines],
            mid_sems.at[2, half, zp], mid_sems.at[3, half, z],
            device_id=place(zp, x, core, y), device_id_type=MESH,
        )

    def joint_arrival(zp, half):
        lines = pl.ds(half * half_rows, half_rows)
        return pltpu.make_async_remote_copy(
            acc.at[zp, x].at[lines, mine], z_in.at[zp, lines],
            mid_sems.at[2, half, zp], mid_sems.at[3, half, zp],
            device_id=place(near, x, core, y), device_id_type=MESH,
        )

    def add(target, *terms):
        total = target[...].astype(jnp.float32)
        for term in terms:
            total = total + term[...].astype(jnp.float32)
        target[...] = total.astype(target.dtype)

    def cores(zp, own):
        down = (((0,), (0,)), ((), ()))
        for xp in range(2):
            core_copy(zp, xp).wait_recv()
            request = (zp * 2 + xp) * 2 + core
            total = lax.dot_general(
                chooser[0, request], parts[zp, xp * 2 + core], down,
                preferred_element_type=jnp.float32,
            ) + lax.dot_general(
                chooser[1, request], part_in[zp, xp], down, preferred_element_type=jnp.float32
            )
            acc[zp, xp] = total.astype(jnp.bfloat16)
        if own:
            for item in free_copies(zp, own):
                item.start()
            others = [plane_at(turn) for turn in range(1, 4)]
            for source in others:
                center_arrival(source).wait_recv()
            add(
                acc.at[zp, 1 - x].at[center, theirs],
                *[center_in.at[source] for source in others],
            )
            for item in diag_copies(zp, own):
                item.start()
        else:
            for item in diag_copies(zp, own) + free_copies(zp, own):
                item.start()
            center_copy(zp).start()

    def corners(zp, own):
        edge = split(own)
        over, under = pl.ds(0, edge), pl.ds(rows - edge, edge)
        from_y, from_x = diag_copies(zp, own)
        over_x_copy, over_y_copy = last_copies(zp, own)
        from_y.wait_recv()
        add(acc.at[zp, 1 - x].at[over, mine], y_diag.at[zp, over])
        over_x_copy.start()
        from_x.wait_recv()
        add(acc.at[zp, x].at[under, theirs], x_diag.at[zp, over])
        over_y_copy.start()

    def arrivals(zp, own):
        for item in free_copies(zp, own) + last_copies(zp, own):
            item.wait_recv()

    def columns(zp):
        arrivals(zp, False)
        add(acc.at[zp, x].at[:, mine], x_in.at[zp], y_in.at[zp])

        @pl.when(zp == near)
        def _():
            plane_copy(zp).start()

        @pl.when((zp != near) & (between == 0))
        def _():
            for half in range(2):
                gather_copy(zp, half).start()

    def joints(zp):
        @pl.when(between > 0)
        def _():
            for half in range(2):
                lines = pl.ds(half * half_rows, half_rows)
                gather_copy(zp, half).wait_recv()
                add(acc.at[zp, x].at[lines, mine], mid_in.at[zp, lines])
                joint_copy(zp, half).start()

    def final(result):
        arrivals(z, True)
        total = acc[z, x, :, mine].astype(jnp.float32)
        total = total + x_in[z].astype(jnp.float32) + y_in[z].astype(jnp.float32)
        plane_arrival(near).wait_recv()
        total = total + z_in[near].astype(jnp.float32)
        far = plane_at(2)
        for half in range(2):
            joint_arrival(far, half).wait_recv()
        result[...] = total + z_in[far].astype(jnp.float32)

    def close(zp):
        for xp in range(2):
            core_copy(zp, xp).wait_send()

        def sent(own):
            for item in diag_copies(zp, own) + free_copies(zp, own) + last_copies(zp, own):
                item.wait_send()
            if not own:
                center_copy(zp).wait_send()

        pl.when(zp == z)(lambda: sent(True))
        pl.when(zp != z)(lambda: sent(False))

        @pl.when(zp == near)
        def _():
            plane_copy(zp).wait_send()

        @pl.when((zp != near) & (zp != z) & (between == 0))
        def _():
            for half in range(2):
                gather_copy(zp, half).wait_send()

        @pl.when((zp != near) & (zp != z) & (between > 0))
        def _():
            for half in range(2):
                joint_copy(zp, half).wait_send()

    return core_copy, cores, corners, columns, joints, final, close


def choose(mine, chooser, which):
    requests, tokens = mine.shape
    capacity = chooser.shape[2]
    named = jnp.where(mine[...] > 0.0, 1.0, 0.0)
    rows = lax.broadcasted_iota(jnp.int32, (tokens, tokens), 0)
    columns = lax.broadcasted_iota(jnp.int32, (tokens, tokens), 1)
    before = jnp.where(rows <= columns, 1.0, 0.0).astype(jnp.bfloat16)
    slot = jnp.dot(named.astype(jnp.bfloat16), before, preferred_element_type=jnp.float32)
    wanted = jnp.where(named > 0.0, slot - 1.0, -1.0).astype(jnp.int32)
    places = lax.broadcasted_iota(jnp.int32, (capacity, tokens), 0)
    for request in range(requests):
        picks = jnp.where(wanted[request : request + 1, :] == places, 1.0, 0.0)
        chooser[which, request] = picks.astype(jnp.bfloat16)


def share_prompts(block_ref, share_ref, keys_ref, mine_ref, send, recv, send_w, recv_w, local):
    me = lax.axis_index("req")
    y = lax.axis_index("tp")
    depth = block_ref.shape[1]
    rows = pl.ds(pl.multiple_of(me * depth, depth), depth)
    core, other = me % 2, me + 1 - 2 * (me % 2)

    def block(source):
        return keys_ref.at[:, pl.ds(pl.multiple_of(source * depth, depth), depth), :]

    def shares(step):
        peer = (me + step) % 16
        return pltpu.make_async_remote_copy(
            share_ref.at[peer], mine_ref.at[me], send_w.at[step], recv_w.at[step],
            device_id={"req": peer, "tp": y}, device_id_type=MESH,
        )

    def direct(step):
        return pltpu.make_async_remote_copy(
            block_ref, keys_ref.at[:, rows, :], send.at[step], recv.at[step],
            device_id={"req": (me + 2 * step) % 16, "tp": y}, device_id_type=MESH,
        )

    def across(source, index):
        return pltpu.make_async_remote_copy(
            block(source), block(source), send.at[index], recv.at[index],
            device_id={"req": other, "tp": y}, device_id_type=MESH,
        )

    home = pltpu.make_async_remote_copy(
        block_ref, keys_ref.at[:, rows, :], send.at[8 + me // 2], recv.at[8 + me // 2],
        device_id={"req": other, "tp": y}, device_id_type=MESH,
    )
    own = pltpu.make_async_copy(block_ref, keys_ref.at[:, rows, :], local.at[0])
    own_share = pltpu.make_async_copy(share_ref.at[me], mine_ref.at[me], local.at[1])

    def start():
        for step in range(1, 8):
            direct(step).start()
        home.start()
        own.start()
        own_share.start()

        def send_share(step, carry):
            shares(step).start()
            return carry

        lax.fori_loop(1, 16, send_share, 0)

    def relay(step):
        source = (me + 2 * step) % 16
        across(source, 8 - step).wait_recv()
        across(source, 8 + source // 2).start()

    def finish():
        own.wait()
        for step in range(8):
            source = (me + 2 * step) % 16 + 1 - 2 * core
            across(source, 8 + source // 2).wait_recv()

    def finish_shares():
        own_share.wait()

        def wait_share(step, carry):
            shares(step).wait_recv()
            return carry

        lax.fori_loop(1, 16, wait_share, 0)

    def close():
        home.wait_send()
        for step in range(1, 8):
            direct(step).wait_send()
            source = (me + 2 * step) % 16
            across(source, 8 + source // 2).wait_send()

        def close_share(step, carry):
            shares(step).wait_send()
            return carry

        lax.fori_loop(1, 16, close_share, 0)

    return start, relay, finish, finish_shares, close


def layer_kernel(
    page_table, prefix_len, prompt_len, group_ids,
    routes, route_weight, gain, prompt_block,
    residual_hbm, query_hbm, stretch_hbm, pool_hbm, absorb_hbm, value_hbm, out_hbm, gate_hbm, up_hbm, down_hbm,
    attention_part, expert_part,
    query, residual, stretch, keys, absorb, value, out_w, prompts, absorbed, bests, totals, latents, bias,
    heads,
    share, share_in, projected,
    whole, outgoing, incoming, squares_out, squares_in, gains, mine_share, other_share, roots,
    chooser, level,
    gate_w, up_w, down_w, rows, hidden, parts, part_in, acc, x_diag, y_diag, x_in, y_in, z_in, mid_in,
    center_in, prompt_send, prompt_recv, share_send, share_recv, local_sems,
    pair_sems, load_sems, root_sems, send, recv, mid_send, mid_recv, sems, mid_sems, center_sems,
):
    z, x, core, y = coordinates()
    me = lax.axis_index("req")
    tokens, half_cols = residual.shape
    quarter = half_cols // 2
    count, nope, rank = absorb.shape
    width = query.shape[1]
    pool_rows = pool_hbm.shape[0]
    own_rows = pool_rows + tokens
    loads = [
        pltpu.make_async_copy(source, target, load_sems.at[index])
        for index, (source, target) in enumerate(
            (
                (query_hbm, query), (absorb_hbm, absorb), (stretch_hbm, stretch),
                (pool_hbm, keys.at[pl.ds(0, pool_rows)]), (value_hbm, value), (out_hbm, out_w),
                (gate_hbm, gate_w), (up_hbm, up_w), (down_hbm, down_w), (residual_hbm, residual),
            )
        )
    ]
    greet()
    for load in loads:
        load.start()
    mine = pl.ds(pl.multiple_of(y * half_cols, half_cols), half_cols)
    theirs = pl.ds(pl.multiple_of((1 - y) * half_cols, half_cols), half_cols)
    over_y, other = place(z, x, core, 1 - y), place(z, x, 1 - core, y)

    def pair(source, target, index, peer=over_y):
        return pltpu.make_async_remote_copy(
            source, target, pair_sems.at[0, index], pair_sems.at[1, index],
            device_id=peer, device_id_type=MESH,
        )

    def swap(half):
        span = pl.ds(half * quarter, quarter)
        return pair(outgoing.at[:, span], incoming.at[:, span], half)

    squares = pair(squares_out, squares_in, 2)
    gain_copy = pair(gains.at[y], gains.at[y], 3)
    share_copy = pair(mine_share, other_share, 4, other)
    start_prompts, relay, finish_prompts, finish_shares, close_prompts = share_prompts(
        prompt_block, share, prompts, share_in, prompt_send, prompt_recv, share_send, share_recv,
        local_sems,
    )
    expert_of = lax.broadcasted_iota(jnp.int32, (16, tokens), 0)
    given = jnp.zeros((16, tokens), jnp.float32)
    for choice in range(routes.shape[0]):
        hit = routes[choice : choice + 1, :] == expert_of
        given = given + jnp.where(hit, route_weight[choice : choice + 1, :], 0.0)
    for expert in range(16):
        share[expert] = given[expert : expert + 1, :]
    for row in range(gain.shape[0]):
        gains[y, :, pl.ds(row * gain.shape[1], gain.shape[1])] = gain[row : row + 1, :].astype(
            jnp.float32
        )
    pl.semaphore_wait(pltpu.get_barrier_semaphore(), 16)
    start_prompts()
    gain_copy.start()
    group = group_ids[me]
    page = pool_rows // page_table.shape[1]
    lane = lax.broadcasted_iota(jnp.int32, (1, pool_rows), 1)
    logical = jnp.zeros((1, pool_rows), jnp.int32)
    for index in range(page_table.shape[1]):
        logical = jnp.where(lane // page == page_table[0, index], index, logical)
    prefix_at = logical * page + lane % page
    bias[:, pl.ds(0, pool_rows)] = jnp.where(prefix_at < prefix_len[me], 0.0, NEGATIVE)
    prompt_rows = prompts.shape[1]
    prompt_lane = lax.broadcasted_iota(jnp.int32, (1, prompt_rows), 1)
    bias[:, pl.ds(pool_rows, prompt_rows)] = jnp.where(prompt_lane < prompt_len[group], 0.0, NEGATIVE)
    loads[2].wait()
    keys[pl.ds(pool_rows, tokens), :] = stretch[...].T
    for index in (0, 1, 3):
        loads[index].wait()
    first = (((0,), (0,)), ((), ()))
    across = (((1,), (1,)), ((), ()))

    factor = width ** (-0.5) * math.log2(math.e)

    batch = count // 2
    deep = batch * tokens

    def own_keys(index, carry):
        lines = pl.ds(pl.multiple_of(index * deep, deep), deep)
        for turn in range(batch):
            head = index * batch + turn
            own = pl.ds(pl.multiple_of(head * tokens, tokens), tokens)
            wide = lax.dot_general(
                query[head, pl.ds(0, nope), :], absorb[head], first,
                preferred_element_type=jnp.float32,
            )
            absorbed[own, pl.ds(0, rank)] = wide.astype(jnp.bfloat16)
            absorbed[own, pl.ds(rank, width - nope)] = query[head, pl.ds(nope, width - nope), :].T
        found = lax.dot_general(
            absorbed[lines, :], keys[pl.ds(0, own_rows), :], across,
            preferred_element_type=jnp.float32,
        )
        token = lax.rem(lax.broadcasted_iota(jnp.int32, (deep, tokens), 0), tokens)
        later = lax.broadcasted_iota(jnp.int32, (deep, tokens), 1) > token
        found = jnp.concatenate(
            [
                found[:, :pool_rows] + bias[:, pl.ds(0, pool_rows)],
                jnp.where(later, NEGATIVE, found[:, pool_rows:]),
            ],
            axis=1,
        )
        best = jnp.max(found, axis=1, keepdims=True)
        weights = jnp.exp2((found - best) * factor)
        bests[lines, :] = best
        totals[lines, :] = jnp.sum(weights, axis=1, keepdims=True)
        latents[lines, :] = jnp.dot(
            weights.astype(jnp.bfloat16), keys[pl.ds(0, own_rows), pl.ds(0, rank)],
            preferred_element_type=jnp.float32,
        )

        if index == 1:
            for step in range(1, 8):
                relay(step)
        return carry

    own_keys(0, 0)
    own_keys(1, 0)
    finish_prompts()
    keys[pl.ds(own_rows, prompt_rows), :] = prompts[group]
    loads[4].wait()
    loads[9].wait()
    size = value.shape[2]

    def prompt_keys(index, carry):
        lines = pl.ds(pl.multiple_of(index * deep, deep), deep)
        found = lax.dot_general(
            absorbed[lines, :], keys[pl.ds(own_rows, prompt_rows), :], across,
            preferred_element_type=jnp.float32,
        ) + bias[:, pl.ds(pool_rows, prompt_rows)]
        held = bests[lines, :]
        best = jnp.maximum(jnp.max(found, axis=1, keepdims=True), held)
        keep = jnp.exp2((held - best) * factor)
        weights = jnp.exp2((found - best) * factor)
        total = totals[lines, :] * keep + jnp.sum(weights, axis=1, keepdims=True)
        latent = latents[lines, :] * keep + jnp.dot(
            weights.astype(jnp.bfloat16), keys[pl.ds(own_rows, prompt_rows), pl.ds(0, rank)],
            preferred_element_type=jnp.float32,
        )
        latent = (latent * (1.0 / total)).astype(jnp.bfloat16)
        for turn in range(batch):
            head = index * batch + turn
            heads[:, pl.ds(pl.multiple_of(head * size, size), size)] = jnp.dot(
                latent[turn * tokens : (turn + 1) * tokens], value[head],
                preferred_element_type=jnp.float32,
            ).astype(jnp.bfloat16)
        return carry

    lax.fori_loop(0, 2, prompt_keys, 0)
    loads[5].wait()
    for half in range(2):
        across_cols = pl.ds(
            pl.multiple_of((1 - y) * half_cols + half * quarter, quarter), quarter
        )
        outgoing[:, pl.ds(half * quarter, quarter)] = jnp.dot(
            heads[...], out_w[:, across_cols], preferred_element_type=jnp.float32
        ).astype(jnp.bfloat16)
        swap(half).start()
    for half in range(2):
        own_cols = pl.ds(pl.multiple_of(y * half_cols + half * quarter, quarter), quarter)
        projected[:, pl.ds(half * quarter, quarter)] = jnp.dot(
            heads[...], out_w[:, own_cols], preferred_element_type=jnp.float32
        )
    finish_shares()
    for request in range(16):
        mine_share[request : request + 1, :] = share_in[request]
    share_copy.start()
    choose(mine_share, chooser, 0)
    (
        column, forward, arrive, beside, relay_middle, diagonal, complete, close_spread,
    ) = spread_tokens(
        whole, send, recv, mid_send, mid_recv
    )
    sums = jnp.zeros((tokens, 1), jnp.float32)
    for half in range(2):
        span = pl.ds(half * quarter, quarter)
        swap(half).wait_recv()
        added = projected[:, span] + incoming[:, span].astype(jnp.float32)
        projected[:, span] = added
        rounded = (residual[:, span].astype(jnp.float32) + added).astype(jnp.bfloat16)
        whole[me, :, pl.ds(pl.multiple_of(y * half_cols + half * quarter, quarter), quarter)] = rounded
        stream = rounded.astype(jnp.float32)
        sums = sums + jnp.sum(stream * stream, axis=1, keepdims=True)
        if half == 1:
            diag = lax.broadcasted_iota(jnp.int32, (tokens, tokens), 1) == (
                lax.broadcasted_iota(jnp.int32, (tokens, tokens), 0)
            )
            squares_out[...] = jnp.sum(jnp.where(diag, sums, 0.0), axis=0, keepdims=True)
            squares.start()
        column(z, False, (half,))
    part_out = pltpu.make_async_copy(projected, attention_part, load_sems.at[10])
    part_out.start()
    share_copy.wait_recv()
    choose(other_share, chooser, 1)

    def root_copy(step):
        peer = (me + step) % 16
        return pltpu.make_async_remote_copy(
            roots.at[me], roots.at[me], root_sems.at[0, peer], root_sems.at[1, me],
            device_id={"req": peer, "tp": y}, device_id_type=MESH,
        )

    def root_arrival(request):
        return pltpu.make_async_remote_copy(
            roots.at[request], roots.at[request], root_sems.at[0, request],
            root_sems.at[1, request], device_id=over_y, device_id_type=MESH,
        )

    forward(plane_at(1))
    arrive(plane_at(1))
    forward(plane_at(2))
    beside(z, False, True)
    squares.wait_recv()
    roots[me] = lax.rsqrt((squares_out[...] + squares_in[...]) / (2 * half_cols) + EPSILON)

    def send_root(step, carry):
        root_copy(step).start()
        return carry

    lax.fori_loop(1, 16, send_root, 0)
    gain_copy.wait_recv()
    for load in loads[6:9]:
        load.wait()
    capacity = chooser.shape[2]
    core_copy, cores, corners, columns, joints, final, close_return = return_sums(
        parts, part_in, chooser, acc, x_diag, y_diag, x_in, y_in, z_in, mid_in, center_in, sems, mid_sems,
        center_sems,
    )

    def compute(zp):
        for index in range(4):
            request = zp * 4 + index

            @pl.when(request != me)
            def _(request=request):
                root_arrival(request).wait_recv()

        for index in range(4):
            request = zp * 4 + index
            lines = pl.ds(index * capacity, capacity)
            picks = chooser[0, request]
            picked = jnp.dot(picks, whole[request], preferred_element_type=jnp.float32)
            wide = picks.astype(jnp.float32)
            picked = picked * jnp.sum(wide * roots[request], axis=1, keepdims=True)
            shared = jnp.sum(wide * share_in[request], axis=1, keepdims=True)
            level[lines, :] = jnp.broadcast_to(shared, (capacity, level.shape[1]))
            for side in range(2):
                span = pl.ds(side * half_cols, half_cols)
                scaled = picked[:, side * half_cols : (side + 1) * half_cols] * gains[side]
                rows[lines, span] = scaled.astype(jnp.bfloat16)
        gate = lax.dot_general(rows[...], gate_w[...], across, preferred_element_type=jnp.float32)
        up = lax.dot_general(rows[...], up_w[...], across, preferred_element_type=jnp.float32)
        hidden[...] = (gate / (1.0 + jnp.exp(-gate)) * up * level[:, :1]).astype(jnp.bfloat16)
        part = jnp.dot(hidden[...], down_w[...], preferred_element_type=jnp.float32)
        for index in range(4):
            parts[zp, index] = part[index * capacity : (index + 1) * capacity].astype(jnp.bfloat16)
        for xp in range(2):
            core_copy(zp, xp).start()

    def close_dispatch():
        def close(zp, carry):
            close_spread(zp)
            return carry

        lax.fori_loop(0, 4, close, 0)

        def close_root(step, carry):
            root_copy(step).wait_send()
            return carry

        lax.fori_loop(1, 16, close_root, 0)
        for item in (swap(0), swap(1), squares, gain_copy, share_copy):
            item.wait_send()
        close_prompts()

    def step(turn, carry):
        @pl.when(turn < 3)
        def _():
            arrive(plane_at(turn + 1))

        @pl.when(turn == 1)
        def _():
            forward(plane_at(3))

        @pl.when(turn == 2)
        def _():
            relay_middle(plane_at(1))
            relay_middle(plane_at(2))

        @pl.when(turn < 4)
        def _():
            beside(plane_at(turn), False, False)

        @pl.when(turn == 2)
        def _():
            relay_middle(plane_at(3))

        @pl.when(turn == 4)
        def _():
            diagonal(plane_at(3), False)

        @pl.when(turn >= 5)
        def _():
            columns(plane_at(turn - 4))

        @pl.when(turn == 7)
        def _():
            joints(plane_at(2))

        @pl.when((turn >= 4) & (turn < 7))
        def _():
            corners(plane_at(turn - 3), False)

        @pl.when((turn >= 3) & (turn < 6))
        def _():
            cores(plane_at(turn - 2), False)

        @pl.when(turn == 6)
        def _():
            cores(z, True)
            close_dispatch()

        @pl.when(turn < 5)
        def _():
            zp = plane_at(turn - 1)

            @pl.when(turn < 4)
            def _():
                diagonal(zp, False)

            complete(zp)
            compute(zp)

        return carry

    lax.fori_loop(1, 8, step, 0)
    corners(z, True)
    for turn in (1, 2):
        close_return(plane_at(turn))
    joints(plane_at(3))
    final(expert_part)
    for turn in (0, 3):
        close_return(plane_at(turn))
    part_out.wait()


def on_block(
    queries, stretch_cache, prefix_pool, page_table, prefix_len, prompt_cache, prompt_len,
    group_ids, absorb_weight, value_weight, out_weight, residual, norm_gain, routes,
    route_weight, gate_weight, up_weight, down_weight,
):
    tokens, count, width = queries.shape
    nope, rank = absorb_weight.shape[1:]
    size = value_weight.shape[2]
    top = routes.shape[1]
    experts = 16
    capacity = max(2, tokens * top * 4 // (3 * experts))
    pages, page, entry = prefix_pool.shape
    groups, depth = prompt_cache.shape[:2]
    half = residual.shape[1]
    model = out_weight.shape[1]
    units = down_weight.shape[1]
    own_rows = pages * page + tokens
    bf16, f32 = jnp.bfloat16, jnp.float32
    dma = pltpu.SemaphoreType.DMA
    vmem = pl.BlockSpec(memory_space=pltpu.VMEM)
    smem = pl.BlockSpec(memory_space=pltpu.SMEM)
    anywhere = pl.BlockSpec(memory_space=pl.ANY)
    attention_part, expert_part = pl.pallas_call(
        layer_kernel,
        out_shape=(jax.ShapeDtypeStruct((tokens, half), f32),) * 2,
        in_specs=[smem] * 4 + [vmem] * 4 + [anywhere] * 10,
        out_specs=(anywhere, vmem),
        scratch_shapes=[
            pltpu.VMEM((count, width, tokens), bf16),
            pltpu.VMEM((tokens, half), bf16),
            pltpu.VMEM((entry, tokens), bf16),
            pltpu.VMEM((own_rows + depth * 16, entry), bf16),
            pltpu.VMEM((count, nope, rank), bf16),
            pltpu.VMEM((count, rank, size), bf16),
            pltpu.VMEM((count * size, model), bf16),
            pltpu.VMEM((groups, depth * 16, entry), bf16),
            pltpu.VMEM((count * tokens, entry), bf16),
            pltpu.VMEM((count * tokens, 1), f32),
            pltpu.VMEM((count * tokens, 1), f32),
            pltpu.VMEM((count * tokens, rank), f32),
            pltpu.VMEM((1, pages * page + depth * 16), f32),
            pltpu.VMEM((tokens, count * size), bf16),
            pltpu.VMEM((16, 1, tokens), f32),
            pltpu.VMEM((16, 1, tokens), f32),
            pltpu.VMEM((tokens, half), f32),
            pltpu.VMEM((16, tokens, model), bf16),
            pltpu.VMEM((tokens, half), bf16),
            pltpu.VMEM((tokens, half), bf16),
            pltpu.VMEM((1, tokens), f32),
            pltpu.VMEM((1, tokens), f32),
            pltpu.VMEM((2, 1, half), f32),
            pltpu.VMEM((16, tokens), f32),
            pltpu.VMEM((16, tokens), f32),
            pltpu.VMEM((16, 1, tokens), f32),
            pltpu.VMEM((2, 16, capacity, tokens), bf16),
            pltpu.VMEM((4 * capacity, 128), f32),
            pltpu.VMEM((units, model), bf16),
            pltpu.VMEM((units, model), bf16),
            pltpu.VMEM((units, model), bf16),
            pltpu.VMEM((4 * capacity, model), bf16),
            pltpu.VMEM((4 * capacity, units), bf16),
            pltpu.VMEM((4, 4, capacity, model), bf16),
            pltpu.VMEM((4, 2, capacity, model), bf16),
            pltpu.VMEM((4, 2, tokens, model), bf16),
            pltpu.VMEM((4, tokens // 2, half), bf16),
            pltpu.VMEM((4, tokens // 2, half), bf16),
            pltpu.VMEM((4, tokens, half), bf16),
            pltpu.VMEM((4, tokens, half), bf16),
            pltpu.VMEM((4, tokens, half), bf16),
            pltpu.VMEM((4, tokens, half), bf16),
            pltpu.VMEM((4, tokens // 2, half), bf16),
            dma((16,)),
            dma((16,)),
            dma((16,)),
            dma((16,)),
            dma((2,)),
            dma((2, 5)),
            dma((11,)),
            dma((2, 16)),
            dma((5, 32)),
            dma((2, 32)),
            dma((2, 4)),
            dma((4,)),
            dma((2, 9, 4)),
            dma((4, 2, 4)),
            dma((2, 4)),
        ],
        compiler_params=pltpu.CompilerParams(
            collective_id=0, has_side_effects=True, vmem_limit_bytes=60 << 20
        ),
    )(
        page_table, prefix_len, prompt_len, group_ids,
        routes.T, route_weight.T, norm_gain.reshape(-1, 128), prompt_cache, residual,
        jnp.transpose(queries, (1, 2, 0)), stretch_cache.T, prefix_pool.reshape(pages * page, entry),
        absorb_weight, value_weight, out_weight,
        jnp.swapaxes(gate_weight[0], 0, 1), jnp.swapaxes(up_weight[0], 0, 1), down_weight[0],
    )
    attended = (residual.astype(f32) + attention_part).astype(bf16)
    return attended, (attended.astype(f32) + expert_part).astype(bf16)


def solution(mesh):
    in_specs = (
        P("req", "tp", None),
        P("req", None),
        P("req", None, None),
        P("req", None),
        P(),
        P(None, "req", None),
        P(),
        P(),
        P("tp", None, None),
        P("tp", None, None),
        P("tp", None),
        P("req", "tp"),
        P("tp"),
        P("req", None),
        P("req", None),
        P("req", None, "tp"),
        P("req", None, "tp"),
        P("req", "tp", None),
    )
    out_specs = (P("req", "tp"), P("req", "tp"))
    body = on_block if mesh.shape["req"] == 16 and mesh.shape["tp"] == 2 else on_device
    return jax.shard_map(
        body, mesh=mesh, in_specs=in_specs, out_specs=out_specs, check_vma=False
    )
```

```python
import math

import jax
import jax.numpy as jnp
from jax import lax
from jax.experimental import pallas as pl
from jax.experimental.pallas import tpu as pltpu
from jax.sharding import PartitionSpec as P

NEGATIVE = -1e30
EPSILON = 1e-06


def on_device(
    queries, stretch_cache, prefix_pool, page_table, prefix_len, prompt_cache, prompt_len,
    group_ids, absorb_weight, value_weight, out_weight, residual, norm_gain, routes,
    route_weight, gate_weight, up_weight, down_weight,
):
    tokens = queries.shape[0]
    prompts = lax.all_gather(prompt_cache, "req", axis=1, tiled=True)
    projected = attend(
        queries, stretch_cache, prefix_pool, page_table, prefix_len, prompts, prompt_len,
        group_ids, absorb_weight, value_weight, out_weight,
    )
    attention_part = lax.psum_scatter(
        projected.astype(jnp.bfloat16), "tp", scatter_dimension=1, tiled=True
    ).astype(jnp.float32)
    attended = (residual.astype(jnp.float32) + attention_part).astype(jnp.bfloat16)
    stream = attended.astype(jnp.float32)
    squares = lax.psum(jnp.sum(stream * stream, axis=1), "tp")
    model_width = out_weight.shape[1]
    normed = (
        stream * lax.rsqrt(squares / model_width + EPSILON)[:, None] * norm_gain.astype(jnp.float32)
    ).astype(jnp.bfloat16)
    experts = lax.axis_size("req")
    top = routes.shape[1]
    capacity = max(2, tokens * top * 4 // (3 * experts))
    choice = routes[:, :, None] == jnp.arange(experts, dtype=jnp.int32)[None, None, :]
    share = jnp.sum(jnp.where(choice, route_weight[:, :, None], 0.0), axis=1).T
    named = share > 0.0
    before = jnp.arange(tokens)[:, None] <= jnp.arange(tokens)[None, :]
    slot = jnp.dot(
        named.astype(jnp.bfloat16), before.astype(jnp.bfloat16), preferred_element_type=jnp.float32
    ).astype(jnp.int32) - 1
    picks = (
        slot[:, None, :] == jnp.arange(capacity, dtype=jnp.int32)[None, :, None]
    ) & named[:, None, :]
    chooser = picks.astype(jnp.bfloat16).reshape(experts * capacity, tokens)
    level = jnp.sum(jnp.where(picks, share[:, None, :], 0.0), axis=2)
    whole = lax.all_gather(normed, "tp", axis=1, tiled=True)
    buffer = (
        jnp.dot(chooser, whole, preferred_element_type=jnp.float32)
        .astype(jnp.bfloat16)
        .reshape(experts, capacity, -1)
    )
    received = lax.all_to_all(buffer, "req", split_axis=0, concat_axis=0, tiled=True)
    gate = jnp.einsum("snd,df->snf", received, gate_weight[0], preferred_element_type=jnp.float32)
    up = jnp.einsum("snd,df->snf", received, up_weight[0], preferred_element_type=jnp.float32)
    hidden = (jax.nn.silu(gate) * up).astype(jnp.bfloat16)
    part_out = jnp.einsum(
        "snf,fd->snd", hidden, down_weight[0], preferred_element_type=jnp.float32
    ).astype(jnp.bfloat16)
    returned = lax.all_to_all(part_out, "req", split_axis=0, concat_axis=0, tiled=True)
    weighted = (returned.astype(jnp.float32) * level[:, :, None]).astype(jnp.bfloat16)
    combined = lax.dot_general(
        chooser, weighted.reshape(experts * capacity, -1), (((0,), (0,)), ((), ())),
        preferred_element_type=jnp.float32,
    )
    expert_part = lax.psum_scatter(
        combined.astype(jnp.bfloat16), "tp", scatter_dimension=1, tiled=True
    ).astype(jnp.float32)
    mixed = (stream + expert_part).astype(jnp.bfloat16)
    return (attended, mixed)


def attend(
    queries, stretch_cache, prefix_pool, page_table, prefix_len, prompts, prompt_len,
    group_ids, absorb_weight, value_weight, out_weight,
):
    tokens, heads, width = queries.shape
    nope, rank = absorb_weight.shape[1], value_weight.shape[1]
    me = lax.axis_index("req")
    requests = jnp.arange(group_ids.shape[0], dtype=jnp.int32) == me
    group = jnp.sum(jnp.where(requests, group_ids, 0))
    own_length = jnp.sum(jnp.where(requests, prefix_len, 0))
    prompt_length = jnp.where(group == 0, prompt_len[0], prompt_len[1])
    pages, page = prefix_pool.shape[:2]
    order = jnp.arange(pages, dtype=jnp.int32)
    logical = jnp.sum(
        jnp.where(page_table[0][None, :] == order[:, None], order[None, :], 0), axis=1
    )
    prefix_at = (logical[:, None] * page + jnp.arange(page, dtype=jnp.int32)[None, :]).reshape(-1)
    prompt = jnp.where(group == 0, prompts[0], prompts[1])
    keys = jnp.concatenate(
        [stretch_cache, prompt, prefix_pool.reshape(pages * page, -1)], axis=0
    )
    seen = jnp.concatenate(
        [jnp.arange(prompt.shape[0]) < prompt_length, prefix_at < own_length]
    )
    token = jnp.arange(tokens)
    visible = jnp.concatenate(
        [
            token[None, :] <= token[:, None],
            jnp.broadcast_to(seen[None, :], (tokens, seen.shape[0])),
        ],
        axis=1,
    )
    turned = jnp.transpose(queries, (1, 0, 2))
    absorbed = jnp.concatenate(
        [
            jnp.einsum(
                "htn,hnr->htr", turned[:, :, :nope], absorb_weight,
                preferred_element_type=jnp.float32,
            ).astype(jnp.bfloat16),
            turned[:, :, nope:],
        ],
        axis=2,
    )
    scores = jnp.einsum("htc,kc->htk", absorbed, keys, preferred_element_type=jnp.float32)
    scores = jnp.where(visible[None], scores * width ** (-0.5), NEGATIVE)
    weights = jnp.exp(scores - jnp.max(scores, axis=2, keepdims=True))
    weights = jnp.where(visible[None], weights, 0.0)
    totals = jnp.sum(weights, axis=2, keepdims=True)
    latent = jnp.einsum(
        "htk,kr->htr", weights.astype(jnp.bfloat16), keys[:, :rank],
        preferred_element_type=jnp.float32,
    )
    latent = (latent / totals).astype(jnp.bfloat16)
    heads_out = jnp.einsum(
        "htr,hrv->thv", latent, value_weight, preferred_element_type=jnp.float32
    ).astype(jnp.bfloat16)
    return jnp.dot(
        heads_out.reshape(tokens, -1), out_weight, preferred_element_type=jnp.float32
    )


MESH = pl.DeviceIdType.MESH


def coordinates():
    me = lax.axis_index("req")
    return me // 4, (me // 2) % 2, me % 2, lax.axis_index("tp")


def place(z, x, core, y):
    return {"req": (z * 2 + x) * 2 + core, "tp": y}


def greet():
    z, x, core, y = coordinates()
    me = lax.axis_index("req")
    barrier = pltpu.get_barrier_semaphore()
    for step in range(1, 16):
        pl.semaphore_signal(
            barrier, inc=1, device_id={"req": (me + step) % 16, "tp": y}, device_id_type=MESH
        )
    pl.semaphore_signal(barrier, inc=1, device_id=place(z, x, core, 1 - y), device_id_type=MESH)


def plane_at(place_in_turn):
    z = coordinates()[0]
    high = z // 2
    near = z + high * (3 - 2 * z)
    late = place_in_turn // 2
    odd = place_in_turn % 2
    first = (1 - odd) * (1 - late) * near + odd * (1 - late) * (1 - near) + late * place_in_turn
    return first + high * (3 - 2 * first)


def spread_tokens(whole, send, recv, mid_send, mid_recv):
    z, x, core, y = coordinates()
    quarter = whole.shape[2] // 4

    def piece(zp, xp, yp, half, cp):
        return whole.at[
            (zp * 2 + xp) * 2 + cp,
            :,
            pl.ds(pl.multiple_of((yp * 2 + half) * quarter, quarter), quarter),
        ]

    def hop(zp, xp, yp, half, cp, kind, peer):
        slot = zp * 8 + xp * 4 + yp * 2 + half
        part = piece(zp, xp, yp, half, cp)
        return pltpu.make_async_remote_copy(
            part, part, send.at[kind, slot], recv.at[cp, slot], device_id=peer, device_id_type=MESH
        )

    def edge(zp, xp, yp, side, kind, peer):
        slot = zp * 8 + xp * 4 + yp * 2 + side
        narrow = quarter // 2
        part = whole.at[
            (zp * 2 + xp) * 2 + core,
            :,
            pl.ds(pl.multiple_of(yp * 2 * quarter + side * 3 * narrow, narrow), narrow),
        ]
        return pltpu.make_async_remote_copy(
            part, part, send.at[kind, slot], recv.at[core, slot], device_id=peer, device_id_type=MESH
        )

    def middle(zp, way, peer):
        narrow = quarter // 2
        part = whole.at[
            (zp * 2 + 1 - x) * 2 + core,
            :,
            pl.ds(pl.multiple_of((1 - y) * 2 * quarter + narrow, narrow), quarter),
        ]
        return pltpu.make_async_remote_copy(
            part, part, mid_send.at[way, zp], mid_recv.at[zp], device_id=peer, device_id_type=MESH
        )

    up, down = place(z + 1, x, core, y), place(z - 1, x, core, y)
    over_x, over_y, other = place(z, 1 - x, core, y), place(z, x, core, 1 - y), place(z, x, 1 - core, y)
    between = z * (3 - z)

    def pass_middle(zp, finish):
        @pl.when((zp <= z) & (z < 3))
        def _():
            copy = middle(zp, 0, up)
            copy.wait_send() if finish else copy.start()

        @pl.when((zp >= z) & (z > 0))
        def _():
            copy = middle(zp, 1, down)
            copy.wait_send() if finish else copy.start()

    def relay_middle(zp):
        @pl.when(between > 0)
        def _():
            middle(zp, 0, over_x).wait_recv()
            pass_middle(zp, False)

    def column(zp, finish, halves=(0, 1), ways=(True, True)):
        for half in halves if ways[0] else ():
            for go, kind, peer in (
                ((zp <= z) & (z < 3), 0, up), ((zp >= z) & (z > 0), 1, down)
            ):
                @pl.when(go)
                def _(kind=kind, peer=peer, half=half):
                    copy = hop(zp, x, y, half, core, kind, peer)
                    copy.wait_send() if finish else copy.start()
        for kind, peer, half in ((2, over_x, 0), (3, over_y, 1), (2, over_x, 1), (3, over_y, 0)):
            if half in halves and ways[1]:
                copy = hop(zp, x, y, half, core, kind, peer)
                copy.wait_send() if finish else copy.start()
        for half in halves if ways[1] else ():
            copy = hop(zp, x, y, half, core, 4, other)
            copy.wait_send() if finish else copy.start()

    def forward(zp):
        @pl.when(between > 0)
        def _():
            for half in range(2):
                hop(zp, x, y, half, core, 0, over_x).wait_recv()
                column(zp, False, (half,), (True, False))

    def arrive(zp):
        @pl.when(between == 0)
        def _():
            for half in range(2):
                hop(zp, x, y, half, core, 0, over_x).wait_recv()

        column(zp, False, (0, 1), (False, True))

    def beside(zp, finish, own):
        if not finish:
            for half in range(2):
                hop(zp, 1 - x, y, half, core, 2, over_x).wait_recv()
                hop(zp, x, 1 - y, half, core, 3, over_y).wait_recv()
        if own:
            copies = [hop(zp, 1 - x, y, 0, core, 3, over_y), hop(zp, x, 1 - y, 1, core, 2, over_x)]
        else:
            copies = [edge(zp, 1 - x, y, 0, 3, over_y), edge(zp, x, 1 - y, 1, 2, over_x)]
        for half in range(2):
            copies.append(hop(zp, 1 - x, y, half, core, 4, other))
            copies.append(hop(zp, x, 1 - y, half, core, 4, other))
        for copy in copies:
            copy.wait_send() if finish else copy.start()

    def diagonal(zp, finish):
        if not finish:
            @pl.when(zp == z)
            def _():
                for half in range(2):
                    hop(zp, 1 - x, 1 - y, half, core, 2, over_x).wait_recv()
                pass_middle(zp, False)

            @pl.when(zp != z)
            def _():
                for side in range(2):
                    edge(zp, 1 - x, 1 - y, side, 2, over_x).wait_recv()

            @pl.when((zp != z) & (between == 0))
            def _():
                middle(zp, 0, over_x).wait_recv()

        for half in range(2):
            copy = hop(zp, 1 - x, 1 - y, half, core, 4, other)
            copy.wait_send() if finish else copy.start()

    def complete(zp):
        for xp in range(2):
            for yp in range(2):
                for half in range(2):
                    hop(zp, xp, yp, half, 1 - core, 4, other).wait_recv()

    def close(zp):
        column(zp, True)

        @pl.when(zp == z)
        def _():
            beside(zp, True, True)

        @pl.when(zp != z)
        def _():
            beside(zp, True, False)

        diagonal(zp, True)
        pass_middle(zp, True)

    return column, forward, arrive, beside, relay_middle, diagonal, complete, close


def return_sums(
    parts, part_in, chooser, acc, x_diag, y_diag, x_in, y_in, z_in, mid_in, center_in, sems, mid_sems,
    center_sems,
):
    z, x, core, y = coordinates()
    rows, half_cols = acc.shape[2], acc.shape[3] // 2
    half_rows = rows // 2
    over_x, over_y, other = place(z, 1 - x, core, y), place(z, x, core, 1 - y), place(z, x, 1 - core, y)
    mine = pl.ds(pl.multiple_of(y * half_cols, half_cols), half_cols)
    theirs = pl.ds(pl.multiple_of((1 - y) * half_cols, half_cols), half_cols)

    def copy(source, target, kind, zp, peer):
        return pltpu.make_async_remote_copy(
            source, target, sems.at[0, kind, zp], sems.at[1, kind, zp],
            device_id=peer, device_id_type=MESH,
        )

    def core_copy(zp, xp):
        return copy(parts.at[zp, xp * 2 + 1 - core], part_in.at[zp, xp], xp, zp, other)

    def split(own):
        return half_rows if own else half_rows // 2

    def diag_copies(zp, own):
        far, edge = acc.at[zp, 1 - x], split(own)
        over, under = pl.ds(0, edge), pl.ds(rows - edge, edge)
        return (
            copy(far.at[over, theirs], y_diag.at[zp, over], 2, zp, over_y),
            copy(far.at[under, theirs], x_diag.at[zp, over], 3, zp, over_x),
        )

    def free_copies(zp, own):
        edge = split(own)
        after, ahead = pl.ds(edge, rows - edge), pl.ds(0, rows - edge)
        return (
            copy(acc.at[zp, 1 - x].at[after, mine], x_in.at[zp, after], 4, zp, over_x),
            copy(acc.at[zp, x].at[ahead, theirs], y_in.at[zp, ahead], 5, zp, over_y),
        )

    def last_copies(zp, own):
        edge = split(own)
        over, under = pl.ds(0, edge), pl.ds(rows - edge, edge)
        return (
            copy(acc.at[zp, 1 - x].at[over, mine], x_in.at[zp, over], 6, zp, over_x),
            copy(acc.at[zp, x].at[under, theirs], y_in.at[zp, under], 7, zp, over_y),
        )

    center = pl.ds(half_rows // 2, half_rows)

    def center_copy(zp):
        return pltpu.make_async_remote_copy(
            acc.at[zp, 1 - x].at[center, theirs], center_in.at[z],
            center_sems.at[0, zp], center_sems.at[1, z],
            device_id=place(zp, x, core, y), device_id_type=MESH,
        )

    def center_arrival(zp):
        return pltpu.make_async_remote_copy(
            acc.at[zp, 1 - x].at[center, theirs], center_in.at[zp],
            center_sems.at[0, zp], center_sems.at[1, zp],
            device_id=place(near, x, core, y), device_id_type=MESH,
        )

    def plane_copy(zp):
        return pltpu.make_async_remote_copy(
            acc.at[zp, x].at[:, mine], z_in.at[z], sems.at[0, 8, zp], sems.at[1, 8, z],
            device_id=place(zp, x, core, y), device_id_type=MESH,
        )

    between = z * (3 - z)
    near = plane_at(1)

    def plane_arrival(zp):
        return pltpu.make_async_remote_copy(
            acc.at[zp, x].at[:, mine], z_in.at[zp], sems.at[0, 8, zp], sems.at[1, 8, zp],
            device_id=place(near, x, core, y), device_id_type=MESH,
        )

    def gather_copy(zp, half):
        lines = pl.ds(half * half_rows, half_rows)
        return pltpu.make_async_remote_copy(
            acc.at[zp, x].at[lines, mine], mid_in.at[zp, lines],
            mid_sems.at[0, half, zp], mid_sems.at[1, half, zp],
            device_id=place(near, x, core, y), device_id_type=MESH,
        )

    def joint_copy(zp, half):
        lines = pl.ds(half * half_rows, half_rows)
        return pltpu.make_async_remote_copy(
            acc.at[zp, x].at[lines, mine], z_in.at[z, lines],
            mid_sems.at[2, half, zp], mid_sems.at[3, half, z],
            device_id=place(zp, x, core, y), device_id_type=MESH,
        )

    def joint_arrival(zp, half):
        lines = pl.ds(half * half_rows, half_rows)
        return pltpu.make_async_remote_copy(
            acc.at[zp, x].at[lines, mine], z_in.at[zp, lines],
            mid_sems.at[2, half, zp], mid_sems.at[3, half, zp],
            device_id=place(near, x, core, y), device_id_type=MESH,
        )

    def add(target, *terms):
        total = target[...].astype(jnp.float32)
        for term in terms:
            total = total + term[...].astype(jnp.float32)
        target[...] = total.astype(target.dtype)

    def cores(zp, own):
        down = (((0,), (0,)), ((), ()))
        for xp in range(2):
            core_copy(zp, xp).wait_recv()
            request = (zp * 2 + xp) * 2 + core
            total = lax.dot_general(
                chooser[0, request], parts[zp, xp * 2 + core], down,
                preferred_element_type=jnp.float32,
            ) + lax.dot_general(
                chooser[1, request], part_in[zp, xp], down, preferred_element_type=jnp.float32
            )
            acc[zp, xp] = total.astype(jnp.bfloat16)
        if own:
            for item in free_copies(zp, own):
                item.start()
            others = [plane_at(turn) for turn in range(1, 4)]
            for source in others:
                center_arrival(source).wait_recv()
            add(
                acc.at[zp, 1 - x].at[center, theirs],
                *[center_in.at[source] for source in others],
            )
            for item in diag_copies(zp, own):
                item.start()
        else:
            for item in diag_copies(zp, own) + free_copies(zp, own):
                item.start()
            center_copy(zp).start()

    def corners(zp, own):
        edge = split(own)
        over, under = pl.ds(0, edge), pl.ds(rows - edge, edge)
        from_y, from_x = diag_copies(zp, own)
        over_x_copy, over_y_copy = last_copies(zp, own)
        from_y.wait_recv()
        add(acc.at[zp, 1 - x].at[over, mine], y_diag.at[zp, over])
        over_x_copy.start()
        from_x.wait_recv()
        add(acc.at[zp, x].at[under, theirs], x_diag.at[zp, over])
        over_y_copy.start()

    def arrivals(zp, own):
        for item in free_copies(zp, own) + last_copies(zp, own):
            item.wait_recv()

    def columns(zp):
        arrivals(zp, False)
        add(acc.at[zp, x].at[:, mine], x_in.at[zp], y_in.at[zp])

        @pl.when(zp == near)
        def _():
            plane_copy(zp).start()

        @pl.when((zp != near) & (between == 0))
        def _():
            for half in range(2):
                gather_copy(zp, half).start()

    def joints(zp):
        @pl.when(between > 0)
        def _():
            for half in range(2):
                lines = pl.ds(half * half_rows, half_rows)
                gather_copy(zp, half).wait_recv()
                add(acc.at[zp, x].at[lines, mine], mid_in.at[zp, lines])
                joint_copy(zp, half).start()

    def final(result):
        arrivals(z, True)
        total = acc[z, x, :, mine].astype(jnp.float32)
        total = total + x_in[z].astype(jnp.float32) + y_in[z].astype(jnp.float32)
        plane_arrival(near).wait_recv()
        total = total + z_in[near].astype(jnp.float32)
        far = plane_at(2)
        for half in range(2):
            joint_arrival(far, half).wait_recv()
        result[...] = total + z_in[far].astype(jnp.float32)

    def close(zp):
        for xp in range(2):
            core_copy(zp, xp).wait_send()

        def sent(own):
            for item in diag_copies(zp, own) + free_copies(zp, own) + last_copies(zp, own):
                item.wait_send()
            if not own:
                center_copy(zp).wait_send()

        pl.when(zp == z)(lambda: sent(True))
        pl.when(zp != z)(lambda: sent(False))

        @pl.when(zp == near)
        def _():
            plane_copy(zp).wait_send()

        @pl.when((zp != near) & (zp != z) & (between == 0))
        def _():
            for half in range(2):
                gather_copy(zp, half).wait_send()

        @pl.when((zp != near) & (zp != z) & (between > 0))
        def _():
            for half in range(2):
                joint_copy(zp, half).wait_send()

    return core_copy, cores, corners, columns, joints, final, close


def choose(mine, chooser, which):
    requests, tokens = mine.shape
    capacity = chooser.shape[2]
    named = jnp.where(mine[...] > 0.0, 1.0, 0.0)
    rows = lax.broadcasted_iota(jnp.int32, (tokens, tokens), 0)
    columns = lax.broadcasted_iota(jnp.int32, (tokens, tokens), 1)
    before = jnp.where(rows <= columns, 1.0, 0.0).astype(jnp.bfloat16)
    slot = jnp.dot(named.astype(jnp.bfloat16), before, preferred_element_type=jnp.float32)
    wanted = jnp.where(named > 0.0, slot - 1.0, -1.0).astype(jnp.int32)
    places = lax.broadcasted_iota(jnp.int32, (capacity, tokens), 0)
    for request in range(requests):
        picks = jnp.where(wanted[request : request + 1, :] == places, 1.0, 0.0)
        chooser[which, request] = picks.astype(jnp.bfloat16)


def share_prompts(block_ref, share_ref, keys_ref, mine_ref, send, recv, send_w, recv_w, local):
    me = lax.axis_index("req")
    y = lax.axis_index("tp")
    depth = block_ref.shape[1]
    rows = pl.ds(pl.multiple_of(me * depth, depth), depth)
    core, other = me % 2, me + 1 - 2 * (me % 2)

    def block(source):
        return keys_ref.at[:, pl.ds(pl.multiple_of(source * depth, depth), depth), :]

    def shares(step):
        peer = (me + step) % 16
        return pltpu.make_async_remote_copy(
            share_ref.at[peer], mine_ref.at[me], send_w.at[step], recv_w.at[step],
            device_id={"req": peer, "tp": y}, device_id_type=MESH,
        )

    def direct(step):
        return pltpu.make_async_remote_copy(
            block_ref, keys_ref.at[:, rows, :], send.at[step], recv.at[step],
            device_id={"req": (me + 2 * step) % 16, "tp": y}, device_id_type=MESH,
        )

    def across(source, index):
        return pltpu.make_async_remote_copy(
            block(source), block(source), send.at[index], recv.at[index],
            device_id={"req": other, "tp": y}, device_id_type=MESH,
        )

    home = pltpu.make_async_remote_copy(
        block_ref, keys_ref.at[:, rows, :], send.at[8 + me // 2], recv.at[8 + me // 2],
        device_id={"req": other, "tp": y}, device_id_type=MESH,
    )
    own = pltpu.make_async_copy(block_ref, keys_ref.at[:, rows, :], local.at[0])
    own_share = pltpu.make_async_copy(share_ref.at[me], mine_ref.at[me], local.at[1])

    def start():
        for step in (4, 3, 5, 2, 6, 1, 7):
            direct(step).start()
        home.start()
        own.start()
        own_share.start()

    def start_shares():
        def send_share(step, carry):
            shares(step).start()
            return carry

        lax.fori_loop(1, 16, send_share, 0)

    def relay(step):
        source = (me + 2 * step) % 16
        across(source, 8 - step).wait_recv()
        across(source, 8 + source // 2).start()

    def finish():
        own.wait()
        for step in range(8):
            source = (me + 2 * step) % 16 + 1 - 2 * core
            across(source, 8 + source // 2).wait_recv()

    def finish_shares():
        own_share.wait()

        def wait_share(step, carry):
            shares(step).wait_recv()
            return carry

        lax.fori_loop(1, 16, wait_share, 0)

    def close():
        home.wait_send()
        for step in range(1, 8):
            direct(step).wait_send()
            source = (me + 2 * step) % 16
            across(source, 8 + source // 2).wait_send()

        def close_share(step, carry):
            shares(step).wait_send()
            return carry

        lax.fori_loop(1, 16, close_share, 0)

    return start, start_shares, relay, finish, finish_shares, close


def layer_kernel(
    page_table, prefix_len, prompt_len, group_ids,
    routes, route_weight, gain, prompt_block,
    residual_hbm, query_hbm, stretch_hbm, pool_hbm, absorb_hbm, value_hbm, out_hbm, gate_hbm, up_hbm, down_hbm,
    attention_part, expert_part,
    query, residual, stretch, keys, absorb, value, out_w, prompts, absorbed, bests, totals, latents, bias,
    heads,
    share, share_in, projected,
    whole, outgoing, incoming, squares_out, squares_in, gains, mine_share, other_share, roots,
    chooser, level,
    gate_w, up_w, down_w, rows, hidden, parts, part_in, acc, x_diag, y_diag, x_in, y_in, z_in, mid_in,
    center_in, prompt_send, prompt_recv, share_send, share_recv, local_sems,
    pair_sems, load_sems, root_sems, send, recv, mid_send, mid_recv, sems, mid_sems, center_sems,
):
    z, x, core, y = coordinates()
    me = lax.axis_index("req")
    tokens, half_cols = residual.shape
    quarter = half_cols // 2
    count, nope, rank = absorb.shape
    width = query.shape[1]
    pool_rows = pool_hbm.shape[0]
    own_rows = pool_rows + tokens
    loads = [
        pltpu.make_async_copy(source, target, load_sems.at[index])
        for index, (source, target) in enumerate(
            (
                (query_hbm, query), (absorb_hbm, absorb), (stretch_hbm, stretch),
                (pool_hbm, keys.at[pl.ds(0, pool_rows)]), (value_hbm, value), (out_hbm, out_w),
                (gate_hbm, gate_w), (up_hbm, up_w), (down_hbm, down_w), (residual_hbm, residual),
            )
        )
    ]
    greet()
    for load in loads:
        load.start()
    mine = pl.ds(pl.multiple_of(y * half_cols, half_cols), half_cols)
    theirs = pl.ds(pl.multiple_of((1 - y) * half_cols, half_cols), half_cols)
    over_y, other = place(z, x, core, 1 - y), place(z, x, 1 - core, y)

    def pair(source, target, index, peer=over_y):
        return pltpu.make_async_remote_copy(
            source, target, pair_sems.at[0, index], pair_sems.at[1, index],
            device_id=peer, device_id_type=MESH,
        )

    def swap(half):
        span = pl.ds(half * quarter, quarter)
        return pair(outgoing.at[:, span], incoming.at[:, span], half)

    squares = pair(squares_out, squares_in, 2)
    gain_copy = pair(gains.at[y], gains.at[y], 3)
    share_copy = pair(mine_share, other_share, 4, other)
    start_prompts, start_shares, relay, finish_prompts, finish_shares, close_prompts = share_prompts(
        prompt_block, share, prompts, share_in, prompt_send, prompt_recv, share_send, share_recv,
        local_sems,
    )
    expert_of = lax.broadcasted_iota(jnp.int32, (16, tokens), 0)
    given = jnp.zeros((16, tokens), jnp.float32)
    for choice in range(routes.shape[0]):
        hit = routes[choice : choice + 1, :] == expert_of
        given = given + jnp.where(hit, route_weight[choice : choice + 1, :], 0.0)
    for expert in range(16):
        share[expert] = given[expert : expert + 1, :]
    for row in range(gain.shape[0]):
        gains[y, :, pl.ds(row * gain.shape[1], gain.shape[1])] = gain[row : row + 1, :].astype(
            jnp.float32
        )
    pl.semaphore_wait(pltpu.get_barrier_semaphore(), 16)
    start_prompts()
    gain_copy.start()
    group = group_ids[me]
    page = pool_rows // page_table.shape[1]
    lane = lax.broadcasted_iota(jnp.int32, (1, pool_rows), 1)
    logical = jnp.zeros((1, pool_rows), jnp.int32)
    for index in range(page_table.shape[1]):
        logical = jnp.where(lane // page == page_table[0, index], index, logical)
    prefix_at = logical * page + lane % page
    bias[:, pl.ds(0, pool_rows)] = jnp.where(prefix_at < prefix_len[me], 0.0, NEGATIVE)
    prompt_rows = prompts.shape[1]
    prompt_lane = lax.broadcasted_iota(jnp.int32, (1, prompt_rows), 1)
    bias[:, pl.ds(pool_rows, prompt_rows)] = jnp.where(prompt_lane < prompt_len[group], 0.0, NEGATIVE)
    loads[2].wait()
    keys[pl.ds(pool_rows, tokens), :] = stretch[...].T
    for index in (0, 1, 3):
        loads[index].wait()
    first = (((0,), (0,)), ((), ()))
    across = (((1,), (1,)), ((), ()))

    factor = width ** (-0.5) * math.log2(math.e)

    batch = count // 2
    deep = batch * tokens

    def own_keys(index, carry):
        lines = pl.ds(pl.multiple_of(index * deep, deep), deep)
        for turn in range(batch):
            head = index * batch + turn
            own = pl.ds(pl.multiple_of(head * tokens, tokens), tokens)
            wide = lax.dot_general(
                query[head, pl.ds(0, nope), :], absorb[head], first,
                preferred_element_type=jnp.float32,
            )
            absorbed[own, pl.ds(0, rank)] = wide.astype(jnp.bfloat16)
            absorbed[own, pl.ds(rank, width - nope)] = query[head, pl.ds(nope, width - nope), :].T
        found = lax.dot_general(
            absorbed[lines, :], keys[pl.ds(0, own_rows), :], across,
            preferred_element_type=jnp.float32,
        )
        token = lax.rem(lax.broadcasted_iota(jnp.int32, (deep, tokens), 0), tokens)
        later = lax.broadcasted_iota(jnp.int32, (deep, tokens), 1) > token
        found = jnp.concatenate(
            [
                found[:, :pool_rows] + bias[:, pl.ds(0, pool_rows)],
                jnp.where(later, NEGATIVE, found[:, pool_rows:]),
            ],
            axis=1,
        )
        best = jnp.max(found, axis=1, keepdims=True)
        weights = jnp.exp2((found - best) * factor)
        bests[lines, :] = best
        totals[lines, :] = jnp.sum(weights, axis=1, keepdims=True)
        latents[lines, :] = jnp.dot(
            weights.astype(jnp.bfloat16), keys[pl.ds(0, own_rows), pl.ds(0, rank)],
            preferred_element_type=jnp.float32,
        )

        if index == 1:
            for step in range(1, 8):
                relay(step)
        return carry

    own_keys(0, 0)
    start_shares()
    own_keys(1, 0)
    finish_prompts()
    keys[pl.ds(own_rows, prompt_rows), :] = prompts[group]
    loads[4].wait()
    loads[9].wait()
    size = value.shape[2]

    def prompt_keys(index, carry):
        lines = pl.ds(pl.multiple_of(index * deep, deep), deep)
        found = lax.dot_general(
            absorbed[lines, :], keys[pl.ds(own_rows, prompt_rows), :], across,
            preferred_element_type=jnp.float32,
        ) + bias[:, pl.ds(pool_rows, prompt_rows)]
        held = bests[lines, :]
        best = jnp.maximum(jnp.max(found, axis=1, keepdims=True), held)
        keep = jnp.exp2((held - best) * factor)
        weights = jnp.exp2((found - best) * factor)
        total = totals[lines, :] * keep + jnp.sum(weights, axis=1, keepdims=True)
        latent = latents[lines, :] * keep + jnp.dot(
            weights.astype(jnp.bfloat16), keys[pl.ds(own_rows, prompt_rows), pl.ds(0, rank)],
            preferred_element_type=jnp.float32,
        )
        latent = (latent * (1.0 / total)).astype(jnp.bfloat16)
        for turn in range(batch):
            head = index * batch + turn
            heads[:, pl.ds(pl.multiple_of(head * size, size), size)] = jnp.dot(
                latent[turn * tokens : (turn + 1) * tokens], value[head],
                preferred_element_type=jnp.float32,
            ).astype(jnp.bfloat16)
        return carry

    prompt_keys(0, 0)
    prompt_keys(1, 0)
    loads[5].wait()
    for half in range(2):
        across_cols = pl.ds(
            pl.multiple_of((1 - y) * half_cols + half * quarter, quarter), quarter
        )
        outgoing[:, pl.ds(half * quarter, quarter)] = jnp.dot(
            heads[...], out_w[:, across_cols], preferred_element_type=jnp.float32
        ).astype(jnp.bfloat16)
        swap(half).start()
    for half in range(2):
        own_cols = pl.ds(pl.multiple_of(y * half_cols + half * quarter, quarter), quarter)
        projected[:, pl.ds(half * quarter, quarter)] = jnp.dot(
            heads[...], out_w[:, own_cols], preferred_element_type=jnp.float32
        )
    finish_shares()
    for request in range(16):
        mine_share[request : request + 1, :] = share_in[request]
    share_copy.start()
    choose(mine_share, chooser, 0)
    (
        column, forward, arrive, beside, relay_middle, diagonal, complete, close_spread,
    ) = spread_tokens(
        whole, send, recv, mid_send, mid_recv
    )
    sums = jnp.zeros((tokens, 1), jnp.float32)
    for half in range(2):
        span = pl.ds(half * quarter, quarter)
        swap(half).wait_recv()
        added = projected[:, span] + incoming[:, span].astype(jnp.float32)
        projected[:, span] = added
        rounded = (residual[:, span].astype(jnp.float32) + added).astype(jnp.bfloat16)
        whole[me, :, pl.ds(pl.multiple_of(y * half_cols + half * quarter, quarter), quarter)] = rounded
        stream = rounded.astype(jnp.float32)
        sums = sums + jnp.sum(stream * stream, axis=1, keepdims=True)
        if half == 1:
            diag = lax.broadcasted_iota(jnp.int32, (tokens, tokens), 1) == (
                lax.broadcasted_iota(jnp.int32, (tokens, tokens), 0)
            )
            squares_out[...] = jnp.sum(jnp.where(diag, sums, 0.0), axis=0, keepdims=True)
            squares.start()
        column(z, False, (half,))
    part_out = pltpu.make_async_copy(projected, attention_part, load_sems.at[10])
    part_out.start()
    share_copy.wait_recv()
    choose(other_share, chooser, 1)

    def root_copy(step):
        peer = (me + step) % 16
        return pltpu.make_async_remote_copy(
            roots.at[me], roots.at[me], root_sems.at[0, peer], root_sems.at[1, me],
            device_id={"req": peer, "tp": y}, device_id_type=MESH,
        )

    def root_arrival(request):
        return pltpu.make_async_remote_copy(
            roots.at[request], roots.at[request], root_sems.at[0, request],
            root_sems.at[1, request], device_id=over_y, device_id_type=MESH,
        )

    forward(plane_at(1))
    arrive(plane_at(1))
    forward(plane_at(2))
    beside(z, False, True)
    squares.wait_recv()
    roots[me] = lax.rsqrt((squares_out[...] + squares_in[...]) / (2 * half_cols) + EPSILON)

    def send_root(step, carry):
        root_copy(step).start()
        return carry

    lax.fori_loop(1, 16, send_root, 0)
    gain_copy.wait_recv()
    for load in loads[6:9]:
        load.wait()
    capacity = chooser.shape[2]
    core_copy, cores, corners, columns, joints, final, close_return = return_sums(
        parts, part_in, chooser, acc, x_diag, y_diag, x_in, y_in, z_in, mid_in, center_in, sems, mid_sems,
        center_sems,
    )

    def compute(zp):
        for index in range(4):
            request = zp * 4 + index

            @pl.when(request != me)
            def _(request=request):
                root_arrival(request).wait_recv()

        for index in range(4):
            request = zp * 4 + index
            lines = pl.ds(index * capacity, capacity)
            picks = chooser[0, request]
            picked = jnp.dot(picks, whole[request], preferred_element_type=jnp.float32)
            wide = picks.astype(jnp.float32)
            picked = picked * jnp.sum(wide * roots[request], axis=1, keepdims=True)
            shared = jnp.sum(wide * share_in[request], axis=1, keepdims=True)
            level[lines, :] = jnp.broadcast_to(shared, (capacity, level.shape[1]))
            for side in range(2):
                span = pl.ds(side * half_cols, half_cols)
                scaled = picked[:, side * half_cols : (side + 1) * half_cols] * gains[side]
                rows[lines, span] = scaled.astype(jnp.bfloat16)
        gate = lax.dot_general(rows[...], gate_w[...], across, preferred_element_type=jnp.float32)
        up = lax.dot_general(rows[...], up_w[...], across, preferred_element_type=jnp.float32)
        hidden[...] = (gate / (1.0 + jnp.exp(-gate)) * up * level[:, :1]).astype(jnp.bfloat16)
        part = jnp.dot(hidden[...], down_w[...], preferred_element_type=jnp.float32)
        for index in range(4):
            parts[zp, index] = part[index * capacity : (index + 1) * capacity].astype(jnp.bfloat16)
        for xp in range(2):
            core_copy(zp, xp).start()

    def close_dispatch():
        def close(zp, carry):
            close_spread(zp)
            return carry

        lax.fori_loop(0, 4, close, 0)

        def close_root(step, carry):
            root_copy(step).wait_send()
            return carry

        lax.fori_loop(1, 16, close_root, 0)
        for item in (swap(0), swap(1), squares, gain_copy, share_copy):
            item.wait_send()
        close_prompts()

    def step(turn, carry):
        @pl.when(turn < 3)
        def _():
            arrive(plane_at(turn + 1))

        @pl.when(turn == 1)
        def _():
            forward(plane_at(3))

        @pl.when(turn == 2)
        def _():
            relay_middle(plane_at(1))
            relay_middle(plane_at(2))

        @pl.when(turn < 4)
        def _():
            beside(plane_at(turn), False, False)

        @pl.when(turn == 2)
        def _():
            relay_middle(plane_at(3))

        @pl.when(turn == 4)
        def _():
            diagonal(plane_at(3), False)

        @pl.when(turn >= 5)
        def _():
            columns(plane_at(turn - 4))

        @pl.when(turn == 7)
        def _():
            joints(plane_at(2))

        @pl.when((turn >= 4) & (turn < 7))
        def _():
            corners(plane_at(turn - 3), False)

        @pl.when((turn >= 3) & (turn < 6))
        def _():
            cores(plane_at(turn - 2), False)

        @pl.when(turn == 6)
        def _():
            cores(z, True)
            close_dispatch()

        @pl.when(turn < 5)
        def _():
            zp = plane_at(turn - 1)

            @pl.when(turn < 4)
            def _():
                diagonal(zp, False)

            complete(zp)
            compute(zp)

        return carry

    lax.fori_loop(1, 8, step, 0)
    corners(z, True)
    for turn in (1, 2):
        close_return(plane_at(turn))
    joints(plane_at(3))
    final(expert_part)
    for turn in (0, 3):
        close_return(plane_at(turn))
    part_out.wait()


def on_block(
    queries, stretch_cache, prefix_pool, page_table, prefix_len, prompt_cache, prompt_len,
    group_ids, absorb_weight, value_weight, out_weight, residual, norm_gain, routes,
    route_weight, gate_weight, up_weight, down_weight,
):
    tokens, count, width = queries.shape
    nope, rank = absorb_weight.shape[1:]
    size = value_weight.shape[2]
    top = routes.shape[1]
    experts = 16
    capacity = max(2, tokens * top * 4 // (3 * experts))
    pages, page, entry = prefix_pool.shape
    groups, depth = prompt_cache.shape[:2]
    half = residual.shape[1]
    model = out_weight.shape[1]
    units = down_weight.shape[1]
    own_rows = pages * page + tokens
    bf16, f32 = jnp.bfloat16, jnp.float32
    dma = pltpu.SemaphoreType.DMA
    vmem = pl.BlockSpec(memory_space=pltpu.VMEM)
    smem = pl.BlockSpec(memory_space=pltpu.SMEM)
    anywhere = pl.BlockSpec(memory_space=pl.ANY)
    attention_part, expert_part = pl.pallas_call(
        layer_kernel,
        out_shape=(jax.ShapeDtypeStruct((tokens, half), f32),) * 2,
        in_specs=[smem] * 4 + [vmem] * 4 + [anywhere] * 10,
        out_specs=(anywhere, vmem),
        scratch_shapes=[
            pltpu.VMEM((count, width, tokens), bf16),
            pltpu.VMEM((tokens, half), bf16),
            pltpu.VMEM((entry, tokens), bf16),
            pltpu.VMEM((own_rows + depth * 16, entry), bf16),
            pltpu.VMEM((count, nope, rank), bf16),
            pltpu.VMEM((count, rank, size), bf16),
            pltpu.VMEM((count * size, model), bf16),
            pltpu.VMEM((groups, depth * 16, entry), bf16),
            pltpu.VMEM((count * tokens, entry), bf16),
            pltpu.VMEM((count * tokens, 1), f32),
            pltpu.VMEM((count * tokens, 1), f32),
            pltpu.VMEM((count * tokens, rank), f32),
            pltpu.VMEM((1, pages * page + depth * 16), f32),
            pltpu.VMEM((tokens, count * size), bf16),
            pltpu.VMEM((16, 1, tokens), f32),
            pltpu.VMEM((16, 1, tokens), f32),
            pltpu.VMEM((tokens, half), f32),
            pltpu.VMEM((16, tokens, model), bf16),
            pltpu.VMEM((tokens, half), bf16),
            pltpu.VMEM((tokens, half), bf16),
            pltpu.VMEM((1, tokens), f32),
            pltpu.VMEM((1, tokens), f32),
            pltpu.VMEM((2, 1, half), f32),
            pltpu.VMEM((16, tokens), f32),
            pltpu.VMEM((16, tokens), f32),
            pltpu.VMEM((16, 1, tokens), f32),
            pltpu.VMEM((2, 16, capacity, tokens), bf16),
            pltpu.VMEM((4 * capacity, 128), f32),
            pltpu.VMEM((units, model), bf16),
            pltpu.VMEM((units, model), bf16),
            pltpu.VMEM((units, model), bf16),
            pltpu.VMEM((4 * capacity, model), bf16),
            pltpu.VMEM((4 * capacity, units), bf16),
            pltpu.VMEM((4, 4, capacity, model), bf16),
            pltpu.VMEM((4, 2, capacity, model), bf16),
            pltpu.VMEM((4, 2, tokens, model), bf16),
            pltpu.VMEM((4, tokens // 2, half), bf16),
            pltpu.VMEM((4, tokens // 2, half), bf16),
            pltpu.VMEM((4, tokens, half), bf16),
            pltpu.VMEM((4, tokens, half), bf16),
            pltpu.VMEM((4, tokens, half), bf16),
            pltpu.VMEM((4, tokens, half), bf16),
            pltpu.VMEM((4, tokens // 2, half), bf16),
            dma((16,)),
            dma((16,)),
            dma((16,)),
            dma((16,)),
            dma((2,)),
            dma((2, 5)),
            dma((11,)),
            dma((2, 16)),
            dma((5, 32)),
            dma((2, 32)),
            dma((2, 4)),
            dma((4,)),
            dma((2, 9, 4)),
            dma((4, 2, 4)),
            dma((2, 4)),
        ],
        compiler_params=pltpu.CompilerParams(
            collective_id=0, has_side_effects=True, vmem_limit_bytes=60 << 20
        ),
    )(
        page_table, prefix_len, prompt_len, group_ids,
        routes.T, route_weight.T, norm_gain.reshape(-1, 128), prompt_cache, residual,
        jnp.transpose(queries, (1, 2, 0)), stretch_cache.T, prefix_pool.reshape(pages * page, entry),
        absorb_weight, value_weight, out_weight,
        jnp.swapaxes(gate_weight[0], 0, 1), jnp.swapaxes(up_weight[0], 0, 1), down_weight[0],
    )
    attended = (residual.astype(f32) + attention_part).astype(bf16)
    return attended, (attended.astype(f32) + expert_part).astype(bf16)


def solution(mesh):
    in_specs = (
        P("req", "tp", None),
        P("req", None),
        P("req", None, None),
        P("req", None),
        P(),
        P(None, "req", None),
        P(),
        P(),
        P("tp", None, None),
        P("tp", None, None),
        P("tp", None),
        P("req", "tp"),
        P("tp"),
        P("req", None),
        P("req", None),
        P("req", None, "tp"),
        P("req", None, "tp"),
        P("req", "tp", None),
    )
    out_specs = (P("req", "tp"), P("req", "tp"))
    body = on_block if mesh.shape["req"] == 16 and mesh.shape["tp"] == 2 else on_device
    return jax.shard_map(
        body, mesh=mesh, in_specs=in_specs, out_specs=out_specs, check_vma=False
    )
```
